32 devices in a mesh: ctx: 8 (over z, y), ch: 4 (over x, core).
Axes of the slice: x: 2, y: 2, z: 4, core: 2. Of those that a mesh axis runs over, the one named last changes fastest.
Arguments:
- queries: bfloat16 [2048, 4096], P('ctx', 'ch'), may hold values from -6 to 6
- keys: bfloat16 [2048, 4096], P('ctx', 'ch'), may hold values from -6 to 6
- values: bfloat16 [2048, 4096], P('ctx', 'ch'), may hold values from -6 to 6
- long_filter: float32 [2048, 4096], P('ctx', 'ch'), may hold values from -1.05 to 1.05
- short_filters: float32 [3, 3, 4096], P(None, None, 'ch'), may hold values from -3.6 to 3.6
- skip: float32 [4096], P('ch'), may hold values from -1 to 1
- w_out: bfloat16 [4096, 8192], P('ch'), may hold values from -0.09375 to 0.09375
- d_out: bfloat16 [2048, 8192], P('ctx', 'ch'), may hold values from -6 to 6
Outputs:
- d_queries: bfloat16 [2048, 4096], P('ctx', 'ch')
- d_keys: bfloat16 [2048, 4096], P('ctx', 'ch')
- d_values: bfloat16 [2048, 4096], P('ctx', 'ch')
- d_long: float32 [2048, 4096], P('ctx', 'ch')
- d_short: float32 [3, 3, 4096], P(None, None, 'ch')
- d_skip: float32 [4096], P('ch')
The draws below stay inside these ranges and needn't reach their ends.
All inputs are finite; a program needn't handle non-finite values.
Results may differ from the reference program's by a relative error of at most 0.0049.
Values may be sent and summed in bfloat16 or wider, within the bound.
A program may use at most 128 MiB of HBM per device.

```python
import jax
import jax.numpy as jnp
from jax import lax

D = 8192
CHANNELS = 4096
TAPS = 3
LENGTH = 2048


def draw_long_filter(key, part):
    rate_key = jax.random.fold_in(key, 11)
    noise_key = jax.random.fold_in(key, 23)
    low = jnp.log(jnp.float32(1.0) / (4.0 * LENGTH))
    high = jnp.log(jnp.float32(1.0) / 30.0)
    rates = jnp.exp(jax.random.uniform(rate_key, (CHANNELS,), jnp.float32, low, high))
    steps = jnp.arange(LENGTH, dtype=jnp.float32)
    scale = jnp.sqrt(jnp.maximum(2.0 * rates, 1.0 / LENGTH))
    envelope = jnp.exp(-steps[:, None] * rates[None, :]) * scale[None, :]
    noise = jnp.clip(jax.random.normal(noise_key, (LENGTH, CHANNELS), jnp.float32), -4.0, 4.0)
    return (noise * envelope).astype(jnp.float32)


def block_scale(stream_key, dims, shards, smallest, largest):
    factor_of, own = 1.0, jax.random.fold_in(stream_key, 6)
    for axis_at, shards_of in shards:
        steps = jnp.exp(jax.random.uniform(jax.random.fold_in(own, axis_at), (shards_of,), jnp.float32, smallest / len(shards), largest / len(shards)))
        factor_of = factor_of * jnp.repeat(steps, dims[axis_at] // shards_of).reshape([-1 if axis == axis_at else 1 for axis in range(len(dims))])
    return factor_of


def scatter_about(own_key, shape, scale, bound, pieces=(), kind=jnp.bfloat16):
    level = block_scale(own_key, shape, pieces, -0.22, 0.18) if pieces else 1.0
    array = jax.random.normal(own_key, shape, jnp.float32) * scale * level
    return jnp.minimum(jnp.maximum(array, -bound), bound).astype(kind)


def setup_inputs(seed: int = 0) -> dict:
    streams_of = jax.random.split(jax.random.key(seed), 9)
    return {
        "queries": scatter_about(streams_of[0], (LENGTH, CHANNELS), 1.0, 6.0, ((0, 8), (1, 4))),
        "keys": scatter_about(streams_of[1], (LENGTH, CHANNELS), 1.0, 6.0, ((0, 8), (1, 4))),
        "values": scatter_about(streams_of[2], (LENGTH, CHANNELS), 1.0, 6.0, ((0, 8), (1, 4))),
        "long_filter": draw_long_filter(jax.random.fold_in(streams_of[8], 71), 0),
        "short_filters": scatter_about(streams_of[4], (3, TAPS, CHANNELS), 0.6, 3.6, ((2, 4),), jnp.float32),
        "skip": jnp.clip(jax.random.uniform(streams_of[5], (CHANNELS,), jnp.float32, -1.0, 1.0) * block_scale(streams_of[5], (CHANNELS,), ((0, 4),), -0.4, 0.0), -1.0, 1.0),
        "w_out": scatter_about(streams_of[6], (CHANNELS, D), CHANNELS ** -0.5, 0.09375, ((0, 4),)),
        "d_out": scatter_about(streams_of[7], (LENGTH, D), 1.0, 6.0, ((0, 8), (1, 4))),
    }


def short_conv(stream, taps):
    padded = jnp.pad(stream, ((TAPS - 1, 0), (0, 0)))
    result = jnp.zeros(stream.shape, jnp.float32)
    for j in range(TAPS):
        result = result + taps[j][None, :] * padded[TAPS - 1 - j:TAPS - 1 - j + LENGTH]
    return result, padded


def back_conv(grad, taps):
    padded = jnp.pad(grad, ((0, TAPS - 1), (0, 0)))
    result = jnp.zeros(grad.shape, jnp.float32)
    for j in range(TAPS):
        result = result + taps[j][None, :] * padded[j:j + LENGTH]
    return result


def reference(queries, keys, values, long_filter, short_filters, skip, w_out, d_out):
    streams = [queries.astype(jnp.float32), keys.astype(jnp.float32), values.astype(jnp.float32)]
    filtered = []
    padded_in = []
    for s in range(3):
        out_s, pad_s = short_conv(streams[s], short_filters[s])
        filtered.append(out_s)
        padded_in.append(pad_s)
    mixed = filtered[1] * filtered[2]
    grad_o = jnp.dot(d_out, w_out.T, preferred_element_type=jnp.float32).astype(jnp.bfloat16)
    grad_o = lax.optimization_barrier(grad_o).astype(jnp.float32)
    grad_y = grad_o * filtered[0]
    total = 2 * LENGTH
    spec_mixed = jnp.fft.rfft(mixed, n=total, axis=0)
    spec_filter = jnp.fft.rfft(long_filter, n=total, axis=0)
    spec_grad = jnp.fft.rfft(grad_y, n=total, axis=0)
    conv_y = jnp.fft.irfft(spec_mixed * spec_filter, n=total, axis=0)[:LENGTH].astype(jnp.float32)
    conv_back = jnp.fft.irfft(spec_grad * jnp.conj(spec_filter), n=total, axis=0)[:LENGTH].astype(jnp.float32)
    d_long = jnp.fft.irfft(spec_grad * jnp.conj(spec_mixed), n=total, axis=0)[:LENGTH].astype(jnp.float32)
    y_full = conv_y + skip[None, :] * mixed
    grad_mixed = conv_back + skip[None, :] * grad_y
    d_skip = jnp.sum(grad_y * mixed, axis=0)
    grads = [grad_o * y_full, grad_mixed * filtered[2], grad_mixed * filtered[1]]
    short_rows = []
    for s in range(3):
        tap_rows = []
        for j in range(TAPS):
            tap_rows.append(jnp.sum(grads[s] * padded_in[s][TAPS - 1 - j:TAPS - 1 - j + LENGTH], axis=0))
        short_rows.append(jnp.stack(tap_rows))
    d_short = jnp.stack(short_rows)
    d_queries = back_conv(grads[0], short_filters[0]).astype(jnp.bfloat16)
    d_keys = back_conv(grads[1], short_filters[1]).astype(jnp.bfloat16)
    d_values = back_conv(grads[2], short_filters[2]).astype(jnp.bfloat16)
    return (d_queries, d_keys, d_values, d_long, d_short, d_skip)
```

```python
import functools
import math
import types

import jax
import jax.numpy as jnp
import numpy as np
from jax import lax
from jax.experimental import pallas as pl
from jax.experimental.pallas import tpu as pltpu
from jax.sharding import PartitionSpec as P

PAD = 8
TAIL = 16
PARAMS = dict(vmem_limit_bytes=60 * 1024 * 1024)
F32 = jnp.float32
BF16 = jnp.bfloat16
MESH = pl.DeviceIdType.MESH


def split_table(table):
    table = table.astype(np.float32)
    high = table.astype(BF16)
    low = (table - high.astype(np.float32)).astype(BF16)
    return np.concatenate([high[None], low[None]], axis=0)


def tables(block):
    freq = np.arange(block)[:, None]
    place = np.arange(block)[None, :]
    angle = (2 * freq + 1) * place % (4 * block) * (math.pi / (2 * block))
    forward = np.concatenate([np.cos(angle), -np.sin(angle)], axis=0)
    return split_table(forward), split_table(forward.T / block)


def fill(scratch, before, own, after, rim):
    rows = own.shape[0]
    scratch[0:PAD, :] = jnp.zeros_like(scratch[0:PAD, :])
    scratch[PAD + rows :, :] = jnp.zeros_like(scratch[PAD + rows :, :])
    scratch[PAD - rim : PAD, :] = before.astype(F32)
    scratch[PAD : PAD + rows, :] = own.astype(F32)
    if after is not None:
        scratch[PAD + rows : PAD + rows + rim, :] = after.astype(F32)


def short(scratch, taps, rows, lanes, s):
    total = None
    for j in range(taps.shape[1]):
        term = taps[s, j : j + 1, lanes] * scratch[PAD - j : PAD - j + rows, :]
        total = term if total is None else total + term
    return total


def times(a, b):
    return a[0] * b[0] - a[1] * b[1], a[0] * b[1] + a[1] * b[0]


def conj_times(a, b):
    return a[0] * b[0] + a[1] * b[1], a[0] * b[1] - a[1] * b[0]


def add(a, b):
    return b if a is None else (a[0] + b[0], a[1] + b[1])


def spectra(table, blocks, spec):
    for at in range(0, len(blocks), 2):
        pair = blocks[at : at + 2]
        data = jnp.concatenate([ref[...] for ref, _, _ in pair], axis=1)
        out = jnp.dot(table[0], data, preferred_element_type=F32) + jnp.dot(
            table[1], data, preferred_element_type=F32
        )
        cw = data.shape[1] // len(pair)
        for p, (_, s, i) in enumerate(pair):
            spec[s, i] = out[:, p * cw : (p + 1) * cw]


def mix_spectra(first, spec, held):
    count, rows2, cw = spec.shape[1:]
    half = rows2 // 2
    step = 8
    sign = 1.0 - 2.0 * (lax.broadcasted_iota(jnp.int32, (step, cw), 0) % 2).astype(F32)
    zero = jnp.zeros((step, cw), F32)

    def primes(blocks):
        out = [blocks[0]]
        for d in range(1, count):
            re, im = blocks[d]
            old_re, old_im = blocks[d - 1]
            out.append((re - sign * old_im, im + sign * old_re))
        return out

    def chunk(r, carry):
        low = pl.ds(pl.multiple_of(r * step, step), step)
        high = pl.ds(pl.multiple_of(half + r * step, step), step)

        def load(s, i):
            return spec[s, i, low, :], spec[s, i, high, :]

        def save(s, i, value):
            spec[s, i, low, :] = value[0]
            spec[s, i, high, :] = value[1]

        def primed(s):
            values = primes([load(s, i) for i in range(count)])
            for i in range(count):
                save(s, i, values[i])
            return values

        if count <= 8 and first:
            taps = primed(1)
            mixed = [load(0, i) for i in range(count)]
            for i in range(count):
                total = None
                for d in range(i + 1):
                    total = add(total, times(taps[d], mixed[i - d]))
                save(2, i, total)
            return carry
        if count <= 8:
            grads = [load(2, i) for i in range(count)]
            for s in (1, 0):
                taps = [load(s, i) for i in range(count)]
                if s == 0:
                    taps = primes(taps)
                for b in range(count):
                    total = None
                    for e in range(count - b):
                        total = add(total, conj_times(taps[e], grads[b + e]))
                    save(s, b, total)
            return carry
        if first:
            primed(1)

            def one(b, inner):
                def of_y(d, total):
                    return add(total, times(load(1, d), load(0, b - d)))

                save(2, b, lax.fori_loop(0, b + 1, of_y, (zero, zero)))
                return inner

            lax.fori_loop(0, count, one, 0)
            return carry
        primed(0)

        def both(b, inner):
            def of_g(e, totals):
                grad = load(2, b + e)
                return (
                    add(totals[0], conj_times(load(1, e), grad)),
                    add(totals[1], conj_times(load(0, e), grad)),
                )

            pair = lax.fori_loop(0, count - b, of_g, ((zero, zero), (zero, zero)))
            for s in range(2):
                held[s, b, 0], held[s, b, 1] = pair[s]
            return inner

        lax.fori_loop(0, count, both, 0)
        for b in range(count):
            save(1, b, (held[0, b, 0], held[0, b, 1]))
            save(0, b, (held[1, b, 0], held[1, b, 1]))
        return carry

    lax.fori_loop(0, half // step, chunk, 0)


def back_pair(table, values):
    data = jnp.concatenate(values, axis=1)
    high = data.astype(BF16)
    low = (data - high.astype(F32)).astype(BF16)
    out = (
        jnp.dot(table[0], high, preferred_element_type=F32)
        + jnp.dot(table[0], low, preferred_element_type=F32)
        + jnp.dot(table[1], high, preferred_element_type=F32)
    )
    cw = data.shape[1] // len(values)
    return [out[:, p * cw : (p + 1) * cw].astype(BF16) for p in range(len(values))]


def greet(sizes):
    barrier = pltpu.get_barrier_semaphore()
    for axis, size in sizes:
        me = lax.axis_index(axis)
        for o in range(1, size):
            peer = lax.rem(me + o, size)
            pl.semaphore_signal(barrier, inc=1, device_id={axis: peer}, device_id_type=MESH)
    pl.semaphore_wait(barrier, sum(size - 1 for _, size in sizes))


def send(source, target, send_sem, recv_sem, peer, axis="ctx"):
    return pltpu.make_async_remote_copy(
        src_ref=source,
        dst_ref=target,
        send_sem=send_sem,
        recv_sem=recv_sem,
        device_id={axis: peer},
        device_id_type=MESH,
    )


def far_first(size):
    return sorted(range(1, size), key=lambda o: abs(o - size // 2))


def gather_kernel(q_ref, k_ref, v_ref, long_ref, taps, d_ref, w_hbm,
                  mh_ref, go_ref, before, after, ext, mh_tx, held, weights, total,
                  edge_sent, edge_came, sent, came, own_sent, pass_sent, d_came, w_sem):
    count, _, rows, cw = mh_ref.shape
    parts, halves = held.shape[:2]
    cols = d_ref.shape[1]
    piece = cols // halves
    rim = taps.shape[1] - 1
    me = lax.axis_index("ctx")
    mine = lax.axis_index("ch")
    partner = mine + 1 - 2 * lax.rem(mine, 2)
    greet([("ctx", count), ("ch", parts)])

    rest = [lax.rem(mine + 2 * o, parts) for o in range(1, parts // 2)]
    other = [lax.rem(partner + 2 * o, parts) for o in range(1, parts // 2)]
    after_me = lax.rem(me + 1, count)
    before_me = lax.rem(me + count - 1, count)

    edges = []
    for s, ref in ((1, k_ref), (2, v_ref), (0, q_ref)):
        edges.append(send(ref.at[rows - TAIL : rows], before.at[s], edge_sent.at[s],
                          edge_came.at[s], after_me))
    for s, ref in ((0, q_ref), (1, k_ref), (2, v_ref)):
        edges.append(send(ref.at[0:TAIL], after.at[s], edge_sent.at[3 + s],
                          edge_came.at[3 + s], before_me))
    for edge in edges:
        edge.start()

    def own(slot, half, peer):
        lanes = slice(half * piece, (half + 1) * piece)
        return send(d_ref.at[:, lanes], held.at[mine, half], own_sent.at[slot, half],
                    d_came.at[mine, half], peer, "ch")

    def passed(slot, half, part):
        return send(held.at[part, half], held.at[part, half], pass_sent.at[slot, half],
                    d_came.at[part, half], partner, "ch")

    for half in range(halves):
        for slot, peer in enumerate(rest + [partner]):
            own(slot, half, peer).start()

    def weight(part):
        lanes = pl.ds(pl.multiple_of(part * cols, cols), cols)
        return pltpu.make_async_copy(w_hbm.at[:, lanes], weights.at[part], w_sem.at[part])

    order = [mine, partner] + [p for pair in zip(rest, other) for p in pair]
    for part in order:
        weight(part).start()
    for edge in edges:
        edge.wait()

    @pl.when(me == 0)
    def _():
        before[...] = jnp.zeros_like(before)

    @pl.when(me == count - 1)
    def _():
        after[...] = jnp.zeros_like(after)

    for c in range(count):
        lanes = slice(c * cw, (c + 1) * cw)
        fill(ext, before[1, TAIL - rim :, lanes], k_ref[:, lanes], None, rim)
        keyed = short(ext, taps, rows, lanes, 1)
        fill(ext, before[2, TAIL - rim :, lanes], v_ref[:, lanes], None, rim)
        mh_tx[c, 0] = (keyed * short(ext, taps, rows, lanes, 2)).astype(BF16)
        mh_tx[c, 1] = long_ref[:, lanes].astype(BF16)

    def exchange(peer):
        return send(mh_tx.at[peer], mh_ref.at[me], sent.at[peer], came.at[me], peer)

    def arrival(peer):
        return send(mh_tx.at[peer], mh_ref.at[peer], sent.at[peer], came.at[peer], peer)

    peers = [lax.rem(me + o, count) for o in far_first(count)]
    for peer in peers:
        exchange(peer).start()
    mh_ref[me] = mh_tx[me]

    def product(data, part, half=None):
        lanes = slice(None) if half is None else slice(half * piece, (half + 1) * piece)
        return lax.dot_general(data, weights[part, :, lanes], (((1,), (1,)), ((), ())),
                               preferred_element_type=F32)

    def take(part, half):
        total[...] += product(held[part, half], part, half)

    weight(mine).wait()
    total[...] = product(d_ref[...], mine)
    weight(partner).wait()
    for half in range(halves):
        passed(0, half, partner).wait_recv()
        take(partner, half)
    for slot, (direct, relayed) in enumerate(zip(rest, other)):
        weight(direct).wait()
        weight(relayed).wait()
        for half in range(halves):
            passed(slot, half, direct).wait_recv()
            passed(slot, half, direct).start()
            take(direct, half)
            passed(slot, half, relayed).wait_recv()
            take(relayed, half)
    go_ref[...] = total[...].astype(BF16)

    for peer in peers:
        arrival(peer).wait_recv()
    for peer in peers:
        exchange(peer).wait_send()
    for half in range(halves):
        for slot, peer in enumerate(rest + [partner]):
            own(slot, half, peer).wait_send()
        for slot, direct in enumerate(rest):
            passed(slot, half, direct).wait_send()


def conv_kernel(q_ref, before, go_ref, taps, mh_ref, forward, inverse, y_ref, b_ref, edge_ref,
                ext, g_tx, g_rx, y_tx, b_tx, spec, held, sent, came, edge_sem):
    count, _, rows, cw = mh_ref.shape
    rim = taps.shape[1] - 1
    me = lax.axis_index("ctx")
    greet([("ctx", count)])
    edge_rows = edge_ref.shape[0]
    previous = lax.rem(me + count - 1, count)
    edge = send(go_ref.at[0:edge_rows], edge_ref, edge_sem.at[0], edge_sem.at[1], previous)
    edge.start()
    for c in range(count):
        lanes = slice(c * cw, (c + 1) * cw)
        fill(ext, before[0, TAIL - rim :, lanes], q_ref[:, lanes], None, rim)
        g_tx[c] = (go_ref[:, lanes].astype(F32) * short(ext, taps, rows, lanes, 0)).astype(BF16)

    def exchange(kind, source, target, peer):
        return send(
            source.at[peer], target.at[me], sent.at[kind, peer], came.at[kind, me], peer
        )

    def arrival(kind, source, target, peer):
        return send(
            source.at[peer], target.at[peer], sent.at[kind, peer], came.at[kind, peer], peer
        )

    peers = [lax.rem(me + o, count) for o in far_first(count)]
    for peer in peers:
        exchange(0, g_tx, g_rx, peer).start()
    g_rx[me] = g_tx[me]

    blocks = []
    for i in range(count):
        blocks += [(mh_ref.at[i, 0], 0, i), (mh_ref.at[i, 1], 1, i)]
    spectra(forward, blocks, spec)
    mix_spectra(True, spec, held)
    for i in range(0, count, 2):
        for p, value in enumerate(back_pair(inverse, [spec[2, i], spec[2, i + 1]])):
            y_tx[i + p, 0:rows, :] = value
            if i + p > 0:
                y_tx[i + p - 1, rows : rows + TAIL, :] = value[:TAIL]
    y_tx[count - 1, rows : rows + TAIL, :] = jnp.zeros((TAIL, cw), BF16)
    for peer in peers:
        exchange(1, y_tx, y_ref, peer).start()
    y_ref[me] = y_tx[me]

    for peer in peers:
        arrival(0, g_tx, g_rx, peer).wait_recv()
    spectra(forward, [(g_rx.at[i], 2, i) for i in range(count)], spec)
    mix_spectra(False, spec, held)

    def give(piece):
        @pl.when(piece != me)
        def _():
            exchange(2, b_tx, b_ref, piece).start()

        @pl.when(piece == me)
        def _():
            b_ref[me] = b_tx[me]

    half = count // 2
    start = lax.rem(me // 2 + half // 2, half)
    for k in range(half):
        at = 2 * lax.rem(start + k, half)
        last = lax.rem(at + count - 1, count)
        backs = back_pair(inverse, [spec[1, at], spec[1, at + 1]])
        longs = back_pair(inverse, [spec[0, at], spec[0, at + 1]])
        for p in range(2):
            b_tx[at + p, 0:rows, :] = backs[p]
            b_tx[at + p, rows + TAIL : 2 * rows + TAIL, :] = longs[p]
        b_tx[at, rows : rows + TAIL, :] = backs[1][:TAIL]
        head = backs[0][:TAIL]
        b_tx[last, rows : rows + TAIL, :] = jnp.where(at == 0, jnp.zeros_like(head), head)
        if k > 0:
            give(last)
        give(at)
    give(lax.rem(2 * start + count - 1, count))

    for kind, source, target in ((1, y_tx, y_ref), (2, b_tx, b_ref)):
        for peer in peers:
            arrival(kind, source, target, peer).wait_recv()
    for kind, source, target in ((0, g_tx, g_rx), (1, y_tx, y_ref), (2, b_tx, b_ref)):
        for peer in peers:
            exchange(kind, source, target, peer).wait_send()
    edge.wait()

    @pl.when(me == count - 1)
    def _():
        edge_ref[...] = jnp.zeros_like(edge_ref)


def sum_kernel(part_ref, short_ref, skip_ref, one_rx, total, two_rx, sent, came):
    count = part_ref.shape[0]
    cw = part_ref.shape[2]
    tap_count = short_ref.shape[1]
    me = lax.axis_index("ctx")
    greet([("ctx", count)])
    peers = [lax.rem(me + o, count) for o in far_first(count)]

    def exchange(kind, source, target, peer):
        return send(source, target.at[me], sent.at[kind, peer], came.at[kind, me], peer)

    def arrival(kind, source, target, peer):
        return send(source, target.at[peer], sent.at[kind, peer], came.at[kind, peer], peer)

    for peer in peers:
        exchange(0, part_ref.at[peer], one_rx, peer).start()
    one_rx[me] = part_ref[me]
    for peer in peers:
        arrival(0, part_ref.at[peer], one_rx, peer).wait_recv()
    value = one_rx[0]
    for c in range(1, count):
        value = value + one_rx[c]
    total[...] = value
    for peer in peers:
        exchange(1, total, two_rx, peer).start()
    two_rx[me] = value
    for peer in peers:
        arrival(1, total, two_rx, peer).wait_recv()
    for c in range(count):
        lanes = slice(c * cw, (c + 1) * cw)
        for s in range(3):
            short_ref[s, :, lanes] = two_rx[c, s * tap_count : (s + 1) * tap_count, :]
        skip_ref[:, lanes] = two_rx[c, 3 * tap_count : 3 * tap_count + 1, :]
    for peer in peers:
        exchange(0, part_ref.at[peer], one_rx, peer).wait_send()
        exchange(1, total, two_rx, peer).wait_send()


def leave_kernel(pieces, q_ref, k_ref, v_ref, before, after, go_ref, go_after, taps, skip_ref,
                 y_ref, b_ref, dq_ref, dk_ref, dv_ref, long_ref, sums_ref, ext, go_ext, grad_ext):
    rows, width = q_ref.shape
    cw = width // pieces
    rim = taps.shape[1] - 1
    tap_count = taps.shape[1]
    more = rows + PAD
    sums_ref[...] = jnp.zeros_like(sums_ref)
    for c in range(pieces):
        lanes = slice(c * cw, (c + 1) * cw)
        filtered = []
        for s, ref in enumerate((q_ref, k_ref, v_ref)):
            fill(ext.at[s], before[s, TAIL - rim :, lanes], ref[:, lanes], after[s, 0:rim, lanes], rim)
            filtered.append(short(ext.at[s], taps, more, lanes, s))
        fill(go_ext, jnp.zeros((rim, cw), F32), go_ref[:, lanes], go_after[0:rim, lanes], rim)
        grad_o = go_ext[PAD : PAD + more, :]
        mixed = filtered[1] * filtered[2]
        grad_y = grad_o * filtered[0]
        gain = skip_ref[:, lanes]
        y_full = y_ref[c, 0:more, :].astype(F32) + gain * mixed
        at = rows + TAIL
        grad_mixed = b_ref[c, 0:more, :].astype(F32) + gain * grad_y
        grad_ext[0, 0:more, :] = grad_o * y_full
        grad_ext[1, 0:more, :] = grad_mixed * filtered[2]
        grad_ext[2, 0:more, :] = grad_mixed * filtered[1]
        long_ref[:, lanes] = b_ref[c, at : at + rows, :].astype(F32)
        for s, ref in enumerate((dq_ref, dk_ref, dv_ref)):
            total = None
            own = grad_ext[s, 0:rows, :]
            for j in range(tap_count):
                term = taps[s, j : j + 1, lanes] * grad_ext[s, j : j + rows, :]
                total = term if total is None else total + term
                stream = ext[s, PAD - j : PAD - j + rows, :]
                row = s * tap_count + j
                sums_ref[c, row : row + 1, :] = jnp.sum(own * stream, axis=0, keepdims=True)
            ref[:, lanes] = total.astype(BF16)
        row = 3 * tap_count
        sums_ref[c, row : row + 1, :] = jnp.sum(
            grad_y[0:rows] * mixed[0:rows], axis=0, keepdims=True
        )


def call(kernel, out_shape, scratch, *args, hbm=(), **params):
    vmem = pl.BlockSpec(memory_space=pltpu.VMEM)
    return pl.pallas_call(
        kernel,
        out_shape=out_shape,
        in_specs=[pl.BlockSpec(memory_space=pl.ANY) if i in hbm else vmem
                  for i in range(len(args))],
        out_specs=jax.tree.map(lambda _: vmem, out_shape),
        scratch_shapes=scratch,
        compiler_params=pltpu.CompilerParams(**PARAMS, **params),
    )(*args)


def whole_kernel(names, *refs):
    s = types.SimpleNamespace(**dict(zip(names, refs)))
    count, rows, cw = s.h_rx.shape
    parts, pieces = s.held.shape[:2]
    cols = s.d_own.shape[1]
    piece = cols // pieces
    tap_count = s.taps.shape[1]
    rim = tap_count - 1
    more = rows + PAD
    me = lax.axis_index("ctx")
    mine = lax.axis_index("ch")
    partner = mine + 1 - 2 * lax.rem(mine, 2)
    rest = [lax.rem(mine + 2 * o, parts) for o in range(1, parts // 2)]
    other = [lax.rem(partner + 2 * o, parts) for o in range(1, parts // 2)]
    after_me = lax.rem(me + 1, count)
    before_me = lax.rem(me + count - 1, count)
    peers = [lax.rem(me + o, count) for o in far_first(count)]
    streams = (s.q_hbm, s.k_hbm, s.v_hbm)

    def load(source, target, i):
        return pltpu.make_async_copy(source, target, s.load_sem.at[i])

    long_load = load(s.long_hbm, s.long_own, 0)
    stream_loads = [load(streams[i], s.own.at[i], 1 + i) for i in range(3)]
    d_load = load(s.d_hbm, s.d_own, 4)
    table_loads = [load(s.fwd_hbm, s.fwd, 5), load(s.inv_hbm, s.inv, 6)]

    def weight(part):
        lanes = pl.ds(pl.multiple_of(part * cols, cols), cols)
        return pltpu.make_async_copy(s.w_hbm.at[:, lanes], s.weights.at[part], s.w_sem.at[part])

    long_load.start()
    for i in (1, 2, 0):
        stream_loads[i].start()
    d_load.start()
    weight(mine).start()
    weight(partner).start()
    for table in table_loads:
        table.start()
    for part in [p for pair in zip(rest, other) for p in pair]:
        weight(part).start()

    greet([("ctx", count), ("ch", parts)])

    edges = []
    for i in (1, 2, 0):
        edges.append(send(streams[i].at[rows - TAIL : rows], s.before.at[i], s.edge_sent.at[i],
                          s.edge_came.at[i], after_me))
    for i in (1, 2, 0):
        edges.append(send(streams[i].at[0:TAIL], s.after.at[i], s.edge_sent.at[3 + i],
                          s.edge_came.at[3 + i], before_me))
    for edge in edges:
        edge.start()

    def own(slot, p, peer):
        lanes = slice(p * piece, (p + 1) * piece)
        return send(s.d_hbm.at[:, lanes], s.held.at[mine, p], s.own_sent.at[slot, p],
                    s.d_came.at[mine, p], peer, "ch")

    def passed(slot, p, part):
        return send(s.held.at[part, p], s.held.at[part, p], s.pass_sent.at[slot, p],
                    s.d_came.at[part, p], partner, "ch")

    for p in range(pieces):
        for slot, peer in enumerate(rest + [partner]):
            own(slot, p, peer).start()

    def exchange(kind, source, target, peer):
        return send(source.at[peer], target.at[me], s.sent.at[kind, peer], s.came.at[kind, me],
                    peer)

    def arrival(kind, source, target, peer):
        return send(source.at[peer], target.at[peer], s.sent.at[kind, peer],
                    s.came.at[kind, peer], peer)

    def arrive(kind, source, target):
        for peer in peers:
            arrival(kind, source, target, peer).wait_recv()

    def chunk(c):
        return pl.ds(pl.multiple_of(c * cw, cw), cw)

    def filtered(i, lanes):
        total = None
        for j in range(tap_count):
            term = s.taps[i, j : j + 1, lanes] * s.ext[i, PAD - j : PAD - j + more, lanes]
            total = term if total is None else total + term
        return total

    def fill_own(i):
        def body(c, carry):
            lanes = chunk(c)
            s.ext[i, 0:PAD, lanes] = jnp.zeros((PAD, cw), F32)
            s.ext[i, PAD + rows :, lanes] = jnp.zeros((3 * PAD, cw), F32)
            s.ext[i, PAD : PAD + rows, lanes] = s.own[i, :, lanes].astype(F32)
            return carry

        lax.fori_loop(0, count, body, 0)

    def fill_rim(i):
        s.ext[i, PAD - rim : PAD, :] = s.before[i, TAIL - rim :, :].astype(F32)
        s.ext[i, PAD + rows : PAD + rows + rim, :] = s.after[i, 0:rim, :].astype(F32)

    long_load.wait()
    for peer in peers + [me]:
        s.h_tx[peer] = s.long_own[:, chunk(peer)].astype(BF16)
        if peer is not me:
            exchange(0, s.h_tx, s.h_rx, peer).start()
    s.h_rx[me] = s.h_tx[me]

    for i in (1, 2, 0):
        stream_loads[i].wait()
        fill_own(i)
    for edge in edges:
        edge.wait()

    @pl.when(me == 0)
    def _():
        s.before[...] = jnp.zeros_like(s.before)

    @pl.when(me == count - 1)
    def _():
        s.after[...] = jnp.zeros_like(s.after)

    for i in (1, 2, 0):
        fill_rim(i)
    for peer in peers + [me]:
        lanes = chunk(peer)
        keyed = filtered(1, lanes)
        valued = filtered(2, lanes)
        s.filt[1, :, lanes] = keyed
        s.filt[2, :, lanes] = valued
        s.m_tx[peer] = (keyed[0:rows] * valued[0:rows]).astype(BF16)
        if peer is not me:
            exchange(1, s.m_tx, s.m_rx, peer).start()
    s.m_rx[me] = s.m_tx[me]

    def query(c, carry):
        s.filt[0, :, chunk(c)] = filtered(0, chunk(c))
        return carry

    lax.fori_loop(0, count, query, 0)

    def product(data, part, p=None):
        lanes = slice(None) if p is None else slice(p * piece, (p + 1) * piece)
        return lax.dot_general(data, s.weights[part, :, lanes], (((1,), (1,)), ((), ())),
                               preferred_element_type=F32)

    def take(part, p):
        s.total[...] += product(s.held[part, p], part, p)

    d_load.wait()
    weight(mine).wait()
    s.total[...] = product(s.d_own[...], mine)
    weight(partner).wait()
    for p in range(pieces):
        passed(0, p, partner).wait_recv()
        take(partner, p)

    def relay(slot, direct, relayed, p):
        passed(slot, p, direct).wait_recv()
        passed(slot, p, direct).start()
        take(direct, p)
        passed(slot, p, relayed).wait_recv()
        take(relayed, p)

    steps = [(slot, pair, p) for slot, pair in enumerate(zip(rest, other)) for p in range(pieces)]
    for direct, relayed in zip(rest, other):
        weight(direct).wait()
        weight(relayed).wait()
    for table in table_loads:
        table.wait()
    for at, (slot, (direct, relayed), p) in enumerate(steps):
        if at == len(steps) // 2:
            arrive(0, s.h_tx, s.h_rx)
            spectra(s.fwd, [(s.h_rx.at[i], 1, i) for i in range(count)], s.spec)
        relay(slot, direct, relayed, p)
    if not steps:
        arrive(0, s.h_tx, s.h_rx)
        spectra(s.fwd, [(s.h_rx.at[i], 1, i) for i in range(count)], s.spec)

    s.go_head[...] = s.total[0:TAIL, :].astype(BF16)
    edge = send(s.go_head, s.go_after, s.edge_sent.at[6], s.edge_came.at[6], before_me)
    edge.start()
    for peer in peers + [me]:
        lanes = chunk(peer)
        value = s.total[:, lanes].astype(BF16).astype(F32)
        s.go[0:rows, lanes] = value
        s.g_tx[peer] = (value * s.filt[0, 0:rows, lanes]).astype(BF16)
        if peer is not me:
            exchange(2, s.g_tx, s.g_rx, peer).start()
    s.g_rx[me] = s.g_tx[me]

    half = count // 2
    start = lax.rem(me // 2 + half // 2, half)

    def give(kind, source, target, to):
        @pl.when(to != me)
        def _():
            exchange(kind, source, target, to).start()

    def deliver(kind, source, target, at_spec, tail):
        for k in range(half):
            at = 2 * lax.rem(start + k, half)
            last = lax.rem(at + count - 1, count)
            out = back_pair(s.inv, [s.spec[at_spec, at], s.spec[at_spec, at + 1]])
            for p in range(2):
                source[at + p, 0:rows, :] = out[p]
            if not tail:
                give(kind, source, target, at)
                give(kind, source, target, at + 1)
                continue
            head = out[0][:TAIL]
            source[at, rows : rows + TAIL, :] = out[1][:TAIL]
            source[last, rows : rows + TAIL, :] = jnp.where(at == 0, jnp.zeros_like(head), head)
            if k > 0:
                give(kind, source, target, last)
            give(kind, source, target, at)
        if tail:
            give(kind, source, target, lax.rem(2 * start + count - 1, count))

    arrive(1, s.m_tx, s.m_rx)
    spectra(s.fwd, [(s.m_rx.at[i], 0, i) for i in range(count)], s.spec)
    mix(s.spec, "y")
    deliver(3, s.y_tx, s.y_rx, 2, True)
    s.y_rx[me] = s.y_tx[me]

    arrive(2, s.g_tx, s.g_rx)
    spectra(s.fwd, [(s.g_rx.at[i], 2, i) for i in range(count)], s.spec)
    mix(s.spec, "b")
    deliver(4, s.b_tx, s.b_rx, 1, True)
    s.b_rx[me] = s.b_tx[me]
    mix(s.spec, "l")
    deliver(5, s.l_tx, s.l_hbm, 0, False)
    l_own = pltpu.make_async_copy(s.l_tx.at[me], s.l_hbm.at[me], s.out_sem.at[3])
    l_own.start()

    edge.wait()

    @pl.when(me == count - 1)
    def _():
        s.go_after[...] = jnp.zeros_like(s.go_after)

    s.go[rows:, :] = jnp.zeros_like(s.go[rows:, :])
    s.go[rows : rows + rim, :] = s.go_after[0:rim, :].astype(F32)

    def finish(i, c, lanes, grad):
        s.grad[i, 0:more, :] = grad
        own_rows = grad[0:rows]
        total = None
        for j in range(tap_count):
            term = s.taps[i, j : j + 1, lanes] * s.grad[i, j : j + rows, :]
            total = term if total is None else total + term
            stream = s.ext[i, PAD - j : PAD - j + rows, lanes]
            row = i * tap_count + j
            s.part[c, row : row + 1, :] = jnp.sum(own_rows * stream, axis=0, keepdims=True)
        s.done[i, :, lanes] = total.astype(BF16)

    def first_half(c, carry):
        lanes = chunk(c)
        mixed = s.filt[1, :, lanes] * s.filt[2, :, lanes]
        grad_o = s.go[:, lanes]
        grad_y = grad_o * s.filt[0, :, lanes]
        row = 3 * tap_count
        s.part[c, row:, :] = jnp.zeros((16 - row, cw), F32)
        s.part[c, row : row + 1, :] = jnp.sum(grad_y[0:rows] * mixed[0:rows], axis=0, keepdims=True)
        y_full = s.y_rx[c, 0:more, :].astype(F32) + s.skip[:, lanes] * mixed
        finish(0, c, lanes, grad_o * y_full)
        return carry

    def second_half(c, carry):
        lanes = chunk(c)
        grad_y = s.go[:, lanes] * s.filt[0, :, lanes]
        grad_mixed = s.b_rx[c, 0:more, :].astype(F32) + s.skip[:, lanes] * grad_y
        finish(1, c, lanes, grad_mixed * s.filt[2, :, lanes])
        finish(2, c, lanes, grad_mixed * s.filt[1, :, lanes])
        return carry

    outs = [pltpu.make_async_copy(s.done.at[i], ref, s.out_sem.at[i])
            for i, ref in enumerate((s.dq_hbm, s.dk_hbm, s.dv_hbm))]
    arrive(3, s.y_tx, s.y_rx)
    lax.fori_loop(0, count, first_half, 0)
    outs[0].start()
    arrive(4, s.b_tx, s.b_rx)
    lax.fori_loop(0, count, second_half, 0)

    for peer in peers:
        exchange(6, s.part, s.one_rx, peer).start()
    outs[1].start()
    outs[2].start()
    s.one_rx[me] = s.part[me]
    arrive(6, s.part, s.one_rx)
    value = s.one_rx[0]
    for c in range(1, count):
        value = value + s.one_rx[c]
    s.sum[...] = value

    def spread(peer):
        return send(s.sum, s.sums_hbm.at[me], s.sent.at[7, peer], s.came.at[7, me], peer)

    for peer in peers:
        spread(peer).start()
    sums_own = pltpu.make_async_copy(s.sum, s.sums_hbm.at[me], s.out_sem.at[4])
    sums_own.start()

    for peer in peers:
        send(s.sum, s.sums_hbm.at[peer], s.sent.at[7, peer], s.came.at[7, peer], peer).wait_recv()
    arrive(5, s.l_tx, s.l_hbm)
    for copy in outs + [l_own, sums_own]:
        copy.wait()
    sends = ((s.h_tx, s.h_rx), (s.m_tx, s.m_rx), (s.g_tx, s.g_rx), (s.y_tx, s.y_rx),
             (s.b_tx, s.b_rx), (s.l_tx, s.l_hbm), (s.part, s.one_rx))
    for kind, (source, target) in enumerate(sends):
        for peer in peers:
            exchange(kind, source, target, peer).wait_send()
    for peer in peers:
        spread(peer).wait_send()
    for p in range(pieces):
        for slot, peer in enumerate(rest + [partner]):
            own(slot, p, peer).wait_send()
        for slot, direct in enumerate(rest):
            passed(slot, p, direct).wait_send()


def mix(spec, what):
    count, rows2, cw = spec.shape[1:]
    half = rows2 // 2
    step = 8
    sign = 1.0 - 2.0 * (lax.broadcasted_iota(jnp.int32, (step, cw), 0) % 2).astype(F32)

    def primes(blocks):
        out = [blocks[0]]
        for d in range(1, count):
            re, im = blocks[d]
            old_re, old_im = blocks[d - 1]
            out.append((re - sign * old_im, im + sign * old_re))
        return out

    def chunk(r, carry):
        low = pl.ds(pl.multiple_of(r * step, step), step)
        high = pl.ds(pl.multiple_of(half + r * step, step), step)

        def load(s, i):
            return spec[s, i, low, :], spec[s, i, high, :]

        def save(s, i, value):
            spec[s, i, low, :] = value[0]
            spec[s, i, high, :] = value[1]

        if what == "y":
            taps = primes([load(1, i) for i in range(count)])
            for i in range(count):
                save(1, i, taps[i])
            mixed = [load(0, i) for i in range(count)]
            for i in range(count):
                total = None
                for d in range(i + 1):
                    total = add(total, times(taps[d], mixed[i - d]))
                save(2, i, total)
            return carry
        s = 1 if what == "b" else 0
        taps = [load(s, i) for i in range(count)]
        if what == "l":
            taps = primes(taps)
        grads = [load(2, i) for i in range(count)]
        for b in range(count):
            total = None
            for e in range(count - b):
                total = add(total, conj_times(taps[e], grads[b + e]))
            save(s, b, total)
        return carry

    lax.fori_loop(0, half // step, chunk, 0)


def result_kernel(dq_in, dk_in, dv_in, l_ref, sums_ref,
                  dq_out, dk_out, dv_out, long_ref, short_ref, skip_ref, sem):
    count, rows, cw = l_ref.shape
    tap_count = short_ref.shape[1]
    pairs = ((dq_in, dq_out), (dk_in, dk_out), (dv_in, dv_out))
    copies = [pltpu.make_async_copy(a, b, sem.at[i]) for i, (a, b) in enumerate(pairs)]
    for copy in copies:
        copy.start()
    for c in range(count):
        lanes = slice(c * cw, (c + 1) * cw)
        long_ref[:, lanes] = l_ref[c].astype(F32)
        for i in range(3):
            short_ref[i, :, lanes] = sums_ref[c, i * tap_count : (i + 1) * tap_count, :]
        skip_ref[:, lanes] = sums_ref[c, 3 * tap_count : 3 * tap_count + 1, :]
    for copy in copies:
        copy.wait()


def joined(queries, keys, values, long_filter, short_filters, skip, w_out, d_out):
    ctx = lax.axis_size("ctx")
    parts = lax.axis_size("ch")
    rows, width = queries.shape
    cw = width // ctx
    tap_count = short_filters.shape[1]
    cols = d_out.shape[1]
    pieces = 4
    shape = jax.ShapeDtypeStruct
    dma = pltpu.SemaphoreType.DMA
    forward, inverse = (jnp.asarray(t) for t in tables(rows))
    anyw = pl.BlockSpec(memory_space=pl.ANY)
    vmem = pl.BlockSpec(memory_space=pltpu.VMEM)
    inputs = [
        ("q_hbm", queries, anyw), ("k_hbm", keys, anyw), ("v_hbm", values, anyw),
        ("long_hbm", long_filter, anyw), ("taps", short_filters, vmem),
        ("skip", skip[None], vmem), ("d_hbm", d_out, anyw), ("w_hbm", w_out, anyw),
        ("fwd_hbm", forward, anyw), ("inv_hbm", inverse, anyw),
    ]
    stream = shape((rows, width), BF16)
    outputs = [
        ("dq_hbm", stream), ("dk_hbm", stream), ("dv_hbm", stream),
        ("l_hbm", shape((ctx, rows, cw), BF16)), ("sums_hbm", shape((ctx, 16, cw), F32)),
    ]
    bulk = pltpu.VMEM((ctx, rows, cw), BF16)
    tailed = pltpu.VMEM((ctx, rows + TAIL, cw), BF16)
    small = pltpu.VMEM((ctx, 16, cw), F32)
    rim = pltpu.VMEM((3, TAIL, width), BF16)
    scratch = [
        ("long_own", pltpu.VMEM((rows, width), F32)), ("own", pltpu.VMEM((3, rows, width), BF16)),
        ("d_own", pltpu.VMEM((rows, cols), BF16)), ("fwd", pltpu.VMEM(forward.shape, BF16)),
        ("inv", pltpu.VMEM(inverse.shape, BF16)), ("before", rim), ("after", rim),
        ("ext", pltpu.VMEM((3, rows + 4 * PAD, width), F32)),
        ("filt", pltpu.VMEM((3, rows + PAD, width), F32)),
        ("held", pltpu.VMEM((parts, pieces, rows, cols // pieces), BF16)),
        ("weights", pltpu.VMEM((parts, width, cols), BF16)),
        ("total", pltpu.VMEM((rows, width), F32)),
        ("go", pltpu.VMEM((rows + PAD, width), F32)),
        ("go_head", pltpu.VMEM((TAIL, width), BF16)), ("go_after", pltpu.VMEM((TAIL, width), BF16)),
        ("h_tx", bulk), ("h_rx", bulk), ("m_tx", bulk), ("m_rx", bulk), ("g_tx", bulk),
        ("g_rx", bulk), ("y_tx", tailed), ("y_rx", tailed), ("b_tx", tailed), ("b_rx", tailed),
        ("l_tx", bulk), ("spec", pltpu.VMEM((3, ctx, 2 * rows, cw), F32)),
        ("grad", pltpu.VMEM((3, rows + 4 * PAD, cw), F32)),
        ("done", pltpu.VMEM((3, rows, width), BF16)),
        ("part", small), ("one_rx", small), ("sum", pltpu.VMEM((16, cw), F32)),
        ("load_sem", dma((7,))), ("w_sem", dma((parts,))), ("edge_sent", dma((7,))),
        ("edge_came", dma((7,))), ("own_sent", dma((parts // 2, pieces))),
        ("pass_sent", dma((parts // 2, pieces))), ("d_came", dma((parts, pieces))),
        ("sent", dma((8, ctx))), ("came", dma((8, ctx))), ("out_sem", dma((5,))),
    ]
    names = tuple(name for name, *_ in inputs + outputs + scratch)
    dq, dk, dv, back, sums = pl.pallas_call(
        functools.partial(whole_kernel, names),
        out_shape=[out for _, out in outputs],
        in_specs=[spec for _, _, spec in inputs],
        out_specs=[anyw] * len(outputs),
        scratch_shapes=[kind for _, kind in scratch],
        compiler_params=pltpu.CompilerParams(**PARAMS, collective_id=0, has_side_effects=True),
    )(*[value for _, value, _ in inputs])
    dq, dk, dv, d_long, d_short, d_skip = pl.pallas_call(
        result_kernel,
        out_shape=[stream, stream, stream, shape((rows, width), F32),
                   shape((3, tap_count, width), F32), shape((1, width), F32)],
        in_specs=[anyw, anyw, anyw, vmem, vmem],
        out_specs=[anyw, anyw, anyw, vmem, vmem, vmem],
        scratch_shapes=[dma((3,))],
        compiler_params=pltpu.CompilerParams(**PARAMS),
    )(dq, dk, dv, back, sums)
    return dq, dk, dv, d_long, d_short, d_skip[0]


def per_device(queries, keys, values, long_filter, short_filters, skip, w_out, d_out):
    ctx = lax.axis_size("ctx")
    rows, width = queries.shape
    cw = width // ctx
    if cw % 128 == 0 and ctx <= 8:
        return joined(queries, keys, values, long_filter, short_filters, skip, w_out, d_out)
    tap_count = short_filters.shape[1]
    parts = lax.axis_size("ch")
    cols = d_out.shape[1]
    halves = 2
    ext = pltpu.VMEM((rows + 4 * PAD, cw), F32)
    shape = jax.ShapeDtypeStruct
    dma = pltpu.SemaphoreType.DMA
    edge = shape((3, TAIL, width), BF16)
    pair = (ctx, 2, rows, cw)
    mh, grad_o, before, after = call(
        gather_kernel,
        (shape(pair, BF16), shape((rows, width), BF16), edge, edge),
        [ext, pltpu.VMEM(pair, BF16), pltpu.VMEM((parts, halves, rows, cols // halves), BF16),
         pltpu.VMEM((parts, width, cols), BF16), pltpu.VMEM((rows, width), F32),
         dma((6,)), dma((6,)), dma((ctx,)), dma((ctx,)), dma((parts // 2, halves)),
         dma((parts // 2, halves)), dma((parts, halves)), dma((parts,))],
        queries, keys, values, long_filter, short_filters, d_out, w_out,
        hbm=(6,), collective_id=3, has_side_effects=True,
    )
    forward, inverse = tables(rows)
    spare = ctx if ctx > 8 else 1
    one = shape((ctx, rows + TAIL, cw), BF16)
    two = shape((ctx, 2 * rows + TAIL, cw), BF16)
    piece = pltpu.VMEM((ctx, rows, cw), BF16)
    y, back, go_after = call(
        conv_kernel,
        (one, two, shape((TAIL, width), BF16)),
        [ext, piece, piece, pltpu.VMEM(one.shape, BF16), pltpu.VMEM(two.shape, BF16),
         pltpu.VMEM((3, ctx, 2 * rows, cw), F32), pltpu.VMEM((2, spare, 2, 8, cw), F32),
         pltpu.SemaphoreType.DMA((3, ctx)), pltpu.SemaphoreType.DMA((3, ctx)),
         pltpu.SemaphoreType.DMA((2,))],
        queries, before, grad_o, short_filters, mh, jnp.asarray(forward), jnp.asarray(inverse),
        collective_id=1, has_side_effects=True,
    )
    stream = shape((rows, width), BF16)
    dq, dk, dv, d_long, sums = call(
        functools.partial(leave_kernel, ctx),
        (stream, stream, stream, shape((rows, width), F32), shape((ctx, 16, cw), F32)),
        [pltpu.VMEM((3, rows + 4 * PAD, cw), F32), ext, pltpu.VMEM((3, rows + 4 * PAD, cw), F32)],
        queries, keys, values, before, after, grad_o, go_after, short_filters, skip[None], y, back,
    )
    small = pltpu.VMEM((ctx, 16, cw), F32)
    d_short, d_skip = call(
        sum_kernel,
        (shape((3, tap_count, width), F32), shape((1, width), F32)),
        [small, pltpu.VMEM((16, cw), F32), small,
         pltpu.SemaphoreType.DMA((2, ctx)), pltpu.SemaphoreType.DMA((2, ctx))],
        sums,
        collective_id=2, has_side_effects=True,
    )
    return dq, dk, dv, d_long, d_short, d_skip[0]


def solution(mesh):
    in_specs = (
        P("ctx", "ch"),
        P("ctx", "ch"),
        P("ctx", "ch"),
        P("ctx", "ch"),
        P(None, None, "ch"),
        P("ch"),
        P("ch", None),
        P("ctx", "ch"),
    )
    out_specs = (
        P("ctx", "ch"),
        P("ctx", "ch"),
        P("ctx", "ch"),
        P("ctx", "ch"),
        P(None, None, "ch"),
        P("ch"),
    )
    return jax.shard_map(
        per_device, mesh=mesh, in_specs=in_specs, out_specs=out_specs, check_vma=False
    )
```

```python
import functools
import math
import types

import jax
import jax.numpy as jnp
import numpy as np
from jax import lax
from jax.experimental import pallas as pl
from jax.experimental.pallas import tpu as pltpu
from jax.sharding import PartitionSpec as P

PAD = 8
TAIL = 16
PARAMS = dict(vmem_limit_bytes=60 * 1024 * 1024)
F32 = jnp.float32
BF16 = jnp.bfloat16
MESH = pl.DeviceIdType.MESH


def split_table(table):
    table = table.astype(np.float32)
    high = table.astype(BF16)
    low = (table - high.astype(np.float32)).astype(BF16)
    return np.concatenate([high[None], low[None]], axis=0)


def tables(block):
    freq = np.arange(block)[:, None]
    place = np.arange(block)[None, :]
    angle = (2 * freq + 1) * place % (4 * block) * (math.pi / (2 * block))
    forward = np.concatenate([np.cos(angle), -np.sin(angle)], axis=0)
    return split_table(forward), split_table(forward.T / block)


def fill(scratch, before, own, after, rim):
    rows = own.shape[0]
    scratch[0:PAD, :] = jnp.zeros_like(scratch[0:PAD, :])
    scratch[PAD + rows :, :] = jnp.zeros_like(scratch[PAD + rows :, :])
    scratch[PAD - rim : PAD, :] = before.astype(F32)
    scratch[PAD : PAD + rows, :] = own.astype(F32)
    if after is not None:
        scratch[PAD + rows : PAD + rows + rim, :] = after.astype(F32)


def short(scratch, taps, rows, lanes, s):
    total = None
    for j in range(taps.shape[1]):
        term = taps[s, j : j + 1, lanes] * scratch[PAD - j : PAD - j + rows, :]
        total = term if total is None else total + term
    return total


def times(a, b):
    return a[0] * b[0] - a[1] * b[1], a[0] * b[1] + a[1] * b[0]


def conj_times(a, b):
    return a[0] * b[0] + a[1] * b[1], a[0] * b[1] - a[1] * b[0]


def add(a, b):
    return b if a is None else (a[0] + b[0], a[1] + b[1])


def spectra(table, blocks, spec):
    for at in range(0, len(blocks), 2):
        pair = blocks[at : at + 2]
        data = jnp.concatenate([ref[...] for ref, _, _ in pair], axis=1)
        out = jnp.dot(table[0], data, preferred_element_type=F32) + jnp.dot(
            table[1], data, preferred_element_type=F32
        )
        cw = data.shape[1] // len(pair)
        for p, (_, s, i) in enumerate(pair):
            spec[s, i] = out[:, p * cw : (p + 1) * cw]


def mix_spectra(first, spec, held):
    count, rows2, cw = spec.shape[1:]
    half = rows2 // 2
    step = 8
    sign = 1.0 - 2.0 * (lax.broadcasted_iota(jnp.int32, (step, cw), 0) % 2).astype(F32)
    zero = jnp.zeros((step, cw), F32)

    def primes(blocks):
        out = [blocks[0]]
        for d in range(1, count):
            re, im = blocks[d]
            old_re, old_im = blocks[d - 1]
            out.append((re - sign * old_im, im + sign * old_re))
        return out

    def chunk(r, carry):
        low = pl.ds(pl.multiple_of(r * step, step), step)
        high = pl.ds(pl.multiple_of(half + r * step, step), step)

        def load(s, i):
            return spec[s, i, low, :], spec[s, i, high, :]

        def save(s, i, value):
            spec[s, i, low, :] = value[0]
            spec[s, i, high, :] = value[1]

        def primed(s):
            values = primes([load(s, i) for i in range(count)])
            for i in range(count):
                save(s, i, values[i])
            return values

        if count <= 8 and first:
            taps = primed(1)
            mixed = [load(0, i) for i in range(count)]
            for i in range(count):
                total = None
                for d in range(i + 1):
                    total = add(total, times(taps[d], mixed[i - d]))
                save(2, i, total)
            return carry
        if count <= 8:
            grads = [load(2, i) for i in range(count)]
            for s in (1, 0):
                taps = [load(s, i) for i in range(count)]
                if s == 0:
                    taps = primes(taps)
                for b in range(count):
                    total = None
                    for e in range(count - b):
                        total = add(total, conj_times(taps[e], grads[b + e]))
                    save(s, b, total)
            return carry
        if first:
            primed(1)

            def one(b, inner):
                def of_y(d, total):
                    return add(total, times(load(1, d), load(0, b - d)))

                save(2, b, lax.fori_loop(0, b + 1, of_y, (zero, zero)))
                return inner

            lax.fori_loop(0, count, one, 0)
            return carry
        primed(0)

        def both(b, inner):
            def of_g(e, totals):
                grad = load(2, b + e)
                return (
                    add(totals[0], conj_times(load(1, e), grad)),
                    add(totals[1], conj_times(load(0, e), grad)),
                )

            pair = lax.fori_loop(0, count - b, of_g, ((zero, zero), (zero, zero)))
            for s in range(2):
                held[s, b, 0], held[s, b, 1] = pair[s]
            return inner

        lax.fori_loop(0, count, both, 0)
        for b in range(count):
            save(1, b, (held[0, b, 0], held[0, b, 1]))
            save(0, b, (held[1, b, 0], held[1, b, 1]))
        return carry

    lax.fori_loop(0, half // step, chunk, 0)


def back_pair(table, values):
    data = jnp.concatenate(values, axis=1)
    high = data.astype(BF16)
    low = (data - high.astype(F32)).astype(BF16)
    out = (
        jnp.dot(table[0], high, preferred_element_type=F32)
        + jnp.dot(table[0], low, preferred_element_type=F32)
        + jnp.dot(table[1], high, preferred_element_type=F32)
    )
    cw = data.shape[1] // len(values)
    return [out[:, p * cw : (p + 1) * cw].astype(BF16) for p in range(len(values))]


def greet(sizes):
    barrier = pltpu.get_barrier_semaphore()
    for axis, size in sizes:
        me = lax.axis_index(axis)
        for o in range(1, size):
            peer = lax.rem(me + o, size)
            pl.semaphore_signal(barrier, inc=1, device_id={axis: peer}, device_id_type=MESH)
    pl.semaphore_wait(barrier, sum(size - 1 for _, size in sizes))


def send(source, target, send_sem, recv_sem, peer, axis="ctx"):
    return pltpu.make_async_remote_copy(
        src_ref=source,
        dst_ref=target,
        send_sem=send_sem,
        recv_sem=recv_sem,
        device_id={axis: peer},
        device_id_type=MESH,
    )


def far_first(size):
    return sorted(range(1, size), key=lambda o: abs(o - size // 2))


def gather_kernel(q_ref, k_ref, v_ref, long_ref, taps, d_ref, w_hbm,
                  mh_ref, go_ref, before, after, ext, mh_tx, held, weights, total,
                  edge_sent, edge_came, sent, came, own_sent, pass_sent, d_came, w_sem):
    count, _, rows, cw = mh_ref.shape
    parts, halves = held.shape[:2]
    cols = d_ref.shape[1]
    piece = cols // halves
    rim = taps.shape[1] - 1
    me = lax.axis_index("ctx")
    mine = lax.axis_index("ch")
    partner = mine + 1 - 2 * lax.rem(mine, 2)
    greet([("ctx", count), ("ch", parts)])

    rest = [lax.rem(mine + 2 * o, parts) for o in range(1, parts // 2)]
    other = [lax.rem(partner + 2 * o, parts) for o in range(1, parts // 2)]
    after_me = lax.rem(me + 1, count)
    before_me = lax.rem(me + count - 1, count)

    edges = []
    for s, ref in ((1, k_ref), (2, v_ref), (0, q_ref)):
        edges.append(send(ref.at[rows - TAIL : rows], before.at[s], edge_sent.at[s],
                          edge_came.at[s], after_me))
    for s, ref in ((0, q_ref), (1, k_ref), (2, v_ref)):
        edges.append(send(ref.at[0:TAIL], after.at[s], edge_sent.at[3 + s],
                          edge_came.at[3 + s], before_me))
    for edge in edges:
        edge.start()

    def own(slot, half, peer):
        lanes = slice(half * piece, (half + 1) * piece)
        return send(d_ref.at[:, lanes], held.at[mine, half], own_sent.at[slot, half],
                    d_came.at[mine, half], peer, "ch")

    def passed(slot, half, part):
        return send(held.at[part, half], held.at[part, half], pass_sent.at[slot, half],
                    d_came.at[part, half], partner, "ch")

    for half in range(halves):
        for slot, peer in enumerate(rest + [partner]):
            own(slot, half, peer).start()

    def weight(part):
        lanes = pl.ds(pl.multiple_of(part * cols, cols), cols)
        return pltpu.make_async_copy(w_hbm.at[:, lanes], weights.at[part], w_sem.at[part])

    order = [mine, partner] + [p for pair in zip(rest, other) for p in pair]
    for part in order:
        weight(part).start()
    for edge in edges:
        edge.wait()

    @pl.when(me == 0)
    def _():
        before[...] = jnp.zeros_like(before)

    @pl.when(me == count - 1)
    def _():
        after[...] = jnp.zeros_like(after)

    for c in range(count):
        lanes = slice(c * cw, (c + 1) * cw)
        fill(ext, before[1, TAIL - rim :, lanes], k_ref[:, lanes], None, rim)
        keyed = short(ext, taps, rows, lanes, 1)
        fill(ext, before[2, TAIL - rim :, lanes], v_ref[:, lanes], None, rim)
        mh_tx[c, 0] = (keyed * short(ext, taps, rows, lanes, 2)).astype(BF16)
        mh_tx[c, 1] = long_ref[:, lanes].astype(BF16)

    def exchange(peer):
        return send(mh_tx.at[peer], mh_ref.at[me], sent.at[peer], came.at[me], peer)

    def arrival(peer):
        return send(mh_tx.at[peer], mh_ref.at[peer], sent.at[peer], came.at[peer], peer)

    peers = [lax.rem(me + o, count) for o in far_first(count)]
    for peer in peers:
        exchange(peer).start()
    mh_ref[me] = mh_tx[me]

    def product(data, part, half=None):
        lanes = slice(None) if half is None else slice(half * piece, (half + 1) * piece)
        return lax.dot_general(data, weights[part, :, lanes], (((1,), (1,)), ((), ())),
                               preferred_element_type=F32)

    def take(part, half):
        total[...] += product(held[part, half], part, half)

    weight(mine).wait()
    total[...] = product(d_ref[...], mine)
    weight(partner).wait()
    for half in range(halves):
        passed(0, half, partner).wait_recv()
        take(partner, half)
    for slot, (direct, relayed) in enumerate(zip(rest, other)):
        weight(direct).wait()
        weight(relayed).wait()
        for half in range(halves):
            passed(slot, half, direct).wait_recv()
            passed(slot, half, direct).start()
            take(direct, half)
            passed(slot, half, relayed).wait_recv()
            take(relayed, half)
    go_ref[...] = total[...].astype(BF16)

    for peer in peers:
        arrival(peer).wait_recv()
    for peer in peers:
        exchange(peer).wait_send()
    for half in range(halves):
        for slot, peer in enumerate(rest + [partner]):
            own(slot, half, peer).wait_send()
        for slot, direct in enumerate(rest):
            passed(slot, half, direct).wait_send()


def conv_kernel(q_ref, before, go_ref, taps, mh_ref, forward, inverse, y_ref, b_ref, edge_ref,
                ext, g_tx, g_rx, y_tx, b_tx, spec, held, sent, came, edge_sem):
    count, _, rows, cw = mh_ref.shape
    rim = taps.shape[1] - 1
    me = lax.axis_index("ctx")
    greet([("ctx", count)])
    edge_rows = edge_ref.shape[0]
    previous = lax.rem(me + count - 1, count)
    edge = send(go_ref.at[0:edge_rows], edge_ref, edge_sem.at[0], edge_sem.at[1], previous)
    edge.start()
    for c in range(count):
        lanes = slice(c * cw, (c + 1) * cw)
        fill(ext, before[0, TAIL - rim :, lanes], q_ref[:, lanes], None, rim)
        g_tx[c] = (go_ref[:, lanes].astype(F32) * short(ext, taps, rows, lanes, 0)).astype(BF16)

    def exchange(kind, source, target, peer):
        return send(
            source.at[peer], target.at[me], sent.at[kind, peer], came.at[kind, me], peer
        )

    def arrival(kind, source, target, peer):
        return send(
            source.at[peer], target.at[peer], sent.at[kind, peer], came.at[kind, peer], peer
        )

    peers = [lax.rem(me + o, count) for o in far_first(count)]
    for peer in peers:
        exchange(0, g_tx, g_rx, peer).start()
    g_rx[me] = g_tx[me]

    blocks = []
    for i in range(count):
        blocks += [(mh_ref.at[i, 0], 0, i), (mh_ref.at[i, 1], 1, i)]
    spectra(forward, blocks, spec)
    mix_spectra(True, spec, held)
    for i in range(0, count, 2):
        for p, value in enumerate(back_pair(inverse, [spec[2, i], spec[2, i + 1]])):
            y_tx[i + p, 0:rows, :] = value
            if i + p > 0:
                y_tx[i + p - 1, rows : rows + TAIL, :] = value[:TAIL]
    y_tx[count - 1, rows : rows + TAIL, :] = jnp.zeros((TAIL, cw), BF16)
    for peer in peers:
        exchange(1, y_tx, y_ref, peer).start()
    y_ref[me] = y_tx[me]

    for peer in peers:
        arrival(0, g_tx, g_rx, peer).wait_recv()
    spectra(forward, [(g_rx.at[i], 2, i) for i in range(count)], spec)
    mix_spectra(False, spec, held)

    def give(piece):
        @pl.when(piece != me)
        def _():
            exchange(2, b_tx, b_ref, piece).start()

        @pl.when(piece == me)
        def _():
            b_ref[me] = b_tx[me]

    half = count // 2
    start = lax.rem(me // 2 + half // 2, half)
    for k in range(half):
        at = 2 * lax.rem(start + k, half)
        last = lax.rem(at + count - 1, count)
        backs = back_pair(inverse, [spec[1, at], spec[1, at + 1]])
        longs = back_pair(inverse, [spec[0, at], spec[0, at + 1]])
        for p in range(2):
            b_tx[at + p, 0:rows, :] = backs[p]
            b_tx[at + p, rows + TAIL : 2 * rows + TAIL, :] = longs[p]
        b_tx[at, rows : rows + TAIL, :] = backs[1][:TAIL]
        head = backs[0][:TAIL]
        b_tx[last, rows : rows + TAIL, :] = jnp.where(at == 0, jnp.zeros_like(head), head)
        if k > 0:
            give(last)
        give(at)
    give(lax.rem(2 * start + count - 1, count))

    for kind, source, target in ((1, y_tx, y_ref), (2, b_tx, b_ref)):
        for peer in peers:
            arrival(kind, source, target, peer).wait_recv()
    for kind, source, target in ((0, g_tx, g_rx), (1, y_tx, y_ref), (2, b_tx, b_ref)):
        for peer in peers:
            exchange(kind, source, target, peer).wait_send()
    edge.wait()

    @pl.when(me == count - 1)
    def _():
        edge_ref[...] = jnp.zeros_like(edge_ref)


def sum_kernel(part_ref, short_ref, skip_ref, one_rx, total, two_rx, sent, came):
    count = part_ref.shape[0]
    cw = part_ref.shape[2]
    tap_count = short_ref.shape[1]
    me = lax.axis_index("ctx")
    greet([("ctx", count)])
    peers = [lax.rem(me + o, count) for o in far_first(count)]

    def exchange(kind, source, target, peer):
        return send(source, target.at[me], sent.at[kind, peer], came.at[kind, me], peer)

    def arrival(kind, source, target, peer):
        return send(source, target.at[peer], sent.at[kind, peer], came.at[kind, peer], peer)

    for peer in peers:
        exchange(0, part_ref.at[peer], one_rx, peer).start()
    one_rx[me] = part_ref[me]
    for peer in peers:
        arrival(0, part_ref.at[peer], one_rx, peer).wait_recv()
    value = one_rx[0]
    for c in range(1, count):
        value = value + one_rx[c]
    total[...] = value
    for peer in peers:
        exchange(1, total, two_rx, peer).start()
    two_rx[me] = value
    for peer in peers:
        arrival(1, total, two_rx, peer).wait_recv()
    for c in range(count):
        lanes = slice(c * cw, (c + 1) * cw)
        for s in range(3):
            short_ref[s, :, lanes] = two_rx[c, s * tap_count : (s + 1) * tap_count, :]
        skip_ref[:, lanes] = two_rx[c, 3 * tap_count : 3 * tap_count + 1, :]
    for peer in peers:
        exchange(0, part_ref.at[peer], one_rx, peer).wait_send()
        exchange(1, total, two_rx, peer).wait_send()


def leave_kernel(pieces, q_ref, k_ref, v_ref, before, after, go_ref, go_after, taps, skip_ref,
                 y_ref, b_ref, dq_ref, dk_ref, dv_ref, long_ref, sums_ref, ext, go_ext, grad_ext):
    rows, width = q_ref.shape
    cw = width // pieces
    rim = taps.shape[1] - 1
    tap_count = taps.shape[1]
    more = rows + PAD
    sums_ref[...] = jnp.zeros_like(sums_ref)
    for c in range(pieces):
        lanes = slice(c * cw, (c + 1) * cw)
        filtered = []
        for s, ref in enumerate((q_ref, k_ref, v_ref)):
            fill(ext.at[s], before[s, TAIL - rim :, lanes], ref[:, lanes], after[s, 0:rim, lanes], rim)
            filtered.append(short(ext.at[s], taps, more, lanes, s))
        fill(go_ext, jnp.zeros((rim, cw), F32), go_ref[:, lanes], go_after[0:rim, lanes], rim)
        grad_o = go_ext[PAD : PAD + more, :]
        mixed = filtered[1] * filtered[2]
        grad_y = grad_o * filtered[0]
        gain = skip_ref[:, lanes]
        y_full = y_ref[c, 0:more, :].astype(F32) + gain * mixed
        at = rows + TAIL
        grad_mixed = b_ref[c, 0:more, :].astype(F32) + gain * grad_y
        grad_ext[0, 0:more, :] = grad_o * y_full
        grad_ext[1, 0:more, :] = grad_mixed * filtered[2]
        grad_ext[2, 0:more, :] = grad_mixed * filtered[1]
        long_ref[:, lanes] = b_ref[c, at : at + rows, :].astype(F32)
        for s, ref in enumerate((dq_ref, dk_ref, dv_ref)):
            total = None
            own = grad_ext[s, 0:rows, :]
            for j in range(tap_count):
                term = taps[s, j : j + 1, lanes] * grad_ext[s, j : j + rows, :]
                total = term if total is None else total + term
                stream = ext[s, PAD - j : PAD - j + rows, :]
                row = s * tap_count + j
                sums_ref[c, row : row + 1, :] = jnp.sum(own * stream, axis=0, keepdims=True)
            ref[:, lanes] = total.astype(BF16)
        row = 3 * tap_count
        sums_ref[c, row : row + 1, :] = jnp.sum(
            grad_y[0:rows] * mixed[0:rows], axis=0, keepdims=True
        )


def call(kernel, out_shape, scratch, *args, hbm=(), **params):
    vmem = pl.BlockSpec(memory_space=pltpu.VMEM)
    return pl.pallas_call(
        kernel,
        out_shape=out_shape,
        in_specs=[pl.BlockSpec(memory_space=pl.ANY) if i in hbm else vmem
                  for i in range(len(args))],
        out_specs=jax.tree.map(lambda _: vmem, out_shape),
        scratch_shapes=scratch,
        compiler_params=pltpu.CompilerParams(**PARAMS, **params),
    )(*args)


def whole_kernel(names, *refs):
    s = types.SimpleNamespace(**dict(zip(names, refs)))
    count, rows, cw = s.h_rx.shape
    parts, _, pieces, tall, _ = s.held.shape
    cols = s.d_own.shape[1]
    piece = cols // pieces
    tap_count = s.taps.shape[1]
    rim = tap_count - 1
    me = lax.axis_index("ctx")
    mine = lax.axis_index("ch")
    partner = mine + 1 - 2 * lax.rem(mine, 2)
    rest = [lax.rem(mine + 2 * o, parts) for o in range(1, parts // 2)]
    other = [lax.rem(partner + 2 * o, parts) for o in range(1, parts // 2)]
    after_me = lax.rem(me + 1, count)
    before_me = lax.rem(me + count - 1, count)
    peers = [lax.rem(me + o, count) for o in far_first(count)]
    streams = (s.q_hbm, s.k_hbm, s.v_hbm)

    def load(source, target, i):
        return pltpu.make_async_copy(source, target, s.load_sem.at[i])

    long_load = load(s.long_hbm, s.long_own, 0)
    stream_loads = [load(streams[i], s.own.at[i], 1 + i) for i in range(3)]
    d_load = load(s.d_hbm, s.d_own, 4)
    table_loads = [load(s.fwd_hbm, s.fwd, 5), load(s.inv_hbm, s.inv, 6)]

    def weight(part):
        lanes = pl.ds(pl.multiple_of(part * cols, cols), cols)
        return pltpu.make_async_copy(s.w_hbm.at[:, lanes], s.weights.at[part], s.w_sem.at[part])

    long_load.start()
    for i in (1, 2, 0):
        stream_loads[i].start()
    d_load.start()
    weight(mine).start()
    weight(partner).start()
    for table in table_loads:
        table.start()
    for part in [p for pair in zip(rest, other) for p in pair]:
        weight(part).start()

    greet([("ctx", count), ("ch", parts)])

    edges = []
    for i in (1, 2, 0):
        edges.append(send(streams[i].at[rows - TAIL : rows], s.before.at[i], s.edge_sent.at[i],
                          s.edge_came.at[i], after_me))
    for edge in edges:
        edge.start()

    batches = [(h, p) for h in range(rows // tall) for p in range(pieces)]

    def own(slot, h, p, peer):
        part = s.d_hbm.at[h * tall : (h + 1) * tall, p * piece : (p + 1) * piece]
        return send(part, s.held.at[mine, h, p], s.own_sent.at[slot, h, p],
                    s.d_came.at[mine, h, p], peer, "ch")

    def passed(slot, h, p, part):
        return send(s.held.at[part, h, p], s.held.at[part, h, p], s.pass_sent.at[slot, h, p],
                    s.d_came.at[part, h, p], partner, "ch")

    for h, p in batches:
        for slot, peer in enumerate(rest + [partner]):
            own(slot, h, p, peer).start()

    def exchange(kind, source, target, peer):
        return send(source.at[peer], target.at[me], s.sent.at[kind, peer], s.came.at[kind, me],
                    peer)

    def arrival(kind, source, target, peer):
        return send(source.at[peer], target.at[peer], s.sent.at[kind, peer],
                    s.came.at[kind, peer], peer)

    def arrive(kind, source, target):
        for peer in peers:
            arrival(kind, source, target, peer).wait_recv()

    def chunk(c):
        return pl.ds(pl.multiple_of(c * cw, cw), cw)

    def filtered(i, lanes):
        total = None
        for j in range(tap_count):
            term = s.taps[i, j : j + 1, lanes] * s.ext[i, PAD - j : PAD - j + rows, lanes]
            total = term if total is None else total + term
        return total

    def fill_own(i):
        def body(c, carry):
            lanes = chunk(c)
            s.ext[i, 0:PAD, lanes] = jnp.zeros((PAD, cw), F32)
            s.ext[i, PAD : PAD + rows, lanes] = s.own[i, :, lanes].astype(F32)
            return carry

        lax.fori_loop(0, count, body, 0)

    def fill_rim(i):
        s.ext[i, PAD - rim : PAD, :] = s.before[i, TAIL - rim :, :].astype(F32)

    long_load.wait()
    for peer in peers + [me]:
        s.h_tx[peer] = s.long_own[:, chunk(peer)].astype(BF16)
        if peer is not me:
            exchange(0, s.h_tx, s.h_rx, peer).start()
    s.h_rx[me] = s.h_tx[me]

    for i in (1, 2, 0):
        stream_loads[i].wait()
        fill_own(i)
    for edge in edges:
        edge.wait()

    @pl.when(me == 0)
    def _():
        s.before[...] = jnp.zeros_like(s.before)

    for i in (1, 2, 0):
        fill_rim(i)
    for peer in peers + [me]:
        lanes = chunk(peer)
        keyed = filtered(1, lanes)
        valued = filtered(2, lanes)
        s.filt[1, :, lanes] = keyed
        s.filt[2, :, lanes] = valued
        s.m_tx[peer] = (keyed * valued).astype(BF16)
        if peer is not me:
            exchange(1, s.m_tx, s.m_rx, peer).start()
    s.m_rx[me] = s.m_tx[me]

    def query(c, carry):
        s.filt[0, :, chunk(c)] = filtered(0, chunk(c))
        return carry

    lax.fori_loop(0, count, query, 0)

    def product(data, part, p=None):
        lanes = slice(None) if p is None else slice(p * piece, (p + 1) * piece)
        return lax.dot_general(data, s.weights[part, :, lanes], (((1,), (1,)), ((), ())),
                               preferred_element_type=F32)

    def take(part, h, p):
        s.total[h * tall : (h + 1) * tall, :] += product(s.held[part, h, p], part, p)

    def g_send(h, source, target, peer, slot):
        at = slice(h * tall, (h + 1) * tall)
        return send(source.at[peer, at], target.at[slot, at], s.g_sent.at[h, peer],
                    s.g_came.at[h, slot], peer)

    def gradient(h):
        at = slice(h * tall, (h + 1) * tall)
        for peer in peers + [me]:
            lanes = chunk(peer)
            value = s.total[at, lanes].astype(BF16).astype(F32)
            s.go[at, lanes] = value
            s.g_tx[peer, at, :] = (value * s.filt[0, at, lanes]).astype(BF16)
            if peer is not me:
                g_send(h, s.g_tx, s.g_rx, peer, me).start()
        s.g_rx[me, at, :] = s.g_tx[me, at, :]

    def long_spectra():
        arrive(0, s.h_tx, s.h_rx)
        spectra(s.fwd, [(s.h_rx.at[i], 1, i) for i in range(count)], s.spec)

    d_load.wait()
    weight(mine).wait()
    s.total[...] = product(s.d_own[...], mine)
    weight(partner).wait()
    for h, p in batches:
        passed(0, h, p, partner).wait_recv()
        take(partner, h, p)
    for direct, relayed in zip(rest, other):
        weight(direct).wait()
        weight(relayed).wait()
    for table in table_loads:
        table.wait()
    for h in range(rows // tall):
        for p in range(pieces):
            for slot, (direct, relayed) in enumerate(zip(rest, other)):
                passed(slot, h, p, direct).wait_recv()
                passed(slot, h, p, direct).start()
                take(direct, h, p)
                passed(slot, h, p, relayed).wait_recv()
                take(relayed, h, p)
        gradient(h)
        if h == 0:
            long_spectra()

    half = count // 2
    start = lax.rem(me // 2 + half // 2, half)

    def give_b(to):
        @pl.when(to != me)
        def _():
            exchange(4, s.b_tx, s.b_rx, to).start()

    def keep(to):
        pass

    def deliver(give, source, at_spec):
        for k in range(half):
            at = 2 * lax.rem(start + k, half)
            out = back_pair(s.inv, [s.spec[at_spec, at], s.spec[at_spec, at + 1]])
            for p in range(2):
                source[at + p] = out[p]
                give(at + p)

    arrive(1, s.m_tx, s.m_rx)
    spectra(s.fwd, [(s.m_rx.at[i], 0, i) for i in range(count)], s.spec)
    mix(s.spec, "y")
    deliver(keep, s.y_tx, 2)
    s.y_rx[me] = s.y_tx[me]

    for h in range(rows // tall):
        for peer in peers:
            g_send(h, s.g_tx, s.g_rx, peer, peer).wait_recv()
    for peer in peers:
        exchange(3, s.y_tx, s.y_rx, peer).start()
    spectra(s.fwd, [(s.g_rx.at[i], 2, i) for i in range(count)], s.spec)
    mix(s.spec, "b")
    deliver(give_b, s.b_tx, 1)
    s.b_rx[me] = s.b_tx[me]
    mix(s.spec, "l")
    deliver(keep, s.l_tx, 0)
    l_own = pltpu.make_async_copy(s.l_tx.at[me], s.l_hbm.at[me], s.out_sem.at[3])
    l_own.start()

    def finish(i, c, lanes, grad):
        s.grad[i, 0:rows, :] = grad
        s.grad[i, rows:, :] = jnp.zeros((PAD, cw), F32)
        s.head_tx[i, :, lanes] = grad[0:PAD]
        s.tail[i, 0:TAIL, lanes] = grad[rows - TAIL :]
        total = None
        for j in range(tap_count):
            term = s.taps[i, j : j + 1, lanes] * s.grad[i, j : j + rows, :]
            total = term if total is None else total + term
            stream = s.ext[i, PAD - j : PAD - j + rows, lanes]
            row = i * tap_count + j
            s.part[c, row : row + 1, :] = jnp.sum(grad * stream, axis=0, keepdims=True)
        s.done[i, :, lanes] = total.astype(BF16)

    def first_half(c, carry):
        lanes = chunk(c)
        mixed = s.filt[1, :, lanes] * s.filt[2, :, lanes]
        grad_o = s.go[:, lanes]
        row = 3 * tap_count
        s.part[c, row:, :] = jnp.zeros((16 - row, cw), F32)
        s.part[c, row : row + 1, :] = jnp.sum(
            grad_o * s.filt[0, :, lanes] * mixed, axis=0, keepdims=True
        )
        y_full = s.y_rx[c].astype(F32) + s.skip[:, lanes] * mixed
        finish(0, c, lanes, grad_o * y_full)
        return carry

    def second_half(k, carry):
        middle = count // 2
        c = lax.rem(me + count - middle + (2 * lax.rem(k, 2) - 1) * ((k + 1) // 2), count)

        @pl.when(c != me)
        def _():
            arrival(4, s.b_tx, s.b_rx, c).wait_recv()

        lanes = chunk(c)
        grad_y = s.go[:, lanes] * s.filt[0, :, lanes]
        grad_mixed = s.b_rx[c].astype(F32) + s.skip[:, lanes] * grad_y
        finish(1, c, lanes, grad_mixed * s.filt[2, :, lanes])
        finish(2, c, lanes, grad_mixed * s.filt[1, :, lanes])
        return carry

    heads = [send(s.head_tx.at[i], s.tail.at[i, TAIL : TAIL + PAD], s.edge_sent.at[3 + i],
                  s.edge_came.at[3 + i], before_me) for i in range(3)]
    outs = [pltpu.make_async_copy(s.done.at[i], ref, s.out_sem.at[i])
            for i, ref in enumerate((s.dq_hbm, s.dk_hbm, s.dv_hbm))]

    def mend(i):
        heads[i].wait_recv()

        @pl.when(me == count - 1)
        def _():
            s.tail[i, TAIL:, :] = jnp.zeros_like(s.tail[i, TAIL:, :])

        total = None
        for j in range(tap_count):
            term = s.taps[i, j : j + 1, :] * s.tail[i, j : j + TAIL, :]
            total = term if total is None else total + term
        s.done[i, rows - TAIL :, :] = total.astype(BF16)
        outs[i].start()

    def long_send(some):
        for peer in some:
            exchange(5, s.l_tx, s.l_hbm, peer).start()

    arrive(3, s.y_tx, s.y_rx)
    lax.fori_loop(0, count, first_half, 0)
    heads[0].start()
    lax.fori_loop(0, count, second_half, 0)
    for peer in peers:
        exchange(6, s.part, s.one_rx, peer).start()
    heads[1].start()
    heads[2].start()
    split = 4
    long_send(peers[:split])
    s.one_rx[me] = s.part[me]
    arrive(6, s.part, s.one_rx)
    value = s.one_rx[0]
    for c in range(1, count):
        value = value + s.one_rx[c]
    s.sum[...] = value

    def spread(peer):
        return send(s.sum, s.sums_hbm.at[me], s.sent.at[7, peer], s.came.at[7, me], peer)

    for peer in peers:
        spread(peer).start()
    long_send(peers[split:])
    for i in range(3):
        mend(i)
    sums_own = pltpu.make_async_copy(s.sum, s.sums_hbm.at[me], s.out_sem.at[4])
    sums_own.start()

    for peer in peers:
        send(s.sum, s.sums_hbm.at[peer], s.sent.at[7, peer], s.came.at[7, peer], peer).wait_recv()
    arrive(5, s.l_tx, s.l_hbm)
    for copy in outs + [l_own, sums_own]:
        copy.wait()
    sends = ((0, s.h_tx, s.h_rx), (1, s.m_tx, s.m_rx), (3, s.y_tx, s.y_rx),
             (4, s.b_tx, s.b_rx), (5, s.l_tx, s.l_hbm), (6, s.part, s.one_rx))
    for kind, source, target in sends:
        for peer in peers:
            exchange(kind, source, target, peer).wait_send()
    for h in range(rows // tall):
        for peer in peers:
            g_send(h, s.g_tx, s.g_rx, peer, me).wait_send()
    for peer in peers:
        spread(peer).wait_send()
    for head in heads:
        head.wait_send()
    for h, p in batches:
        for slot, peer in enumerate(rest + [partner]):
            own(slot, h, p, peer).wait_send()
        for slot, direct in enumerate(rest):
            passed(slot, h, p, direct).wait_send()


def mix(spec, what):
    count, rows2, cw = spec.shape[1:]
    half = rows2 // 2
    step = 8
    sign = 1.0 - 2.0 * (lax.broadcasted_iota(jnp.int32, (step, cw), 0) % 2).astype(F32)

    def primes(blocks):
        out = [blocks[0]]
        for d in range(1, count):
            re, im = blocks[d]
            old_re, old_im = blocks[d - 1]
            out.append((re - sign * old_im, im + sign * old_re))
        return out

    def chunk(r, carry):
        low = pl.ds(pl.multiple_of(r * step, step), step)
        high = pl.ds(pl.multiple_of(half + r * step, step), step)

        def load(s, i):
            return spec[s, i, low, :], spec[s, i, high, :]

        def save(s, i, value):
            spec[s, i, low, :] = value[0]
            spec[s, i, high, :] = value[1]

        if what == "y":
            taps = primes([load(1, i) for i in range(count)])
            for i in range(count):
                save(1, i, taps[i])
            mixed = [load(0, i) for i in range(count)]
            for i in range(count):
                total = None
                for d in range(i + 1):
                    total = add(total, times(taps[d], mixed[i - d]))
                save(2, i, total)
            return carry
        s = 1 if what == "b" else 0
        taps = [load(s, i) for i in range(count)]
        if what == "l":
            taps = primes(taps)
        grads = [load(2, i) for i in range(count)]
        for b in range(count):
            total = None
            for e in range(count - b):
                total = add(total, conj_times(taps[e], grads[b + e]))
            save(s, b, total)
        return carry

    lax.fori_loop(0, half // step, chunk, 0)


def result_kernel(dq_in, dk_in, dv_in, l_in, sums_in,
                  dq_out, dk_out, dv_out, long_out, short_ref, skip_ref,
                  streams, l_ref, long_ref, sums_ref, in_sem, out_sem):
    count, rows, cw = l_ref.shape
    tap_count = short_ref.shape[1]

    def copy(a, b, sem):
        return pltpu.make_async_copy(a, b, sem)

    loads = [copy(l_in, l_ref, in_sem.at[3]), copy(sums_in, sums_ref, in_sem.at[4])]
    loads += [copy(ref, streams.at[i], in_sem.at[i])
              for i, ref in enumerate((dq_in, dk_in, dv_in))]
    stores = [copy(streams.at[i], ref, out_sem.at[i])
              for i, ref in enumerate((dq_out, dk_out, dv_out))]
    long_store = copy(long_ref, long_out, out_sem.at[3])
    for load in loads:
        load.start()
    loads[0].wait()
    for c in range(count):
        long_ref[:, c * cw : (c + 1) * cw] = l_ref[c].astype(F32)
    long_store.start()
    for load, store in zip(loads[2:], stores):
        load.wait()
        store.start()
    loads[1].wait()
    for c in range(count):
        lanes = slice(c * cw, (c + 1) * cw)
        for i in range(3):
            short_ref[i, :, lanes] = sums_ref[c, i * tap_count : (i + 1) * tap_count, :]
        skip_ref[:, lanes] = sums_ref[c, 3 * tap_count : 3 * tap_count + 1, :]
    for store in stores + [long_store]:
        store.wait()


def joined(queries, keys, values, long_filter, short_filters, skip, w_out, d_out):
    ctx = lax.axis_size("ctx")
    parts = lax.axis_size("ch")
    rows, width = queries.shape
    cw = width // ctx
    tap_count = short_filters.shape[1]
    cols = d_out.shape[1]
    halves, pieces = 2, 4
    shape = jax.ShapeDtypeStruct
    dma = pltpu.SemaphoreType.DMA
    forward, inverse = (jnp.asarray(t) for t in tables(rows))
    anyw = pl.BlockSpec(memory_space=pl.ANY)
    vmem = pl.BlockSpec(memory_space=pltpu.VMEM)
    inputs = [
        ("q_hbm", queries, anyw), ("k_hbm", keys, anyw), ("v_hbm", values, anyw),
        ("long_hbm", long_filter, anyw), ("taps", short_filters, vmem),
        ("skip", skip[None], vmem), ("d_hbm", d_out, anyw), ("w_hbm", w_out, anyw),
        ("fwd_hbm", forward, anyw), ("inv_hbm", inverse, anyw),
    ]
    stream = shape((rows, width), BF16)
    outputs = [
        ("dq_hbm", stream), ("dk_hbm", stream), ("dv_hbm", stream),
        ("l_hbm", shape((ctx, rows, cw), BF16)), ("sums_hbm", shape((ctx, 16, cw), F32)),
    ]
    bulk = pltpu.VMEM((ctx, rows, cw), BF16)
    small = pltpu.VMEM((ctx, 16, cw), F32)
    rim = pltpu.VMEM((3, TAIL, width), BF16)
    scratch = [
        ("long_own", pltpu.VMEM((rows, width), F32)), ("own", pltpu.VMEM((3, rows, width), BF16)),
        ("d_own", pltpu.VMEM((rows, cols), BF16)), ("fwd", pltpu.VMEM(forward.shape, BF16)),
        ("inv", pltpu.VMEM(inverse.shape, BF16)), ("before", rim), ("tail", pltpu.VMEM((3, TAIL + PAD, width), F32)),
        ("head_tx", pltpu.VMEM((3, PAD, width), F32)),
        ("ext", pltpu.VMEM((3, rows + PAD, width), F32)),
        ("filt", pltpu.VMEM((3, rows, width), F32)),
        ("held", pltpu.VMEM((parts, halves, pieces, rows // halves, cols // pieces), BF16)),
        ("weights", pltpu.VMEM((parts, width, cols), BF16)),
        ("total", pltpu.VMEM((rows, width), F32)),
        ("go", pltpu.VMEM((rows, width), F32)),
        ("h_tx", bulk), ("h_rx", bulk), ("m_tx", bulk), ("m_rx", bulk), ("g_tx", bulk),
        ("g_rx", bulk), ("y_tx", bulk), ("y_rx", bulk), ("b_tx", bulk), ("b_rx", bulk),
        ("l_tx", bulk), ("spec", pltpu.VMEM((3, ctx, 2 * rows, cw), F32)),
        ("grad", pltpu.VMEM((3, rows + PAD, cw), F32)),
        ("done", pltpu.VMEM((3, rows, width), BF16)),
        ("part", small), ("one_rx", small), ("sum", pltpu.VMEM((16, cw), F32)),
        ("load_sem", dma((7,))), ("w_sem", dma((parts,))), ("edge_sent", dma((6,))),
        ("edge_came", dma((6,))), ("own_sent", dma((parts // 2, halves, pieces))),
        ("pass_sent", dma((parts // 2, halves, pieces))), ("d_came", dma((parts, halves, pieces))),
        ("sent", dma((8, ctx))), ("came", dma((8, ctx))), ("out_sem", dma((5,))),
        ("g_sent", dma((halves, ctx))), ("g_came", dma((halves, ctx))),
    ]
    names = tuple(name for name, *_ in inputs + outputs + scratch)
    dq, dk, dv, back, sums = pl.pallas_call(
        functools.partial(whole_kernel, names),
        out_shape=[out for _, out in outputs],
        in_specs=[spec for _, _, spec in inputs],
        out_specs=[anyw] * len(outputs),
        scratch_shapes=[kind for _, kind in scratch],
        compiler_params=pltpu.CompilerParams(**PARAMS, collective_id=0, has_side_effects=True),
    )(*[value for _, value, _ in inputs])
    dq, dk, dv, d_long, d_short, d_skip = pl.pallas_call(
        result_kernel,
        out_shape=[stream, stream, stream, shape((rows, width), F32),
                   shape((3, tap_count, width), F32), shape((1, width), F32)],
        in_specs=[anyw] * 5,
        out_specs=[anyw] * 4 + [vmem] * 2,
        scratch_shapes=[pltpu.VMEM((3, rows, width), BF16), pltpu.VMEM((ctx, rows, cw), BF16),
                        pltpu.VMEM((rows, width), F32), small, dma((5,)), dma((4,))],
        compiler_params=pltpu.CompilerParams(**PARAMS),
    )(dq, dk, dv, back, sums)
    return dq, dk, dv, d_long, d_short, d_skip[0]


def per_device(queries, keys, values, long_filter, short_filters, skip, w_out, d_out):
    ctx = lax.axis_size("ctx")
    rows, width = queries.shape
    cw = width // ctx
    if cw % 128 == 0 and ctx <= 8:
        return joined(queries, keys, values, long_filter, short_filters, skip, w_out, d_out)
    tap_count = short_filters.shape[1]
    parts = lax.axis_size("ch")
    cols = d_out.shape[1]
    halves = 2
    ext = pltpu.VMEM((rows + 4 * PAD, cw), F32)
    shape = jax.ShapeDtypeStruct
    dma = pltpu.SemaphoreType.DMA
    edge = shape((3, TAIL, width), BF16)
    pair = (ctx, 2, rows, cw)
    mh, grad_o, before, after = call(
        gather_kernel,
        (shape(pair, BF16), shape((rows, width), BF16), edge, edge),
        [ext, pltpu.VMEM(pair, BF16), pltpu.VMEM((parts, halves, rows, cols // halves), BF16),
         pltpu.VMEM((parts, width, cols), BF16), pltpu.VMEM((rows, width), F32),
         dma((6,)), dma((6,)), dma((ctx,)), dma((ctx,)), dma((parts // 2, halves)),
         dma((parts // 2, halves)), dma((parts, halves)), dma((parts,))],
        queries, keys, values, long_filter, short_filters, d_out, w_out,
        hbm=(6,), collective_id=3, has_side_effects=True,
    )
    forward, inverse = tables(rows)
    spare = ctx if ctx > 8 else 1
    one = shape((ctx, rows + TAIL, cw), BF16)
    two = shape((ctx, 2 * rows + TAIL, cw), BF16)
    piece = pltpu.VMEM((ctx, rows, cw), BF16)
    y, back, go_after = call(
        conv_kernel,
        (one, two, shape((TAIL, width), BF16)),
        [ext, piece, piece, pltpu.VMEM(one.shape, BF16), pltpu.VMEM(two.shape, BF16),
         pltpu.VMEM((3, ctx, 2 * rows, cw), F32), pltpu.VMEM((2, spare, 2, 8, cw), F32),
         pltpu.SemaphoreType.DMA((3, ctx)), pltpu.SemaphoreType.DMA((3, ctx)),
         pltpu.SemaphoreType.DMA((2,))],
        queries, before, grad_o, short_filters, mh, jnp.asarray(forward), jnp.asarray(inverse),
        collective_id=1, has_side_effects=True,
    )
    stream = shape((rows, width), BF16)
    dq, dk, dv, d_long, sums = call(
        functools.partial(leave_kernel, ctx),
        (stream, stream, stream, shape((rows, width), F32), shape((ctx, 16, cw), F32)),
        [pltpu.VMEM((3, rows + 4 * PAD, cw), F32), ext, pltpu.VMEM((3, rows + 4 * PAD, cw), F32)],
        queries, keys, values, before, after, grad_o, go_after, short_filters, skip[None], y, back,
    )
    small = pltpu.VMEM((ctx, 16, cw), F32)
    d_short, d_skip = call(
        sum_kernel,
        (shape((3, tap_count, width), F32), shape((1, width), F32)),
        [small, pltpu.VMEM((16, cw), F32), small,
         pltpu.SemaphoreType.DMA((2, ctx)), pltpu.SemaphoreType.DMA((2, ctx))],
        sums,
        collective_id=2, has_side_effects=True,
    )
    return dq, dk, dv, d_long, d_short, d_skip[0]


def solution(mesh):
    in_specs = (
        P("ctx", "ch"),
        P("ctx", "ch"),
        P("ctx", "ch"),
        P("ctx", "ch"),
        P(None, None, "ch"),
        P("ch"),
        P("ch", None),
        P("ctx", "ch"),
    )
    out_specs = (
        P("ctx", "ch"),
        P("ctx", "ch"),
        P("ctx", "ch"),
        P("ctx", "ch"),
        P(None, None, "ch"),
        P("ch"),
    )
    return jax.shard_map(
        per_device, mesh=mesh, in_specs=in_specs, out_specs=out_specs, check_vma=False
    )
```

```python
import functools
import math
import types

import jax
import jax.numpy as jnp
import numpy as np
from jax import lax
from jax.experimental import pallas as pl
from jax.experimental.pallas import tpu as pltpu
from jax.sharding import PartitionSpec as P

PAD = 8
TAIL = 16
PARAMS = dict(vmem_limit_bytes=60 * 1024 * 1024)
F32 = jnp.float32
BF16 = jnp.bfloat16
MESH = pl.DeviceIdType.MESH


def split_table(table):
    table = table.astype(np.float32)
    high = table.astype(BF16)
    low = (table - high.astype(np.float32)).astype(BF16)
    return np.concatenate([high[None], low[None]], axis=0)


def tables(block):
    freq = np.arange(block)[:, None]
    place = np.arange(block)[None, :]
    angle = (2 * freq + 1) * place % (4 * block) * (math.pi / (2 * block))
    forward = np.concatenate([np.cos(angle), -np.sin(angle)], axis=0)
    return split_table(forward), split_table(forward.T / block)


def fill(scratch, before, own, after, rim):
    rows = own.shape[0]
    scratch[0:PAD, :] = jnp.zeros_like(scratch[0:PAD, :])
    scratch[PAD + rows :, :] = jnp.zeros_like(scratch[PAD + rows :, :])
    scratch[PAD - rim : PAD, :] = before.astype(F32)
    scratch[PAD : PAD + rows, :] = own.astype(F32)
    if after is not None:
        scratch[PAD + rows : PAD + rows + rim, :] = after.astype(F32)


def short(scratch, taps, rows, lanes, s):
    total = None
    for j in range(taps.shape[1]):
        term = taps[s, j : j + 1, lanes] * scratch[PAD - j : PAD - j + rows, :]
        total = term if total is None else total + term
    return total


def times(a, b):
    return a[0] * b[0] - a[1] * b[1], a[0] * b[1] + a[1] * b[0]


def conj_times(a, b):
    return a[0] * b[0] + a[1] * b[1], a[0] * b[1] - a[1] * b[0]


def add(a, b):
    return b if a is None else (a[0] + b[0], a[1] + b[1])


def spectra(table, blocks, spec):
    for at in range(0, len(blocks), 2):
        pair = blocks[at : at + 2]
        data = jnp.concatenate([ref[...] for ref, _, _ in pair], axis=1)
        out = jnp.dot(table[0], data, preferred_element_type=F32) + jnp.dot(
            table[1], data, preferred_element_type=F32
        )
        cw = data.shape[1] // len(pair)
        for p, (_, s, i) in enumerate(pair):
            spec[s, i] = out[:, p * cw : (p + 1) * cw]


def mix_spectra(first, spec, held):
    count, rows2, cw = spec.shape[1:]
    half = rows2 // 2
    step = 8
    sign = 1.0 - 2.0 * (lax.broadcasted_iota(jnp.int32, (step, cw), 0) % 2).astype(F32)
    zero = jnp.zeros((step, cw), F32)

    def primes(blocks):
        out = [blocks[0]]
        for d in range(1, count):
            re, im = blocks[d]
            old_re, old_im = blocks[d - 1]
            out.append((re - sign * old_im, im + sign * old_re))
        return out

    def chunk(r, carry):
        low = pl.ds(pl.multiple_of(r * step, step), step)
        high = pl.ds(pl.multiple_of(half + r * step, step), step)

        def load(s, i):
            return spec[s, i, low, :], spec[s, i, high, :]

        def save(s, i, value):
            spec[s, i, low, :] = value[0]
            spec[s, i, high, :] = value[1]

        def primed(s):
            values = primes([load(s, i) for i in range(count)])
            for i in range(count):
                save(s, i, values[i])
            return values

        if count <= 8 and first:
            taps = primed(1)
            mixed = [load(0, i) for i in range(count)]
            for i in range(count):
                total = None
                for d in range(i + 1):
                    total = add(total, times(taps[d], mixed[i - d]))
                save(2, i, total)
            return carry
        if count <= 8:
            grads = [load(2, i) for i in range(count)]
            for s in (1, 0):
                taps = [load(s, i) for i in range(count)]
                if s == 0:
                    taps = primes(taps)
                for b in range(count):
                    total = None
                    for e in range(count - b):
                        total = add(total, conj_times(taps[e], grads[b + e]))
                    save(s, b, total)
            return carry
        if first:
            primed(1)

            def one(b, inner):
                def of_y(d, total):
                    return add(total, times(load(1, d), load(0, b - d)))

                save(2, b, lax.fori_loop(0, b + 1, of_y, (zero, zero)))
                return inner

            lax.fori_loop(0, count, one, 0)
            return carry
        primed(0)

        def both(b, inner):
            def of_g(e, totals):
                grad = load(2, b + e)
                return (
                    add(totals[0], conj_times(load(1, e), grad)),
                    add(totals[1], conj_times(load(0, e), grad)),
                )

            pair = lax.fori_loop(0, count - b, of_g, ((zero, zero), (zero, zero)))
            for s in range(2):
                held[s, b, 0], held[s, b, 1] = pair[s]
            return inner

        lax.fori_loop(0, count, both, 0)
        for b in range(count):
            save(1, b, (held[0, b, 0], held[0, b, 1]))
            save(0, b, (held[1, b, 0], held[1, b, 1]))
        return carry

    lax.fori_loop(0, half // step, chunk, 0)


def back_pair(table, values):
    data = jnp.concatenate(values, axis=1)
    high = data.astype(BF16)
    low = (data - high.astype(F32)).astype(BF16)
    out = (
        jnp.dot(table[0], high, preferred_element_type=F32)
        + jnp.dot(table[0], low, preferred_element_type=F32)
        + jnp.dot(table[1], high, preferred_element_type=F32)
    )
    cw = data.shape[1] // len(values)
    return [out[:, p * cw : (p + 1) * cw].astype(BF16) for p in range(len(values))]


def greet(sizes):
    barrier = pltpu.get_barrier_semaphore()
    for axis, size in sizes:
        me = lax.axis_index(axis)
        for o in range(1, size):
            peer = lax.rem(me + o, size)
            pl.semaphore_signal(barrier, inc=1, device_id={axis: peer}, device_id_type=MESH)
    pl.semaphore_wait(barrier, sum(size - 1 for _, size in sizes))


def send(source, target, send_sem, recv_sem, peer, axis="ctx"):
    return pltpu.make_async_remote_copy(
        src_ref=source,
        dst_ref=target,
        send_sem=send_sem,
        recv_sem=recv_sem,
        device_id={axis: peer},
        device_id_type=MESH,
    )


def far_first(size):
    return sorted(range(1, size), key=lambda o: abs(o - size // 2))


def gather_kernel(q_ref, k_ref, v_ref, long_ref, taps, d_ref, w_hbm,
                  mh_ref, go_ref, before, after, ext, mh_tx, held, weights, total,
                  edge_sent, edge_came, sent, came, own_sent, pass_sent, d_came, w_sem):
    count, _, rows, cw = mh_ref.shape
    parts, halves = held.shape[:2]
    cols = d_ref.shape[1]
    piece = cols // halves
    rim = taps.shape[1] - 1
    me = lax.axis_index("ctx")
    mine = lax.axis_index("ch")
    partner = mine + 1 - 2 * lax.rem(mine, 2)
    greet([("ctx", count), ("ch", parts)])

    rest = [lax.rem(mine + 2 * o, parts) for o in range(1, parts // 2)]
    other = [lax.rem(partner + 2 * o, parts) for o in range(1, parts // 2)]
    after_me = lax.rem(me + 1, count)
    before_me = lax.rem(me + count - 1, count)

    edges = []
    for s, ref in ((1, k_ref), (2, v_ref), (0, q_ref)):
        edges.append(send(ref.at[rows - TAIL : rows], before.at[s], edge_sent.at[s],
                          edge_came.at[s], after_me))
    for s, ref in ((0, q_ref), (1, k_ref), (2, v_ref)):
        edges.append(send(ref.at[0:TAIL], after.at[s], edge_sent.at[3 + s],
                          edge_came.at[3 + s], before_me))
    for edge in edges:
        edge.start()

    def own(slot, half, peer):
        lanes = slice(half * piece, (half + 1) * piece)
        return send(d_ref.at[:, lanes], held.at[mine, half], own_sent.at[slot, half],
                    d_came.at[mine, half], peer, "ch")

    def passed(slot, half, part):
        return send(held.at[part, half], held.at[part, half], pass_sent.at[slot, half],
                    d_came.at[part, half], partner, "ch")

    for half in range(halves):
        for slot, peer in enumerate(rest + [partner]):
            own(slot, half, peer).start()

    def weight(part):
        lanes = pl.ds(pl.multiple_of(part * cols, cols), cols)
        return pltpu.make_async_copy(w_hbm.at[:, lanes], weights.at[part], w_sem.at[part])

    order = [mine, partner] + [p for pair in zip(rest, other) for p in pair]
    for part in order:
        weight(part).start()
    for edge in edges:
        edge.wait()

    @pl.when(me == 0)
    def _():
        before[...] = jnp.zeros_like(before)

    @pl.when(me == count - 1)
    def _():
        after[...] = jnp.zeros_like(after)

    for c in range(count):
        lanes = slice(c * cw, (c + 1) * cw)
        fill(ext, before[1, TAIL - rim :, lanes], k_ref[:, lanes], None, rim)
        keyed = short(ext, taps, rows, lanes, 1)
        fill(ext, before[2, TAIL - rim :, lanes], v_ref[:, lanes], None, rim)
        mh_tx[c, 0] = (keyed * short(ext, taps, rows, lanes, 2)).astype(BF16)
        mh_tx[c, 1] = long_ref[:, lanes].astype(BF16)

    def exchange(peer):
        return send(mh_tx.at[peer], mh_ref.at[me], sent.at[peer], came.at[me], peer)

    def arrival(peer):
        return send(mh_tx.at[peer], mh_ref.at[peer], sent.at[peer], came.at[peer], peer)

    peers = [lax.rem(me + o, count) for o in far_first(count)]
    for peer in peers:
        exchange(peer).start()
    mh_ref[me] = mh_tx[me]

    def product(data, part, half=None):
        lanes = slice(None) if half is None else slice(half * piece, (half + 1) * piece)
        return lax.dot_general(data, weights[part, :, lanes], (((1,), (1,)), ((), ())),
                               preferred_element_type=F32)

    def take(part, half):
        total[...] += product(held[part, half], part, half)

    weight(mine).wait()
    total[...] = product(d_ref[...], mine)
    weight(partner).wait()
    for half in range(halves):
        passed(0, half, partner).wait_recv()
        take(partner, half)
    for slot, (direct, relayed) in enumerate(zip(rest, other)):
        weight(direct).wait()
        weight(relayed).wait()
        for half in range(halves):
            passed(slot, half, direct).wait_recv()
            passed(slot, half, direct).start()
            take(direct, half)
            passed(slot, half, relayed).wait_recv()
            take(relayed, half)
    go_ref[...] = total[...].astype(BF16)

    for peer in peers:
        arrival(peer).wait_recv()
    for peer in peers:
        exchange(peer).wait_send()
    for half in range(halves):
        for slot, peer in enumerate(rest + [partner]):
            own(slot, half, peer).wait_send()
        for slot, direct in enumerate(rest):
            passed(slot, half, direct).wait_send()


def conv_kernel(q_ref, before, go_ref, taps, mh_ref, forward, inverse, y_ref, b_ref, edge_ref,
                ext, g_tx, g_rx, y_tx, b_tx, spec, held, sent, came, edge_sem):
    count, _, rows, cw = mh_ref.shape
    rim = taps.shape[1] - 1
    me = lax.axis_index("ctx")
    greet([("ctx", count)])
    edge_rows = edge_ref.shape[0]
    previous = lax.rem(me + count - 1, count)
    edge = send(go_ref.at[0:edge_rows], edge_ref, edge_sem.at[0], edge_sem.at[1], previous)
    edge.start()
    for c in range(count):
        lanes = slice(c * cw, (c + 1) * cw)
        fill(ext, before[0, TAIL - rim :, lanes], q_ref[:, lanes], None, rim)
        g_tx[c] = (go_ref[:, lanes].astype(F32) * short(ext, taps, rows, lanes, 0)).astype(BF16)

    def exchange(kind, source, target, peer):
        return send(
            source.at[peer], target.at[me], sent.at[kind, peer], came.at[kind, me], peer
        )

    def arrival(kind, source, target, peer):
        return send(
            source.at[peer], target.at[peer], sent.at[kind, peer], came.at[kind, peer], peer
        )

    peers = [lax.rem(me + o, count) for o in far_first(count)]
    for peer in peers:
        exchange(0, g_tx, g_rx, peer).start()
    g_rx[me] = g_tx[me]

    blocks = []
    for i in range(count):
        blocks += [(mh_ref.at[i, 0], 0, i), (mh_ref.at[i, 1], 1, i)]
    spectra(forward, blocks, spec)
    mix_spectra(True, spec, held)
    for i in range(0, count, 2):
        for p, value in enumerate(back_pair(inverse, [spec[2, i], spec[2, i + 1]])):
            y_tx[i + p, 0:rows, :] = value
            if i + p > 0:
                y_tx[i + p - 1, rows : rows + TAIL, :] = value[:TAIL]
    y_tx[count - 1, rows : rows + TAIL, :] = jnp.zeros((TAIL, cw), BF16)
    for peer in peers:
        exchange(1, y_tx, y_ref, peer).start()
    y_ref[me] = y_tx[me]

    for peer in peers:
        arrival(0, g_tx, g_rx, peer).wait_recv()
    spectra(forward, [(g_rx.at[i], 2, i) for i in range(count)], spec)
    mix_spectra(False, spec, held)

    def give(piece):
        @pl.when(piece != me)
        def _():
            exchange(2, b_tx, b_ref, piece).start()

        @pl.when(piece == me)
        def _():
            b_ref[me] = b_tx[me]

    half = count // 2
    start = lax.rem(me // 2 + half // 2, half)
    for k in range(half):
        at = 2 * lax.rem(start + k, half)
        last = lax.rem(at + count - 1, count)
        backs = back_pair(inverse, [spec[1, at], spec[1, at + 1]])
        longs = back_pair(inverse, [spec[0, at], spec[0, at + 1]])
        for p in range(2):
            b_tx[at + p, 0:rows, :] = backs[p]
            b_tx[at + p, rows + TAIL : 2 * rows + TAIL, :] = longs[p]
        b_tx[at, rows : rows + TAIL, :] = backs[1][:TAIL]
        head = backs[0][:TAIL]
        b_tx[last, rows : rows + TAIL, :] = jnp.where(at == 0, jnp.zeros_like(head), head)
        if k > 0:
            give(last)
        give(at)
    give(lax.rem(2 * start + count - 1, count))

    for kind, source, target in ((1, y_tx, y_ref), (2, b_tx, b_ref)):
        for peer in peers:
            arrival(kind, source, target, peer).wait_recv()
    for kind, source, target in ((0, g_tx, g_rx), (1, y_tx, y_ref), (2, b_tx, b_ref)):
        for peer in peers:
            exchange(kind, source, target, peer).wait_send()
    edge.wait()

    @pl.when(me == count - 1)
    def _():
        edge_ref[...] = jnp.zeros_like(edge_ref)


def sum_kernel(part_ref, short_ref, skip_ref, one_rx, total, two_rx, sent, came):
    count = part_ref.shape[0]
    cw = part_ref.shape[2]
    tap_count = short_ref.shape[1]
    me = lax.axis_index("ctx")
    greet([("ctx", count)])
    peers = [lax.rem(me + o, count) for o in far_first(count)]

    def exchange(kind, source, target, peer):
        return send(source, target.at[me], sent.at[kind, peer], came.at[kind, me], peer)

    def arrival(kind, source, target, peer):
        return send(source, target.at[peer], sent.at[kind, peer], came.at[kind, peer], peer)

    for peer in peers:
        exchange(0, part_ref.at[peer], one_rx, peer).start()
    one_rx[me] = part_ref[me]
    for peer in peers:
        arrival(0, part_ref.at[peer], one_rx, peer).wait_recv()
    value = one_rx[0]
    for c in range(1, count):
        value = value + one_rx[c]
    total[...] = value
    for peer in peers:
        exchange(1, total, two_rx, peer).start()
    two_rx[me] = value
    for peer in peers:
        arrival(1, total, two_rx, peer).wait_recv()
    for c in range(count):
        lanes = slice(c * cw, (c + 1) * cw)
        for s in range(3):
            short_ref[s, :, lanes] = two_rx[c, s * tap_count : (s + 1) * tap_count, :]
        skip_ref[:, lanes] = two_rx[c, 3 * tap_count : 3 * tap_count + 1, :]
    for peer in peers:
        exchange(0, part_ref.at[peer], one_rx, peer).wait_send()
        exchange(1, total, two_rx, peer).wait_send()


def leave_kernel(pieces, q_ref, k_ref, v_ref, before, after, go_ref, go_after, taps, skip_ref,
                 y_ref, b_ref, dq_ref, dk_ref, dv_ref, long_ref, sums_ref, ext, go_ext, grad_ext):
    rows, width = q_ref.shape
    cw = width // pieces
    rim = taps.shape[1] - 1
    tap_count = taps.shape[1]
    more = rows + PAD
    sums_ref[...] = jnp.zeros_like(sums_ref)
    for c in range(pieces):
        lanes = slice(c * cw, (c + 1) * cw)
        filtered = []
        for s, ref in enumerate((q_ref, k_ref, v_ref)):
            fill(ext.at[s], before[s, TAIL - rim :, lanes], ref[:, lanes], after[s, 0:rim, lanes], rim)
            filtered.append(short(ext.at[s], taps, more, lanes, s))
        fill(go_ext, jnp.zeros((rim, cw), F32), go_ref[:, lanes], go_after[0:rim, lanes], rim)
        grad_o = go_ext[PAD : PAD + more, :]
        mixed = filtered[1] * filtered[2]
        grad_y = grad_o * filtered[0]
        gain = skip_ref[:, lanes]
        y_full = y_ref[c, 0:more, :].astype(F32) + gain * mixed
        at = rows + TAIL
        grad_mixed = b_ref[c, 0:more, :].astype(F32) + gain * grad_y
        grad_ext[0, 0:more, :] = grad_o * y_full
        grad_ext[1, 0:more, :] = grad_mixed * filtered[2]
        grad_ext[2, 0:more, :] = grad_mixed * filtered[1]
        long_ref[:, lanes] = b_ref[c, at : at + rows, :].astype(F32)
        for s, ref in enumerate((dq_ref, dk_ref, dv_ref)):
            total = None
            own = grad_ext[s, 0:rows, :]
            for j in range(tap_count):
                term = taps[s, j : j + 1, lanes] * grad_ext[s, j : j + rows, :]
                total = term if total is None else total + term
                stream = ext[s, PAD - j : PAD - j + rows, :]
                row = s * tap_count + j
                sums_ref[c, row : row + 1, :] = jnp.sum(own * stream, axis=0, keepdims=True)
            ref[:, lanes] = total.astype(BF16)
        row = 3 * tap_count
        sums_ref[c, row : row + 1, :] = jnp.sum(
            grad_y[0:rows] * mixed[0:rows], axis=0, keepdims=True
        )


def call(kernel, out_shape, scratch, *args, hbm=(), **params):
    vmem = pl.BlockSpec(memory_space=pltpu.VMEM)
    return pl.pallas_call(
        kernel,
        out_shape=out_shape,
        in_specs=[pl.BlockSpec(memory_space=pl.ANY) if i in hbm else vmem
                  for i in range(len(args))],
        out_specs=jax.tree.map(lambda _: vmem, out_shape),
        scratch_shapes=scratch,
        compiler_params=pltpu.CompilerParams(**PARAMS, **params),
    )(*args)


def whole_kernel(names, *refs):
    s = types.SimpleNamespace(**dict(zip(names, refs)))
    count, rows, cw = s.h_rx.shape
    parts, _, pieces, tall, _ = s.held.shape
    cols = s.d_own.shape[1]
    piece = cols // pieces
    tap_count = s.taps.shape[1]
    rim = tap_count - 1
    me = lax.axis_index("ctx")
    mine = lax.axis_index("ch")
    partner = mine + 1 - 2 * lax.rem(mine, 2)
    rest = [lax.rem(mine + 2 * o, parts) for o in range(1, parts // 2)]
    other = [lax.rem(partner + 2 * o, parts) for o in range(1, parts // 2)]
    after_me = lax.rem(me + 1, count)
    before_me = lax.rem(me + count - 1, count)
    peers = [lax.rem(me + o, count) for o in far_first(count)]
    sources = [lax.rem(me + count - o, count) for o in far_first(count)]
    streams = (s.q_hbm, s.k_hbm, s.v_hbm)

    def load(source, target, i):
        return pltpu.make_async_copy(source, target, s.load_sem.at[i])

    long_load = load(s.long_hbm, s.long_own, 0)
    stream_loads = [load(streams[i], s.own.at[i], 1 + i) for i in range(3)]
    d_load = load(s.d_hbm, s.d_own, 4)
    table_loads = [load(s.fwd_hbm, s.fwd, 5), load(s.inv_hbm, s.inv, 6)]

    def weight(part):
        lanes = pl.ds(pl.multiple_of(part * cols, cols), cols)
        return pltpu.make_async_copy(s.w_hbm.at[:, lanes], s.weights.at[part], s.w_sem.at[part])

    small_loads = [load(s.taps_hbm, s.taps, 7), load(s.skip_hbm, s.skip, 8)]
    long_load.start()
    for i in (1, 2, 0):
        stream_loads[i].start()
    for small in small_loads:
        small.start()
    d_load.start()
    weight(mine).start()
    weight(partner).start()
    for table in table_loads:
        table.start()
    for part in [p for pair in zip(rest, other) for p in pair]:
        weight(part).start()

    greet([("ctx", count), ("ch", parts)])

    edges = []
    for i in (1, 2, 0):
        edges.append(send(streams[i].at[rows - TAIL : rows], s.before.at[i], s.edge_sent.at[i],
                          s.edge_came.at[i], after_me))
    for edge in edges:
        edge.start()

    batches = [(h, p) for h in range(rows // tall) for p in range(pieces)]

    def own(slot, h, p, peer):
        part = s.d_hbm.at[h * tall : (h + 1) * tall, p * piece : (p + 1) * piece]
        return send(part, s.held.at[mine, h, p], s.own_sent.at[slot, h, p],
                    s.d_came.at[mine, h, p], peer, "ch")

    def passed(slot, h, p, part):
        return send(s.held.at[part, h, p], s.held.at[part, h, p], s.pass_sent.at[slot, h, p],
                    s.d_came.at[part, h, p], partner, "ch")

    for h, p in batches:
        for slot, peer in enumerate(rest + [partner]):
            own(slot, h, p, peer).start()

    def exchange(kind, source, target, peer):
        return send(source.at[peer], target.at[me], s.sent.at[kind, peer], s.came.at[kind, me],
                    peer)

    def arrival(kind, source, target, peer):
        return send(source.at[peer], target.at[peer], s.sent.at[kind, peer],
                    s.came.at[kind, peer], peer)

    def arrive(kind, source, target):
        for peer in peers:
            arrival(kind, source, target, peer).wait_recv()

    def chunk(c):
        return pl.ds(pl.multiple_of(c * cw, cw), cw)

    def filtered(i, lanes):
        total = None
        for j in range(tap_count):
            term = s.taps[i, j : j + 1, lanes] * s.ext[i, PAD - j : PAD - j + rows, lanes]
            total = term if total is None else total + term
        return total

    def fill_own(i):
        def body(c, carry):
            lanes = chunk(c)
            s.ext[i, 0:PAD, lanes] = jnp.zeros((PAD, cw), F32)
            s.ext[i, PAD : PAD + rows, lanes] = s.own[i, :, lanes].astype(F32)
            return carry

        lax.fori_loop(0, count, body, 0)

    def fill_rim(i):
        s.ext[i, PAD - rim : PAD, :] = s.before[i, TAIL - rim :, :].astype(F32)

    long_load.wait()
    for peer in peers + [me]:
        s.h_tx[peer] = s.long_own[:, chunk(peer)].astype(BF16)
        if peer is not me:
            exchange(0, s.h_tx, s.h_rx, peer).start()
    s.h_rx[me] = s.h_tx[me]

    for i in (1, 2, 0):
        stream_loads[i].wait()
        fill_own(i)
    for edge in edges:
        edge.wait()

    @pl.when(me == 0)
    def _():
        s.before[...] = jnp.zeros_like(s.before)

    for small in small_loads:
        small.wait()
    for i in (1, 2, 0):
        fill_rim(i)
    for peer in peers + [me]:
        lanes = chunk(peer)
        keyed = filtered(1, lanes)
        valued = filtered(2, lanes)
        s.filt[1, :, lanes] = keyed
        s.filt[2, :, lanes] = valued
        s.m_tx[peer] = (keyed * valued).astype(BF16)
        if peer is not me:
            exchange(1, s.m_tx, s.m_rx, peer).start()
    s.m_rx[me] = s.m_tx[me]

    def query(c, carry):
        s.filt[0, :, chunk(c)] = filtered(0, chunk(c))
        return carry

    lax.fori_loop(0, count, query, 0)

    def product(data, part, p=None):
        lanes = slice(None) if p is None else slice(p * piece, (p + 1) * piece)
        return lax.dot_general(data, s.weights[part, :, lanes], (((1,), (1,)), ((), ())),
                               preferred_element_type=F32)

    def take(part, h, p):
        s.total[h * tall : (h + 1) * tall, :] += product(s.held[part, h, p], part, p)

    def g_send(h, source, target, peer, slot):
        at = slice(h * tall, (h + 1) * tall)
        return send(source.at[peer, at], target.at[slot, at], s.g_sent.at[h, peer],
                    s.g_came.at[h, slot], peer)

    def gradient(h):
        at = slice(h * tall, (h + 1) * tall)
        for peer in peers + [me]:
            lanes = chunk(peer)
            value = s.total[at, lanes].astype(BF16).astype(F32)
            s.go[at, lanes] = value
            s.g_tx[peer, at, :] = (value * s.filt[0, at, lanes]).astype(BF16)
            if peer is not me:
                g_send(h, s.g_tx, s.g_rx, peer, me).start()
        s.g_rx[me, at, :] = s.g_tx[me, at, :]

    def long_spectra():
        arrive(0, s.h_tx, s.h_rx)
        spectra(s.fwd, [(s.h_rx.at[i], 1, i) for i in range(count)], s.spec)

    d_load.wait()
    weight(mine).wait()
    s.total[...] = product(s.d_own[...], mine)
    weight(partner).wait()
    for h, p in batches:
        passed(0, h, p, partner).wait_recv()
        take(partner, h, p)
    for direct, relayed in zip(rest, other):
        weight(direct).wait()
        weight(relayed).wait()
    for table in table_loads:
        table.wait()
    for h in range(rows // tall):
        for p in range(pieces):
            for slot, (direct, relayed) in enumerate(zip(rest, other)):
                passed(slot, h, p, direct).wait_recv()
                passed(slot, h, p, direct).start()
                take(direct, h, p)
                passed(slot, h, p, relayed).wait_recv()
                take(relayed, h, p)
        gradient(h)
        if h == 0:
            long_spectra()

    half = count // 2
    start = lax.rem(me // 2 + half // 2, half)

    def give_b(to):
        @pl.when(to != me)
        def _():
            exchange(4, s.b_tx, s.b_rx, to).start()

    def keep(to):
        pass

    def deliver(give, source, at_spec):
        for k in range(half):
            at = 2 * lax.rem(start + k, half)
            out = back_pair(s.inv, [s.spec[at_spec, at], s.spec[at_spec, at + 1]])
            for p in range(2):
                source[at + p] = out[p]
                give(at + p)

    arrive(1, s.m_tx, s.m_rx)
    spectra(s.fwd, [(s.m_rx.at[i], 0, i) for i in range(count)], s.spec)
    mix(s.spec, "y")
    deliver(keep, s.y_tx, 2)
    s.y_rx[me] = s.y_tx[me]

    for peer in sources:
        for h in range(rows // tall):
            g_send(h, s.g_tx, s.g_rx, peer, peer).wait_recv()
        exchange(3, s.y_tx, s.y_rx, peer).start()
    spectra(s.fwd, [(s.g_rx.at[i], 2, i) for i in range(count)], s.spec)
    mix(s.spec, "b")
    deliver(give_b, s.b_tx, 1)
    s.b_rx[me] = s.b_tx[me]
    mix(s.spec, "l")
    deliver(keep, s.l_tx, 0)
    l_own = pltpu.make_async_copy(s.l_tx.at[me], s.l_hbm.at[me], s.out_sem.at[3])
    l_own.start()

    def finish(i, c, lanes, grad):
        s.grad[i, 0:rows, :] = grad
        s.grad[i, rows:, :] = jnp.zeros((PAD, cw), F32)
        s.head_tx[i, :, lanes] = grad[0:PAD]
        s.tail[i, 0:TAIL, lanes] = grad[rows - TAIL :]
        total = None
        for j in range(tap_count):
            term = s.taps[i, j : j + 1, lanes] * s.grad[i, j : j + rows, :]
            total = term if total is None else total + term
            stream = s.ext[i, PAD - j : PAD - j + rows, lanes]
            row = i * tap_count + j
            s.part[c, row : row + 1, :] = jnp.sum(grad * stream, axis=0, keepdims=True)
        s.done[i, :, lanes] = total.astype(BF16)

    def first_half(c, carry):
        lanes = chunk(c)
        mixed = s.filt[1, :, lanes] * s.filt[2, :, lanes]
        grad_o = s.go[:, lanes]
        row = 3 * tap_count
        s.part[c, row:, :] = jnp.zeros((16 - row, cw), F32)
        s.part[c, row : row + 1, :] = jnp.sum(
            grad_o * s.filt[0, :, lanes] * mixed, axis=0, keepdims=True
        )
        y_full = s.y_rx[c].astype(F32) + s.skip[:, lanes] * mixed
        finish(0, c, lanes, grad_o * y_full)
        return carry

    def second_half(k, carry):
        middle = count // 2
        c = lax.rem(me + count - middle + (2 * lax.rem(k, 2) - 1) * ((k + 1) // 2), count)

        @pl.when(c != me)
        def _():
            arrival(4, s.b_tx, s.b_rx, c).wait_recv()

        @pl.when((c != me) & (k < split))
        def _():
            exchange(5, s.l_tx, s.l_hbm, c).start()

        lanes = chunk(c)
        grad_y = s.go[:, lanes] * s.filt[0, :, lanes]
        grad_mixed = s.b_rx[c].astype(F32) + s.skip[:, lanes] * grad_y
        finish(1, c, lanes, grad_mixed * s.filt[2, :, lanes])
        finish(2, c, lanes, grad_mixed * s.filt[1, :, lanes])
        return carry

    heads = [send(s.head_tx.at[i], s.tail.at[i, TAIL : TAIL + PAD], s.edge_sent.at[3 + i],
                  s.edge_came.at[3 + i], before_me) for i in range(3)]
    outs = [pltpu.make_async_copy(s.done.at[i], ref, s.out_sem.at[i])
            for i, ref in enumerate((s.dq_hbm, s.dk_hbm, s.dv_hbm))]

    def mend(i):
        heads[i].wait_recv()

        @pl.when(me == count - 1)
        def _():
            s.tail[i, TAIL:, :] = jnp.zeros_like(s.tail[i, TAIL:, :])

        total = None
        for j in range(tap_count):
            term = s.taps[i, j : j + 1, :] * s.tail[i, j : j + TAIL, :]
            total = term if total is None else total + term
        s.done[i, rows - TAIL :, :] = total.astype(BF16)
        outs[i].start()

    split, later = 0, 3 * count // 8

    def long_send(some):
        for peer in some:
            exchange(5, s.l_tx, s.l_hbm, peer).start()

    arrive(3, s.y_tx, s.y_rx)
    lax.fori_loop(0, count, first_half, 0)
    heads[0].start()
    lax.fori_loop(0, count, second_half, 0)
    s.part_tx[...] = s.part[...].astype(BF16)
    for peer in peers:
        exchange(6, s.part_tx, s.one_rx, peer).start()
    heads[1].start()
    heads[2].start()
    long_send(sources[split:later])
    s.one_rx[me] = s.part_tx[me]
    arrive(6, s.part_tx, s.one_rx)
    value = s.one_rx[0].astype(F32)
    for c in range(1, count):
        value = value + s.one_rx[c].astype(F32)
    s.sum[...] = value.astype(BF16)

    def spread(peer):
        return send(s.sum, s.sums_hbm.at[me], s.sent.at[7, peer], s.came.at[7, me], peer)

    for peer in peers:
        spread(peer).start()
    long_send(sources[later:])
    for i in range(3):
        mend(i)
    sums_own = pltpu.make_async_copy(s.sum, s.sums_hbm.at[me], s.out_sem.at[4])
    sums_own.start()

    for peer in peers:
        send(s.sum, s.sums_hbm.at[peer], s.sent.at[7, peer], s.came.at[7, peer], peer).wait_recv()
    arrive(5, s.l_tx, s.l_hbm)
    for copy in outs + [l_own, sums_own]:
        copy.wait()
    sends = ((0, s.h_tx, s.h_rx), (1, s.m_tx, s.m_rx), (3, s.y_tx, s.y_rx),
             (4, s.b_tx, s.b_rx), (5, s.l_tx, s.l_hbm), (6, s.part_tx, s.one_rx))
    for kind, source, target in sends:
        for peer in peers:
            exchange(kind, source, target, peer).wait_send()
    for h in range(rows // tall):
        for peer in peers:
            g_send(h, s.g_tx, s.g_rx, peer, me).wait_send()
    for peer in peers:
        spread(peer).wait_send()
    for head in heads:
        head.wait_send()
    for h, p in batches:
        for slot, peer in enumerate(rest + [partner]):
            own(slot, h, p, peer).wait_send()
        for slot, direct in enumerate(rest):
            passed(slot, h, p, direct).wait_send()


def mix(spec, what):
    count, rows2, cw = spec.shape[1:]
    half = rows2 // 2
    step = 8
    sign = 1.0 - 2.0 * (lax.broadcasted_iota(jnp.int32, (step, cw), 0) % 2).astype(F32)

    def primes(blocks):
        out = [blocks[0]]
        for d in range(1, count):
            re, im = blocks[d]
            old_re, old_im = blocks[d - 1]
            out.append((re - sign * old_im, im + sign * old_re))
        return out

    def chunk(r, carry):
        low = pl.ds(pl.multiple_of(r * step, step), step)
        high = pl.ds(pl.multiple_of(half + r * step, step), step)

        def load(s, i):
            return spec[s, i, low, :], spec[s, i, high, :]

        def save(s, i, value):
            spec[s, i, low, :] = value[0]
            spec[s, i, high, :] = value[1]

        if what == "y":
            taps = primes([load(1, i) for i in range(count)])
            for i in range(count):
                save(1, i, taps[i])
            mixed = [load(0, i) for i in range(count)]
            for i in range(count):
                total = None
                for d in range(i + 1):
                    total = add(total, times(taps[d], mixed[i - d]))
                save(2, i, total)
            return carry
        s = 1 if what == "b" else 0
        taps = [load(s, i) for i in range(count)]
        if what == "l":
            taps = primes(taps)
        grads = [load(2, i) for i in range(count)]
        for b in range(count):
            total = None
            for e in range(count - b):
                total = add(total, conj_times(taps[e], grads[b + e]))
            save(s, b, total)
        return carry

    lax.fori_loop(0, half // step, chunk, 0)


def result_kernel(dq_in, dk_in, dv_in, l_in, sums_in,
                  dq_out, dk_out, dv_out, long_out, short_out, skip_out,
                  streams, l_ref, long_ref, sums_ref, short_ref, skip_ref,
                  in_sem, out_sem, l_sem, long_sem):
    count, rows, cw = l_ref.shape
    tap_count = short_ref.shape[1]
    steps = l_sem.shape[0]
    tall = rows // steps
    copy = pltpu.make_async_copy
    l_loads, l_stores = [], []
    for n in range(steps):
        at = slice(n * tall, (n + 1) * tall)
        l_loads.append(copy(l_in.at[:, at], l_ref.at[:, at], l_sem.at[n]))
        l_stores.append(copy(long_ref.at[at], long_out.at[at], long_sem.at[n]))
    sums_load = copy(sums_in, sums_ref, in_sem.at[3])
    loads = [copy(ref, streams.at[i], in_sem.at[i])
             for i, ref in enumerate((dq_in, dk_in, dv_in))]
    stores = [copy(streams.at[i], ref, out_sem.at[i])
              for i, ref in enumerate((dq_out, dk_out, dv_out))]
    stores += [copy(short_ref, short_out, out_sem.at[3]), copy(skip_ref, skip_out, out_sem.at[4])]
    for load in [sums_load] + l_loads + loads:
        load.start()
    sums_load.wait()
    for c in range(count):
        lanes = slice(c * cw, (c + 1) * cw)
        sums = sums_ref[c].astype(F32)
        for i in range(3):
            short_ref[i, :, lanes] = sums[i * tap_count : (i + 1) * tap_count, :]
        skip_ref[:, lanes] = sums[3 * tap_count : 3 * tap_count + 1, :]
    stores[3].start()
    stores[4].start()
    for n in range(steps):
        l_loads[n].wait()
        at = slice(n * tall, (n + 1) * tall)
        for c in range(count):
            long_ref[at, c * cw : (c + 1) * cw] = l_ref[c, at, :].astype(F32)
        l_stores[n].start()
    for load, store in zip(loads, stores):
        load.wait()
        store.start()
    for store in stores + l_stores:
        store.wait()


def joined(queries, keys, values, long_filter, short_filters, skip, w_out, d_out):
    ctx = lax.axis_size("ctx")
    parts = lax.axis_size("ch")
    rows, width = queries.shape
    cw = width // ctx
    tap_count = short_filters.shape[1]
    cols = d_out.shape[1]
    halves, pieces = 2, 4
    shape = jax.ShapeDtypeStruct
    dma = pltpu.SemaphoreType.DMA
    forward, inverse = (jnp.asarray(t) for t in tables(rows))
    anyw = pl.BlockSpec(memory_space=pl.ANY)
    inputs = [
        ("q_hbm", queries, anyw), ("k_hbm", keys, anyw), ("v_hbm", values, anyw),
        ("long_hbm", long_filter, anyw), ("taps_hbm", short_filters, anyw),
        ("skip_hbm", skip[None], anyw), ("d_hbm", d_out, anyw), ("w_hbm", w_out, anyw),
        ("fwd_hbm", forward, anyw), ("inv_hbm", inverse, anyw),
    ]
    stream = shape((rows, width), BF16)
    outputs = [
        ("dq_hbm", stream), ("dk_hbm", stream), ("dv_hbm", stream),
        ("l_hbm", shape((ctx, rows, cw), BF16)), ("sums_hbm", shape((ctx, 16, cw), BF16)),
    ]
    bulk = pltpu.VMEM((ctx, rows, cw), BF16)
    small = pltpu.VMEM((ctx, 16, cw), BF16)
    rim = pltpu.VMEM((3, TAIL, width), BF16)
    scratch = [
        ("taps", pltpu.VMEM(short_filters.shape, F32)), ("skip", pltpu.VMEM((1, width), F32)),
        ("long_own", pltpu.VMEM((rows, width), F32)), ("own", pltpu.VMEM((3, rows, width), BF16)),
        ("d_own", pltpu.VMEM((rows, cols), BF16)), ("fwd", pltpu.VMEM(forward.shape, BF16)),
        ("inv", pltpu.VMEM(inverse.shape, BF16)), ("before", rim), ("tail", pltpu.VMEM((3, TAIL + PAD, width), F32)),
        ("head_tx", pltpu.VMEM((3, PAD, width), F32)),
        ("ext", pltpu.VMEM((3, rows + PAD, width), F32)),
        ("filt", pltpu.VMEM((3, rows, width), F32)),
        ("held", pltpu.VMEM((parts, halves, pieces, rows // halves, cols // pieces), BF16)),
        ("weights", pltpu.VMEM((parts, width, cols), BF16)),
        ("total", pltpu.VMEM((rows, width), F32)),
        ("go", pltpu.VMEM((rows, width), F32)),
        ("h_tx", bulk), ("h_rx", bulk), ("m_tx", bulk), ("m_rx", bulk), ("g_tx", bulk),
        ("g_rx", bulk), ("y_tx", bulk), ("y_rx", bulk), ("b_tx", bulk), ("b_rx", bulk),
        ("l_tx", bulk), ("spec", pltpu.VMEM((3, ctx, 2 * rows, cw), F32)),
        ("grad", pltpu.VMEM((3, rows + PAD, cw), F32)),
        ("done", pltpu.VMEM((3, rows, width), BF16)),
        ("part", pltpu.VMEM((ctx, 16, cw), F32)), ("part_tx", small), ("one_rx", small),
        ("sum", pltpu.VMEM((16, cw), BF16)),
        ("load_sem", dma((9,))), ("w_sem", dma((parts,))), ("edge_sent", dma((6,))),
        ("edge_came", dma((6,))), ("own_sent", dma((parts // 2, halves, pieces))),
        ("pass_sent", dma((parts // 2, halves, pieces))), ("d_came", dma((parts, halves, pieces))),
        ("sent", dma((8, ctx))), ("came", dma((8, ctx))), ("out_sem", dma((5,))),
        ("g_sent", dma((halves, ctx))), ("g_came", dma((halves, ctx))),
    ]
    names = tuple(name for name, *_ in inputs + outputs + scratch)
    dq, dk, dv, back, sums = pl.pallas_call(
        functools.partial(whole_kernel, names),
        out_shape=[out for _, out in outputs],
        in_specs=[spec for _, _, spec in inputs],
        out_specs=[anyw] * len(outputs),
        scratch_shapes=[kind for _, kind in scratch],
        compiler_params=pltpu.CompilerParams(**PARAMS, collective_id=0, has_side_effects=True),
    )(*[value for _, value, _ in inputs])
    dq, dk, dv, d_long, d_short, d_skip = pl.pallas_call(
        result_kernel,
        out_shape=[stream, stream, stream, shape((rows, width), F32),
                   shape((3, tap_count, width), F32), shape((1, width), F32)],
        in_specs=[anyw] * 5,
        out_specs=[anyw] * 6,
        scratch_shapes=[pltpu.VMEM((3, rows, width), BF16), pltpu.VMEM((ctx, rows, cw), BF16),
                        pltpu.VMEM((rows, width), F32), small,
                        pltpu.VMEM((3, tap_count, width), F32), pltpu.VMEM((1, width), F32),
                        dma((4,)), dma((5,)), dma((4,)), dma((4,))],
        compiler_params=pltpu.CompilerParams(**PARAMS),
    )(dq, dk, dv, back, sums)
    return dq, dk, dv, d_long, d_short, d_skip[0]


def per_device(queries, keys, values, long_filter, short_filters, skip, w_out, d_out):
    ctx = lax.axis_size("ctx")
    rows, width = queries.shape
    cw = width // ctx
    if cw % 128 == 0 and ctx <= 8:
        return joined(queries, keys, values, long_filter, short_filters, skip, w_out, d_out)
    tap_count = short_filters.shape[1]
    parts = lax.axis_size("ch")
    cols = d_out.shape[1]
    halves = 2
    ext = pltpu.VMEM((rows + 4 * PAD, cw), F32)
    shape = jax.ShapeDtypeStruct
    dma = pltpu.SemaphoreType.DMA
    edge = shape((3, TAIL, width), BF16)
    pair = (ctx, 2, rows, cw)
    mh, grad_o, before, after = call(
        gather_kernel,
        (shape(pair, BF16), shape((rows, width), BF16), edge, edge),
        [ext, pltpu.VMEM(pair, BF16), pltpu.VMEM((parts, halves, rows, cols // halves), BF16),
         pltpu.VMEM((parts, width, cols), BF16), pltpu.VMEM((rows, width), F32),
         dma((6,)), dma((6,)), dma((ctx,)), dma((ctx,)), dma((parts // 2, halves)),
         dma((parts // 2, halves)), dma((parts, halves)), dma((parts,))],
        queries, keys, values, long_filter, short_filters, d_out, w_out,
        hbm=(6,), collective_id=3, has_side_effects=True,
    )
    forward, inverse = tables(rows)
    spare = ctx if ctx > 8 else 1
    one = shape((ctx, rows + TAIL, cw), BF16)
    two = shape((ctx, 2 * rows + TAIL, cw), BF16)
    piece = pltpu.VMEM((ctx, rows, cw), BF16)
    y, back, go_after = call(
        conv_kernel,
        (one, two, shape((TAIL, width), BF16)),
        [ext, piece, piece, pltpu.VMEM(one.shape, BF16), pltpu.VMEM(two.shape, BF16),
         pltpu.VMEM((3, ctx, 2 * rows, cw), F32), pltpu.VMEM((2, spare, 2, 8, cw), F32),
         pltpu.SemaphoreType.DMA((3, ctx)), pltpu.SemaphoreType.DMA((3, ctx)),
         pltpu.SemaphoreType.DMA((2,))],
        queries, before, grad_o, short_filters, mh, jnp.asarray(forward), jnp.asarray(inverse),
        collective_id=1, has_side_effects=True,
    )
    stream = shape((rows, width), BF16)
    dq, dk, dv, d_long, sums = call(
        functools.partial(leave_kernel, ctx),
        (stream, stream, stream, shape((rows, width), F32), shape((ctx, 16, cw), F32)),
        [pltpu.VMEM((3, rows + 4 * PAD, cw), F32), ext, pltpu.VMEM((3, rows + 4 * PAD, cw), F32)],
        queries, keys, values, before, after, grad_o, go_after, short_filters, skip[None], y, back,
    )
    small = pltpu.VMEM((ctx, 16, cw), F32)
    d_short, d_skip = call(
        sum_kernel,
        (shape((3, tap_count, width), F32), shape((1, width), F32)),
        [small, pltpu.VMEM((16, cw), F32), small,
         pltpu.SemaphoreType.DMA((2, ctx)), pltpu.SemaphoreType.DMA((2, ctx))],
        sums,
        collective_id=2, has_side_effects=True,
    )
    return dq, dk, dv, d_long, d_short, d_skip[0]


def solution(mesh):
    in_specs = (
        P("ctx", "ch"),
        P("ctx", "ch"),
        P("ctx", "ch"),
        P("ctx", "ch"),
        P(None, None, "ch"),
        P("ch"),
        P("ch", None),
        P("ctx", "ch"),
    )
    out_specs = (
        P("ctx", "ch"),
        P("ctx", "ch"),
        P("ctx", "ch"),
        P("ctx", "ch"),
        P(None, None, "ch"),
        P("ch"),
    )
    return jax.shard_map(
        per_device, mesh=mesh, in_specs=in_specs, out_specs=out_specs, check_vma=False
    )
```

```python
import functools
import math
import types

import jax
import jax.numpy as jnp
import numpy as np
from jax import lax
from jax.experimental import pallas as pl
from jax.experimental.pallas import tpu as pltpu
from jax.sharding import PartitionSpec as P

PAD = 8
TAIL = 16
PARAMS = dict(vmem_limit_bytes=60 * 1024 * 1024)
F32 = jnp.float32
BF16 = jnp.bfloat16
MESH = pl.DeviceIdType.MESH


def split_table(table):
    table = table.astype(np.float32)
    high = table.astype(BF16)
    low = (table - high.astype(np.float32)).astype(BF16)
    return np.concatenate([high[None], low[None]], axis=0)


def tables(block):
    freq = np.arange(block)[:, None]
    place = np.arange(block)[None, :]
    angle = (2 * freq + 1) * place % (4 * block) * (math.pi / (2 * block))
    forward = np.concatenate([np.cos(angle), -np.sin(angle)], axis=0)
    return split_table(forward), split_table(forward.T / block)


def fill(scratch, before, own, after, rim):
    rows = own.shape[0]
    scratch[0:PAD, :] = jnp.zeros_like(scratch[0:PAD, :])
    scratch[PAD + rows :, :] = jnp.zeros_like(scratch[PAD + rows :, :])
    scratch[PAD - rim : PAD, :] = before.astype(F32)
    scratch[PAD : PAD + rows, :] = own.astype(F32)
    if after is not None:
        scratch[PAD + rows : PAD + rows + rim, :] = after.astype(F32)


def short(scratch, taps, rows, lanes, s):
    total = None
    for j in range(taps.shape[1]):
        term = taps[s, j : j + 1, lanes] * scratch[PAD - j : PAD - j + rows, :]
        total = term if total is None else total + term
    return total


def times(a, b):
    return a[0] * b[0] - a[1] * b[1], a[0] * b[1] + a[1] * b[0]


def conj_times(a, b):
    return a[0] * b[0] + a[1] * b[1], a[0] * b[1] - a[1] * b[0]


def add(a, b):
    return b if a is None else (a[0] + b[0], a[1] + b[1])


def spectra(table, blocks, spec):
    for at in range(0, len(blocks), 2):
        pair = blocks[at : at + 2]
        data = jnp.concatenate([ref[...] for ref, _, _ in pair], axis=1)
        out = jnp.dot(table[0], data, preferred_element_type=F32) + jnp.dot(
            table[1], data, preferred_element_type=F32
        )
        cw = data.shape[1] // len(pair)
        for p, (_, s, i) in enumerate(pair):
            spec[s, i] = out[:, p * cw : (p + 1) * cw]


def mix_spectra(first, spec, held):
    count, rows2, cw = spec.shape[1:]
    half = rows2 // 2
    step = 8
    sign = 1.0 - 2.0 * (lax.broadcasted_iota(jnp.int32, (step, cw), 0) % 2).astype(F32)
    zero = jnp.zeros((step, cw), F32)

    def primes(blocks):
        out = [blocks[0]]
        for d in range(1, count):
            re, im = blocks[d]
            old_re, old_im = blocks[d - 1]
            out.append((re - sign * old_im, im + sign * old_re))
        return out

    def chunk(r, carry):
        low = pl.ds(pl.multiple_of(r * step, step), step)
        high = pl.ds(pl.multiple_of(half + r * step, step), step)

        def load(s, i):
            return spec[s, i, low, :], spec[s, i, high, :]

        def save(s, i, value):
            spec[s, i, low, :] = value[0]
            spec[s, i, high, :] = value[1]

        def primed(s):
            values = primes([load(s, i) for i in range(count)])
            for i in range(count):
                save(s, i, values[i])
            return values

        if count <= 8 and first:
            taps = primed(1)
            mixed = [load(0, i) for i in range(count)]
            for i in range(count):
                total = None
                for d in range(i + 1):
                    total = add(total, times(taps[d], mixed[i - d]))
                save(2, i, total)
            return carry
        if count <= 8:
            grads = [load(2, i) for i in range(count)]
            for s in (1, 0):
                taps = [load(s, i) for i in range(count)]
                if s == 0:
                    taps = primes(taps)
                for b in range(count):
                    total = None
                    for e in range(count - b):
                        total = add(total, conj_times(taps[e], grads[b + e]))
                    save(s, b, total)
            return carry
        if first:
            primed(1)

            def one(b, inner):
                def of_y(d, total):
                    return add(total, times(load(1, d), load(0, b - d)))

                save(2, b, lax.fori_loop(0, b + 1, of_y, (zero, zero)))
                return inner

            lax.fori_loop(0, count, one, 0)
            return carry
        primed(0)

        def both(b, inner):
            def of_g(e, totals):
                grad = load(2, b + e)
                return (
                    add(totals[0], conj_times(load(1, e), grad)),
                    add(totals[1], conj_times(load(0, e), grad)),
                )

            pair = lax.fori_loop(0, count - b, of_g, ((zero, zero), (zero, zero)))
            for s in range(2):
                held[s, b, 0], held[s, b, 1] = pair[s]
            return inner

        lax.fori_loop(0, count, both, 0)
        for b in range(count):
            save(1, b, (held[0, b, 0], held[0, b, 1]))
            save(0, b, (held[1, b, 0], held[1, b, 1]))
        return carry

    lax.fori_loop(0, half // step, chunk, 0)


def back_pair(table, values):
    data = jnp.concatenate(values, axis=1)
    high = data.astype(BF16)
    low = (data - high.astype(F32)).astype(BF16)
    out = (
        jnp.dot(table[0], high, preferred_element_type=F32)
        + jnp.dot(table[0], low, preferred_element_type=F32)
        + jnp.dot(table[1], high, preferred_element_type=F32)
    )
    cw = data.shape[1] // len(values)
    return [out[:, p * cw : (p + 1) * cw].astype(BF16) for p in range(len(values))]


def greet(sizes):
    barrier = pltpu.get_barrier_semaphore()
    for axis, size in sizes:
        me = lax.axis_index(axis)
        for o in range(1, size):
            peer = lax.rem(me + o, size)
            pl.semaphore_signal(barrier, inc=1, device_id={axis: peer}, device_id_type=MESH)
    pl.semaphore_wait(barrier, sum(size - 1 for _, size in sizes))


def send(source, target, send_sem, recv_sem, peer, axis="ctx"):
    return pltpu.make_async_remote_copy(
        src_ref=source,
        dst_ref=target,
        send_sem=send_sem,
        recv_sem=recv_sem,
        device_id={axis: peer},
        device_id_type=MESH,
    )


def far_first(size):
    return sorted(range(1, size), key=lambda o: abs(o - size // 2))


def gather_kernel(q_ref, k_ref, v_ref, long_ref, taps, d_ref, w_hbm,
                  mh_ref, go_ref, before, after, ext, mh_tx, held, weights, total,
                  edge_sent, edge_came, sent, came, own_sent, pass_sent, d_came, w_sem):
    count, _, rows, cw = mh_ref.shape
    parts, halves = held.shape[:2]
    cols = d_ref.shape[1]
    piece = cols // halves
    rim = taps.shape[1] - 1
    me = lax.axis_index("ctx")
    mine = lax.axis_index("ch")
    partner = mine + 1 - 2 * lax.rem(mine, 2)
    greet([("ctx", count), ("ch", parts)])

    rest = [lax.rem(mine + 2 * o, parts) for o in range(1, parts // 2)]
    other = [lax.rem(partner + 2 * o, parts) for o in range(1, parts // 2)]
    after_me = lax.rem(me + 1, count)
    before_me = lax.rem(me + count - 1, count)

    edges = []
    for s, ref in ((1, k_ref), (2, v_ref), (0, q_ref)):
        edges.append(send(ref.at[rows - TAIL : rows], before.at[s], edge_sent.at[s],
                          edge_came.at[s], after_me))
    for s, ref in ((0, q_ref), (1, k_ref), (2, v_ref)):
        edges.append(send(ref.at[0:TAIL], after.at[s], edge_sent.at[3 + s],
                          edge_came.at[3 + s], before_me))
    for edge in edges:
        edge.start()

    def own(slot, half, peer):
        lanes = slice(half * piece, (half + 1) * piece)
        return send(d_ref.at[:, lanes], held.at[mine, half], own_sent.at[slot, half],
                    d_came.at[mine, half], peer, "ch")

    def passed(slot, half, part):
        return send(held.at[part, half], held.at[part, half], pass_sent.at[slot, half],
                    d_came.at[part, half], partner, "ch")

    for half in range(halves):
        for slot, peer in enumerate(rest + [partner]):
            own(slot, half, peer).start()

    def weight(part):
        lanes = pl.ds(pl.multiple_of(part * cols, cols), cols)
        return pltpu.make_async_copy(w_hbm.at[:, lanes], weights.at[part], w_sem.at[part])

    order = [mine, partner] + [p for pair in zip(rest, other) for p in pair]
    for part in order:
        weight(part).start()
    for edge in edges:
        edge.wait()

    @pl.when(me == 0)
    def _():
        before[...] = jnp.zeros_like(before)

    @pl.when(me == count - 1)
    def _():
        after[...] = jnp.zeros_like(after)

    for c in range(count):
        lanes = slice(c * cw, (c + 1) * cw)
        fill(ext, before[1, TAIL - rim :, lanes], k_ref[:, lanes], None, rim)
        keyed = short(ext, taps, rows, lanes, 1)
        fill(ext, before[2, TAIL - rim :, lanes], v_ref[:, lanes], None, rim)
        mh_tx[c, 0] = (keyed * short(ext, taps, rows, lanes, 2)).astype(BF16)
        mh_tx[c, 1] = long_ref[:, lanes].astype(BF16)

    def exchange(peer):
        return send(mh_tx.at[peer], mh_ref.at[me], sent.at[peer], came.at[me], peer)

    def arrival(peer):
        return send(mh_tx.at[peer], mh_ref.at[peer], sent.at[peer], came.at[peer], peer)

    peers = [lax.rem(me + o, count) for o in far_first(count)]
    for peer in peers:
        exchange(peer).start()
    mh_ref[me] = mh_tx[me]

    def product(data, part, half=None):
        lanes = slice(None) if half is None else slice(half * piece, (half + 1) * piece)
        return lax.dot_general(data, weights[part, :, lanes], (((1,), (1,)), ((), ())),
                               preferred_element_type=F32)

    def take(part, half):
        total[...] += product(held[part, half], part, half)

    weight(mine).wait()
    total[...] = product(d_ref[...], mine)
    weight(partner).wait()
    for half in range(halves):
        passed(0, half, partner).wait_recv()
        take(partner, half)
    for slot, (direct, relayed) in enumerate(zip(rest, other)):
        weight(direct).wait()
        weight(relayed).wait()
        for half in range(halves):
            passed(slot, half, direct).wait_recv()
            passed(slot, half, direct).start()
            take(direct, half)
            passed(slot, half, relayed).wait_recv()
            take(relayed, half)
    go_ref[...] = total[...].astype(BF16)

    for peer in peers:
        arrival(peer).wait_recv()
    for peer in peers:
        exchange(peer).wait_send()
    for half in range(halves):
        for slot, peer in enumerate(rest + [partner]):
            own(slot, half, peer).wait_send()
        for slot, direct in enumerate(rest):
            passed(slot, half, direct).wait_send()


def conv_kernel(q_ref, before, go_ref, taps, mh_ref, forward, inverse, y_ref, b_ref, edge_ref,
                ext, g_tx, g_rx, y_tx, b_tx, spec, held, sent, came, edge_sem):
    count, _, rows, cw = mh_ref.shape
    rim = taps.shape[1] - 1
    me = lax.axis_index("ctx")
    greet([("ctx", count)])
    edge_rows = edge_ref.shape[0]
    previous = lax.rem(me + count - 1, count)
    edge = send(go_ref.at[0:edge_rows], edge_ref, edge_sem.at[0], edge_sem.at[1], previous)
    edge.start()
    for c in range(count):
        lanes = slice(c * cw, (c + 1) * cw)
        fill(ext, before[0, TAIL - rim :, lanes], q_ref[:, lanes], None, rim)
        g_tx[c] = (go_ref[:, lanes].astype(F32) * short(ext, taps, rows, lanes, 0)).astype(BF16)

    def exchange(kind, source, target, peer):
        return send(
            source.at[peer], target.at[me], sent.at[kind, peer], came.at[kind, me], peer
        )

    def arrival(kind, source, target, peer):
        return send(
            source.at[peer], target.at[peer], sent.at[kind, peer], came.at[kind, peer], peer
        )

    peers = [lax.rem(me + o, count) for o in far_first(count)]
    for peer in peers:
        exchange(0, g_tx, g_rx, peer).start()
    g_rx[me] = g_tx[me]

    blocks = []
    for i in range(count):
        blocks += [(mh_ref.at[i, 0], 0, i), (mh_ref.at[i, 1], 1, i)]
    spectra(forward, blocks, spec)
    mix_spectra(True, spec, held)
    for i in range(0, count, 2):
        for p, value in enumerate(back_pair(inverse, [spec[2, i], spec[2, i + 1]])):
            y_tx[i + p, 0:rows, :] = value
            if i + p > 0:
                y_tx[i + p - 1, rows : rows + TAIL, :] = value[:TAIL]
    y_tx[count - 1, rows : rows + TAIL, :] = jnp.zeros((TAIL, cw), BF16)
    for peer in peers:
        exchange(1, y_tx, y_ref, peer).start()
    y_ref[me] = y_tx[me]

    for peer in peers:
        arrival(0, g_tx, g_rx, peer).wait_recv()
    spectra(forward, [(g_rx.at[i], 2, i) for i in range(count)], spec)
    mix_spectra(False, spec, held)

    def give(piece):
        @pl.when(piece != me)
        def _():
            exchange(2, b_tx, b_ref, piece).start()

        @pl.when(piece == me)
        def _():
            b_ref[me] = b_tx[me]

    half = count // 2
    start = lax.rem(me // 2 + half // 2, half)
    for k in range(half):
        at = 2 * lax.rem(start + k, half)
        last = lax.rem(at + count - 1, count)
        backs = back_pair(inverse, [spec[1, at], spec[1, at + 1]])
        longs = back_pair(inverse, [spec[0, at], spec[0, at + 1]])
        for p in range(2):
            b_tx[at + p, 0:rows, :] = backs[p]
            b_tx[at + p, rows + TAIL : 2 * rows + TAIL, :] = longs[p]
        b_tx[at, rows : rows + TAIL, :] = backs[1][:TAIL]
        head = backs[0][:TAIL]
        b_tx[last, rows : rows + TAIL, :] = jnp.where(at == 0, jnp.zeros_like(head), head)
        if k > 0:
            give(last)
        give(at)
    give(lax.rem(2 * start + count - 1, count))

    for kind, source, target in ((1, y_tx, y_ref), (2, b_tx, b_ref)):
        for peer in peers:
            arrival(kind, source, target, peer).wait_recv()
    for kind, source, target in ((0, g_tx, g_rx), (1, y_tx, y_ref), (2, b_tx, b_ref)):
        for peer in peers:
            exchange(kind, source, target, peer).wait_send()
    edge.wait()

    @pl.when(me == count - 1)
    def _():
        edge_ref[...] = jnp.zeros_like(edge_ref)


def sum_kernel(part_ref, short_ref, skip_ref, one_rx, total, two_rx, sent, came):
    count = part_ref.shape[0]
    cw = part_ref.shape[2]
    tap_count = short_ref.shape[1]
    me = lax.axis_index("ctx")
    greet([("ctx", count)])
    peers = [lax.rem(me + o, count) for o in far_first(count)]

    def exchange(kind, source, target, peer):
        return send(source, target.at[me], sent.at[kind, peer], came.at[kind, me], peer)

    def arrival(kind, source, target, peer):
        return send(source, target.at[peer], sent.at[kind, peer], came.at[kind, peer], peer)

    for peer in peers:
        exchange(0, part_ref.at[peer], one_rx, peer).start()
    one_rx[me] = part_ref[me]
    for peer in peers:
        arrival(0, part_ref.at[peer], one_rx, peer).wait_recv()
    value = one_rx[0]
    for c in range(1, count):
        value = value + one_rx[c]
    total[...] = value
    for peer in peers:
        exchange(1, total, two_rx, peer).start()
    two_rx[me] = value
    for peer in peers:
        arrival(1, total, two_rx, peer).wait_recv()
    for c in range(count):
        lanes = slice(c * cw, (c + 1) * cw)
        for s in range(3):
            short_ref[s, :, lanes] = two_rx[c, s * tap_count : (s + 1) * tap_count, :]
        skip_ref[:, lanes] = two_rx[c, 3 * tap_count : 3 * tap_count + 1, :]
    for peer in peers:
        exchange(0, part_ref.at[peer], one_rx, peer).wait_send()
        exchange(1, total, two_rx, peer).wait_send()


def leave_kernel(pieces, q_ref, k_ref, v_ref, before, after, go_ref, go_after, taps, skip_ref,
                 y_ref, b_ref, dq_ref, dk_ref, dv_ref, long_ref, sums_ref, ext, go_ext, grad_ext):
    rows, width = q_ref.shape
    cw = width // pieces
    rim = taps.shape[1] - 1
    tap_count = taps.shape[1]
    more = rows + PAD
    sums_ref[...] = jnp.zeros_like(sums_ref)
    for c in range(pieces):
        lanes = slice(c * cw, (c + 1) * cw)
        filtered = []
        for s, ref in enumerate((q_ref, k_ref, v_ref)):
            fill(ext.at[s], before[s, TAIL - rim :, lanes], ref[:, lanes], after[s, 0:rim, lanes], rim)
            filtered.append(short(ext.at[s], taps, more, lanes, s))
        fill(go_ext, jnp.zeros((rim, cw), F32), go_ref[:, lanes], go_after[0:rim, lanes], rim)
        grad_o = go_ext[PAD : PAD + more, :]
        mixed = filtered[1] * filtered[2]
        grad_y = grad_o * filtered[0]
        gain = skip_ref[:, lanes]
        y_full = y_ref[c, 0:more, :].astype(F32) + gain * mixed
        at = rows + TAIL
        grad_mixed = b_ref[c, 0:more, :].astype(F32) + gain * grad_y
        grad_ext[0, 0:more, :] = grad_o * y_full
        grad_ext[1, 0:more, :] = grad_mixed * filtered[2]
        grad_ext[2, 0:more, :] = grad_mixed * filtered[1]
        long_ref[:, lanes] = b_ref[c, at : at + rows, :].astype(F32)
        for s, ref in enumerate((dq_ref, dk_ref, dv_ref)):
            total = None
            own = grad_ext[s, 0:rows, :]
            for j in range(tap_count):
                term = taps[s, j : j + 1, lanes] * grad_ext[s, j : j + rows, :]
                total = term if total is None else total + term
                stream = ext[s, PAD - j : PAD - j + rows, :]
                row = s * tap_count + j
                sums_ref[c, row : row + 1, :] = jnp.sum(own * stream, axis=0, keepdims=True)
            ref[:, lanes] = total.astype(BF16)
        row = 3 * tap_count
        sums_ref[c, row : row + 1, :] = jnp.sum(
            grad_y[0:rows] * mixed[0:rows], axis=0, keepdims=True
        )


def call(kernel, out_shape, scratch, *args, hbm=(), **params):
    vmem = pl.BlockSpec(memory_space=pltpu.VMEM)
    return pl.pallas_call(
        kernel,
        out_shape=out_shape,
        in_specs=[pl.BlockSpec(memory_space=pl.ANY) if i in hbm else vmem
                  for i in range(len(args))],
        out_specs=jax.tree.map(lambda _: vmem, out_shape),
        scratch_shapes=scratch,
        compiler_params=pltpu.CompilerParams(**PARAMS, **params),
    )(*args)


def whole_kernel(names, *refs):
    s = types.SimpleNamespace(**dict(zip(names, refs)))
    count, rows, cw = s.h_rx.shape
    parts, _, pieces, tall, _ = s.held.shape
    cols = s.d_own.shape[1]
    piece = cols // pieces
    tap_count = s.taps.shape[1]
    rim = tap_count - 1
    me = lax.axis_index("ctx")
    mine = lax.axis_index("ch")
    partner = mine + 1 - 2 * lax.rem(mine, 2)
    rest = [lax.rem(mine + 2 * o, parts) for o in range(1, parts // 2)]
    other = [lax.rem(partner + 2 * o, parts) for o in range(1, parts // 2)]
    after_me = lax.rem(me + 1, count)
    before_me = lax.rem(me + count - 1, count)
    peers = [lax.rem(me + o, count) for o in far_first(count)]
    sources = [lax.rem(me + count - o, count) for o in far_first(count)]
    streams = (s.q_hbm, s.k_hbm, s.v_hbm)

    def load(source, target, i):
        return pltpu.make_async_copy(source, target, s.load_sem.at[i])

    long_load = load(s.long_hbm, s.long_own, 0)
    stream_loads = [load(streams[i], s.own.at[i], 1 + i) for i in range(3)]
    d_load = load(s.d_hbm, s.d_own, 4)
    table_loads = [load(s.fwd_hbm, s.fwd, 5), load(s.inv_hbm, s.inv, 6)]

    def weight(part):
        lanes = pl.ds(pl.multiple_of(part * cols, cols), cols)
        return pltpu.make_async_copy(s.w_hbm.at[:, lanes], s.weights.at[part], s.w_sem.at[part])

    small_loads = [load(s.taps_hbm, s.taps, 7), load(s.skip_hbm, s.skip, 8)]
    long_load.start()
    for i in (1, 2, 0):
        stream_loads[i].start()
    for small in small_loads:
        small.start()
    d_load.start()
    weight(mine).start()
    weight(partner).start()
    for table in table_loads:
        table.start()
    for part in [p for pair in zip(rest, other) for p in pair]:
        weight(part).start()

    greet([("ctx", count), ("ch", parts)])

    edges = []
    for i in (1, 2, 0):
        edges.append(send(streams[i].at[rows - TAIL : rows], s.before.at[i], s.edge_sent.at[i],
                          s.edge_came.at[i], after_me))
    for edge in edges:
        edge.start()

    batches = [(h, p) for h in range(rows // tall) for p in range(pieces)]

    def own(slot, h, p, peer):
        part = s.d_hbm.at[h * tall : (h + 1) * tall, p * piece : (p + 1) * piece]
        return send(part, s.held.at[mine, h, p], s.own_sent.at[slot, h, p],
                    s.d_came.at[mine, h, p], peer, "ch")

    def passed(slot, h, p, part):
        return send(s.held.at[part, h, p], s.held.at[part, h, p], s.pass_sent.at[slot, h, p],
                    s.d_came.at[part, h, p], partner, "ch")

    for h, p in batches:
        for slot, peer in enumerate(rest + [partner]):
            own(slot, h, p, peer).start()

    def exchange(kind, source, target, peer):
        return send(source.at[peer], target.at[me], s.sent.at[kind, peer], s.came.at[kind, me],
                    peer)

    def arrival(kind, source, target, peer):
        return send(source.at[peer], target.at[peer], s.sent.at[kind, peer],
                    s.came.at[kind, peer], peer)

    def arrive(kind, source, target):
        for peer in peers:
            arrival(kind, source, target, peer).wait_recv()

    def chunk(c):
        return pl.ds(pl.multiple_of(c * cw, cw), cw)

    def filtered(i, lanes):
        total = None
        for j in range(tap_count):
            term = s.taps[i, j : j + 1, lanes] * s.ext[i, PAD - j : PAD - j + rows, lanes]
            total = term if total is None else total + term
        return total

    def fill_own(i):
        def body(c, carry):
            lanes = chunk(c)
            s.ext[i, 0:PAD, lanes] = jnp.zeros((PAD, cw), F32)
            s.ext[i, PAD : PAD + rows, lanes] = s.own[i, :, lanes].astype(F32)
            return carry

        lax.fori_loop(0, count, body, 0)

    def fill_rim(i):
        s.ext[i, PAD - rim : PAD, :] = s.before[i, TAIL - rim :, :].astype(F32)

    long_load.wait()
    for peer in peers + [me]:
        s.h_tx[peer] = s.long_own[:, chunk(peer)].astype(BF16)
        if peer is not me:
            exchange(0, s.h_tx, s.h_rx, peer).start()
    s.h_rx[me] = s.h_tx[me]

    for i in (1, 2, 0):
        stream_loads[i].wait()
        fill_own(i)
    for edge in edges:
        edge.wait()

    @pl.when(me == 0)
    def _():
        s.before[...] = jnp.zeros_like(s.before)

    for small in small_loads:
        small.wait()
    for i in (1, 2, 0):
        fill_rim(i)
    for peer in peers + [me]:
        lanes = chunk(peer)
        keyed = filtered(1, lanes)
        valued = filtered(2, lanes)
        s.filt[1, :, lanes] = keyed
        s.filt[2, :, lanes] = valued
        s.m_tx[peer] = (keyed * valued).astype(BF16)
        if peer is not me:
            exchange(1, s.m_tx, s.m_rx, peer).start()
    s.m_rx[me] = s.m_tx[me]

    def query(c, carry):
        s.filt[0, :, chunk(c)] = filtered(0, chunk(c))
        return carry

    lax.fori_loop(0, count, query, 0)

    def product(data, part, p=None):
        lanes = slice(None) if p is None else slice(p * piece, (p + 1) * piece)
        return lax.dot_general(data, s.weights[part, :, lanes], (((1,), (1,)), ((), ())),
                               preferred_element_type=F32)

    def take(part, h, p):
        s.total[h * tall : (h + 1) * tall, :] += product(s.held[part, h, p], part, p)

    def g_send(h, source, target, peer, slot):
        at = slice(h * tall, (h + 1) * tall)
        return send(source.at[peer, at], target.at[slot, at], s.g_sent.at[h, peer],
                    s.g_came.at[h, slot], peer)

    def gradient(h):
        at = slice(h * tall, (h + 1) * tall)
        for peer in peers + [me]:
            lanes = chunk(peer)
            value = s.total[at, lanes].astype(BF16).astype(F32)
            s.go[at, lanes] = value
            s.g_tx[peer, at, :] = (value * s.filt[0, at, lanes]).astype(BF16)
            if peer is not me:
                g_send(h, s.g_tx, s.g_rx, peer, me).start()
        s.g_rx[me, at, :] = s.g_tx[me, at, :]

    def long_spectra():
        arrive(0, s.h_tx, s.h_rx)
        spectra(s.fwd, [(s.h_rx.at[i], 1, i) for i in range(count)], s.spec)

    d_load.wait()
    weight(mine).wait()
    s.total[...] = product(s.d_own[...], mine)
    weight(partner).wait()
    for h, p in batches:
        passed(0, h, p, partner).wait_recv()
        take(partner, h, p)
    for direct, relayed in zip(rest, other):
        weight(direct).wait()
        weight(relayed).wait()
    for table in table_loads:
        table.wait()
    for h in range(rows // tall):
        for p in range(pieces):
            for slot, (direct, relayed) in enumerate(zip(rest, other)):
                passed(slot, h, p, direct).wait_recv()
                passed(slot, h, p, direct).start()
                take(direct, h, p)
                passed(slot, h, p, relayed).wait_recv()
                take(relayed, h, p)
        gradient(h)
        if h == 0:
            long_spectra()

    half = count // 2
    start = lax.rem(me // 2 + half // 2, half)

    def give_b(to):
        @pl.when(to != me)
        def _():
            exchange(4, s.b_tx, s.b_rx, to).start()

    def keep(to):
        pass

    def deliver(give, source, at_spec):
        for k in range(half):
            at = 2 * lax.rem(start + k, half)
            out = back_pair(s.inv, [s.spec[at_spec, at], s.spec[at_spec, at + 1]])
            for p in range(2):
                source[at + p] = out[p]
                give(at + p)

    arrive(1, s.m_tx, s.m_rx)
    spectra(s.fwd, [(s.m_rx.at[i], 0, i) for i in range(count)], s.spec)
    mix(s.spec, "y")
    deliver(keep, s.y_tx, 2)
    s.y_rx[me] = s.y_tx[me]

    for peer in sources:
        for h in range(rows // tall):
            g_send(h, s.g_tx, s.g_rx, peer, peer).wait_recv()
        exchange(3, s.y_tx, s.y_rx, peer).start()
    spectra(s.fwd, [(s.g_rx.at[i], 2, i) for i in range(count)], s.spec)
    mix(s.spec, "b")
    deliver(give_b, s.b_tx, 1)
    s.b_rx[me] = s.b_tx[me]
    mix(s.spec, "l")
    deliver(keep, s.l_tx, 0)
    l_own = pltpu.make_async_copy(s.l_tx.at[me], s.l_hbm.at[me], s.out_sem.at[3])
    l_own.start()

    def gather_sums(i, c, lanes, grad):
        s.grads[i, 0:rows, lanes] = grad
        s.head_tx[i * rim : (i + 1) * rim, lanes] = grad[0:rim]
        for j in range(tap_count):
            stream = s.ext[i, PAD - j : PAD - j + rows, lanes]
            row = i * tap_count + j
            s.part[c, row : row + 1, :] = jnp.sum(grad * stream, axis=0, keepdims=True)

    def write_out(c, carry):
        lanes = chunk(c)
        for i in range(3):
            total = None
            for j in range(tap_count):
                term = s.taps[i, j : j + 1, lanes] * s.grads[i, j : j + rows, lanes]
                total = term if total is None else total + term
            s.done[i, :, lanes] = total.astype(BF16)
        return carry

    def first_half(c, carry):
        lanes = chunk(c)
        mixed = s.filt[1, :, lanes] * s.filt[2, :, lanes]
        grad_o = s.go[:, lanes]
        row = 3 * tap_count
        s.part[c, row:, :] = jnp.zeros((16 - row, cw), F32)
        s.part[c, row : row + 1, :] = jnp.sum(
            grad_o * s.filt[0, :, lanes] * mixed, axis=0, keepdims=True
        )
        y_full = s.y_rx[c].astype(F32) + s.skip[:, lanes] * mixed
        gather_sums(0, c, lanes, grad_o * y_full)
        return carry

    def second_half(k, carry):
        middle = count // 2
        c = lax.rem(me + count - middle + (2 * lax.rem(k, 2) - 1) * ((k + 1) // 2), count)

        @pl.when(c != me)
        def _():
            arrival(4, s.b_tx, s.b_rx, c).wait_recv()

        lanes = chunk(c)
        grad_y = s.go[:, lanes] * s.filt[0, :, lanes]
        grad_mixed = s.b_rx[c].astype(F32) + s.skip[:, lanes] * grad_y
        gather_sums(1, c, lanes, grad_mixed * s.filt[2, :, lanes])
        gather_sums(2, c, lanes, grad_mixed * s.filt[1, :, lanes])
        return carry

    heads = send(s.head_tx, s.head_rx, s.edge_sent.at[3], s.edge_came.at[3], before_me)
    outs = [pltpu.make_async_copy(s.done.at[i], ref, s.out_sem.at[i])
            for i, ref in enumerate((s.dq_hbm, s.dk_hbm, s.dv_hbm))]

    even = lax.rem(mine, 2) == 0
    steps_even, steps_odd = (0, 3, 3, 5, count), (0, 0, 0, 1, count)

    def long_send(stage):
        for n, peer in enumerate(sources):
            due_even = steps_even[stage] <= n < steps_even[stage + 1]
            due_odd = steps_odd[stage] <= n < steps_odd[stage + 1]
            if not due_even and not due_odd:
                continue

            @pl.when((even & due_even) | (jnp.logical_not(even) & due_odd))
            def _():
                exchange(5, s.l_tx, s.l_hbm, peer).start()

    arrive(3, s.y_tx, s.y_rx)
    long_send(0)
    s.head_tx[...] = jnp.zeros_like(s.head_tx)
    lax.fori_loop(0, count, first_half, 0)
    lax.fori_loop(0, count, second_half, 0)
    long_send(1)
    s.part_tx[...] = s.part[...].astype(BF16)
    for peer in peers:
        exchange(6, s.part_tx, s.one_rx, peer).start()
    heads.start()
    long_send(2)
    s.one_rx[me] = s.part_tx[me]
    arrive(6, s.part_tx, s.one_rx)
    value = s.one_rx[0].astype(F32)
    for c in range(1, count):
        value = value + s.one_rx[c].astype(F32)
    s.sum[...] = value.astype(BF16)

    def spread(peer):
        return send(s.sum, s.sums_hbm.at[me], s.sent.at[7, peer], s.came.at[7, me], peer)

    for peer in peers:
        spread(peer).start()
    long_send(3)
    heads.wait_recv()
    s.grads[:, rows:, :] = jnp.zeros_like(s.grads[:, rows:, :])

    @pl.when(me != count - 1)
    def _():
        for i in range(3):
            s.grads[i, rows : rows + rim, :] = s.head_rx[i * rim : (i + 1) * rim, :]

    lax.fori_loop(0, count, write_out, 0)
    for copy in outs:
        copy.start()
    sums_own = pltpu.make_async_copy(s.sum, s.sums_hbm.at[me], s.out_sem.at[4])
    sums_own.start()

    for peer in peers:
        send(s.sum, s.sums_hbm.at[peer], s.sent.at[7, peer], s.came.at[7, peer], peer).wait_recv()
    arrive(5, s.l_tx, s.l_hbm)
    for copy in outs + [l_own, sums_own]:
        copy.wait()
    sends = ((0, s.h_tx, s.h_rx), (1, s.m_tx, s.m_rx), (3, s.y_tx, s.y_rx),
             (4, s.b_tx, s.b_rx), (5, s.l_tx, s.l_hbm), (6, s.part_tx, s.one_rx))
    for kind, source, target in sends:
        for peer in peers:
            exchange(kind, source, target, peer).wait_send()
    for h in range(rows // tall):
        for peer in peers:
            g_send(h, s.g_tx, s.g_rx, peer, me).wait_send()
    for peer in peers:
        spread(peer).wait_send()
    heads.wait_send()
    for h, p in batches:
        for slot, peer in enumerate(rest + [partner]):
            own(slot, h, p, peer).wait_send()
        for slot, direct in enumerate(rest):
            passed(slot, h, p, direct).wait_send()


def mix(spec, what):
    count, rows2, cw = spec.shape[1:]
    half = rows2 // 2
    step = 8
    sign = 1.0 - 2.0 * (lax.broadcasted_iota(jnp.int32, (step, cw), 0) % 2).astype(F32)

    def primes(blocks):
        out = [blocks[0]]
        for d in range(1, count):
            re, im = blocks[d]
            old_re, old_im = blocks[d - 1]
            out.append((re - sign * old_im, im + sign * old_re))
        return out

    def chunk(r, carry):
        low = pl.ds(pl.multiple_of(r * step, step), step)
        high = pl.ds(pl.multiple_of(half + r * step, step), step)

        def load(s, i):
            return spec[s, i, low, :], spec[s, i, high, :]

        def save(s, i, value):
            spec[s, i, low, :] = value[0]
            spec[s, i, high, :] = value[1]

        if what == "y":
            taps = primes([load(1, i) for i in range(count)])
            for i in range(count):
                save(1, i, taps[i])
            mixed = [load(0, i) for i in range(count)]
            for i in range(count):
                total = None
                for d in range(i + 1):
                    total = add(total, times(taps[d], mixed[i - d]))
                save(2, i, total)
            return carry
        s = 1 if what == "b" else 0
        taps = [load(s, i) for i in range(count)]
        if what == "l":
            taps = primes(taps)
        grads = [load(2, i) for i in range(count)]
        for b in range(count):
            total = None
            for e in range(count - b):
                total = add(total, conj_times(taps[e], grads[b + e]))
            save(s, b, total)
        return carry

    lax.fori_loop(0, half // step, chunk, 0)


def result_kernel(dq_in, dk_in, dv_in, l_in, sums_in,
                  dq_out, dk_out, dv_out, long_out, short_out, skip_out,
                  streams, l_ref, long_ref, sums_ref, short_ref, skip_ref,
                  in_sem, out_sem, l_sem, long_sem):
    count, rows, cw = l_ref.shape
    tap_count = short_ref.shape[1]
    steps = l_sem.shape[0]
    tall = rows // steps
    copy = pltpu.make_async_copy
    l_loads, l_stores = [], []
    for n in range(steps):
        at = slice(n * tall, (n + 1) * tall)
        l_loads.append(copy(l_in.at[:, at], l_ref.at[:, at], l_sem.at[n]))
        l_stores.append(copy(long_ref.at[at], long_out.at[at], long_sem.at[n]))
    sums_load = copy(sums_in, sums_ref, in_sem.at[3])
    loads = [copy(ref, streams.at[i], in_sem.at[i])
             for i, ref in enumerate((dq_in, dk_in, dv_in))]
    stores = [copy(streams.at[i], ref, out_sem.at[i])
              for i, ref in enumerate((dq_out, dk_out, dv_out))]
    stores += [copy(short_ref, short_out, out_sem.at[3]), copy(skip_ref, skip_out, out_sem.at[4])]
    for load in [sums_load] + l_loads + loads:
        load.start()
    sums_load.wait()
    for c in range(count):
        lanes = slice(c * cw, (c + 1) * cw)
        sums = sums_ref[c].astype(F32)
        for i in range(3):
            short_ref[i, :, lanes] = sums[i * tap_count : (i + 1) * tap_count, :]
        skip_ref[:, lanes] = sums[3 * tap_count : 3 * tap_count + 1, :]
    stores[3].start()
    stores[4].start()
    for n in range(steps):
        l_loads[n].wait()
        at = slice(n * tall, (n + 1) * tall)
        for c in range(count):
            long_ref[at, c * cw : (c + 1) * cw] = l_ref[c, at, :].astype(F32)
        l_stores[n].start()
    for load, store in zip(loads, stores):
        load.wait()
        store.start()
    for store in stores + l_stores:
        store.wait()


def joined(queries, keys, values, long_filter, short_filters, skip, w_out, d_out):
    ctx = lax.axis_size("ctx")
    parts = lax.axis_size("ch")
    rows, width = queries.shape
    cw = width // ctx
    tap_count = short_filters.shape[1]
    cols = d_out.shape[1]
    halves, pieces = 2, 4
    shape = jax.ShapeDtypeStruct
    dma = pltpu.SemaphoreType.DMA
    forward, inverse = (jnp.asarray(t) for t in tables(rows))
    anyw = pl.BlockSpec(memory_space=pl.ANY)
    inputs = [
        ("q_hbm", queries, anyw), ("k_hbm", keys, anyw), ("v_hbm", values, anyw),
        ("long_hbm", long_filter, anyw), ("taps_hbm", short_filters, anyw),
        ("skip_hbm", skip[None], anyw), ("d_hbm", d_out, anyw), ("w_hbm", w_out, anyw),
        ("fwd_hbm", forward, anyw), ("inv_hbm", inverse, anyw),
    ]
    stream = shape((rows, width), BF16)
    outputs = [
        ("dq_hbm", stream), ("dk_hbm", stream), ("dv_hbm", stream),
        ("l_hbm", shape((ctx, rows, cw), BF16)), ("sums_hbm", shape((ctx, 16, cw), BF16)),
    ]
    bulk = pltpu.VMEM((ctx, rows, cw), BF16)
    small = pltpu.VMEM((ctx, 16, cw), BF16)
    rim = pltpu.VMEM((3, TAIL, width), BF16)
    rim_rows = -(-3 * (tap_count - 1) // PAD) * PAD
    scratch = [
        ("taps", pltpu.VMEM(short_filters.shape, F32)), ("skip", pltpu.VMEM((1, width), F32)),
        ("long_own", pltpu.VMEM((rows, width), F32)), ("own", pltpu.VMEM((3, rows, width), BF16)),
        ("d_own", pltpu.VMEM((rows, cols), BF16)), ("fwd", pltpu.VMEM(forward.shape, BF16)),
        ("inv", pltpu.VMEM(inverse.shape, BF16)), ("before", rim), ("head_tx", pltpu.VMEM((rim_rows, width), F32)),
        ("head_rx", pltpu.VMEM((rim_rows, width), F32)),
        ("ext", pltpu.VMEM((3, rows + PAD, width), F32)),
        ("filt", pltpu.VMEM((3, rows, width), F32)),
        ("held", pltpu.VMEM((parts, halves, pieces, rows // halves, cols // pieces), BF16)),
        ("weights", pltpu.VMEM((parts, width, cols), BF16)),
        ("total", pltpu.VMEM((rows, width), F32)),
        ("go", pltpu.VMEM((rows, width), F32)),
        ("h_tx", bulk), ("h_rx", bulk), ("m_tx", bulk), ("m_rx", bulk), ("g_tx", bulk),
        ("g_rx", bulk), ("y_tx", bulk), ("y_rx", bulk), ("b_tx", bulk), ("b_rx", bulk),
        ("l_tx", bulk), ("spec", pltpu.VMEM((3, ctx, 2 * rows, cw), F32)),
        ("grads", pltpu.VMEM((3, rows + PAD, width), F32)),
        ("done", pltpu.VMEM((3, rows, width), BF16)),
        ("part", pltpu.VMEM((ctx, 16, cw), F32)), ("part_tx", small), ("one_rx", small),
        ("sum", pltpu.VMEM((16, cw), BF16)),
        ("load_sem", dma((9,))), ("w_sem", dma((parts,))), ("edge_sent", dma((6,))),
        ("edge_came", dma((6,))), ("own_sent", dma((parts // 2, halves, pieces))),
        ("pass_sent", dma((parts // 2, halves, pieces))), ("d_came", dma((parts, halves, pieces))),
        ("sent", dma((8, ctx))), ("came", dma((8, ctx))), ("out_sem", dma((5,))),
        ("g_sent", dma((halves, ctx))), ("g_came", dma((halves, ctx))),
    ]
    names = tuple(name for name, *_ in inputs + outputs + scratch)
    dq, dk, dv, back, sums = pl.pallas_call(
        functools.partial(whole_kernel, names),
        out_shape=[out for _, out in outputs],
        in_specs=[spec for _, _, spec in inputs],
        out_specs=[anyw] * len(outputs),
        scratch_shapes=[kind for _, kind in scratch],
        compiler_params=pltpu.CompilerParams(**PARAMS, collective_id=0, has_side_effects=True),
    )(*[value for _, value, _ in inputs])
    dq, dk, dv, d_long, d_short, d_skip = pl.pallas_call(
        result_kernel,
        out_shape=[stream, stream, stream, shape((rows, width), F32),
                   shape((3, tap_count, width), F32), shape((1, width), F32)],
        in_specs=[anyw] * 5,
        out_specs=[anyw] * 6,
        scratch_shapes=[pltpu.VMEM((3, rows, width), BF16), pltpu.VMEM((ctx, rows, cw), BF16),
                        pltpu.VMEM((rows, width), F32), small,
                        pltpu.VMEM((3, tap_count, width), F32), pltpu.VMEM((1, width), F32),
                        dma((4,)), dma((5,)), dma((4,)), dma((4,))],
        compiler_params=pltpu.CompilerParams(**PARAMS),
    )(dq, dk, dv, back, sums)
    return dq, dk, dv, d_long, d_short, d_skip[0]


def per_device(queries, keys, values, long_filter, short_filters, skip, w_out, d_out):
    ctx = lax.axis_size("ctx")
    rows, width = queries.shape
    cw = width // ctx
    if cw % 128 == 0 and ctx <= 8 and ctx % 2 == 0:
        return joined(queries, keys, values, long_filter, short_filters, skip, w_out, d_out)
    tap_count = short_filters.shape[1]
    parts = lax.axis_size("ch")
    cols = d_out.shape[1]
    halves = 2
    ext = pltpu.VMEM((rows + 4 * PAD, cw), F32)
    shape = jax.ShapeDtypeStruct
    dma = pltpu.SemaphoreType.DMA
    edge = shape((3, TAIL, width), BF16)
    pair = (ctx, 2, rows, cw)
    mh, grad_o, before, after = call(
        gather_kernel,
        (shape(pair, BF16), shape((rows, width), BF16), edge, edge),
        [ext, pltpu.VMEM(pair, BF16), pltpu.VMEM((parts, halves, rows, cols // halves), BF16),
         pltpu.VMEM((parts, width, cols), BF16), pltpu.VMEM((rows, width), F32),
         dma((6,)), dma((6,)), dma((ctx,)), dma((ctx,)), dma((parts // 2, halves)),
         dma((parts // 2, halves)), dma((parts, halves)), dma((parts,))],
        queries, keys, values, long_filter, short_filters, d_out, w_out,
        hbm=(6,), collective_id=3, has_side_effects=True,
    )
    forward, inverse = tables(rows)
    spare = ctx if ctx > 8 else 1
    one = shape((ctx, rows + TAIL, cw), BF16)
    two = shape((ctx, 2 * rows + TAIL, cw), BF16)
    piece = pltpu.VMEM((ctx, rows, cw), BF16)
    y, back, go_after = call(
        conv_kernel,
        (one, two, shape((TAIL, width), BF16)),
        [ext, piece, piece, pltpu.VMEM(one.shape, BF16), pltpu.VMEM(two.shape, BF16),
         pltpu.VMEM((3, ctx, 2 * rows, cw), F32), pltpu.VMEM((2, spare, 2, 8, cw), F32),
         pltpu.SemaphoreType.DMA((3, ctx)), pltpu.SemaphoreType.DMA((3, ctx)),
         pltpu.SemaphoreType.DMA((2,))],
        queries, before, grad_o, short_filters, mh, jnp.asarray(forward), jnp.asarray(inverse),
        collective_id=1, has_side_effects=True,
    )
    stream = shape((rows, width), BF16)
    dq, dk, dv, d_long, sums = call(
        functools.partial(leave_kernel, ctx),
        (stream, stream, stream, shape((rows, width), F32), shape((ctx, 16, cw), F32)),
        [pltpu.VMEM((3, rows + 4 * PAD, cw), F32), ext, pltpu.VMEM((3, rows + 4 * PAD, cw), F32)],
        queries, keys, values, before, after, grad_o, go_after, short_filters, skip[None], y, back,
    )
    small = pltpu.VMEM((ctx, 16, cw), F32)
    d_short, d_skip = call(
        sum_kernel,
        (shape((3, tap_count, width), F32), shape((1, width), F32)),
        [small, pltpu.VMEM((16, cw), F32), small,
         pltpu.SemaphoreType.DMA((2, ctx)), pltpu.SemaphoreType.DMA((2, ctx))],
        sums,
        collective_id=2, has_side_effects=True,
    )
    return dq, dk, dv, d_long, d_short, d_skip[0]


def solution(mesh):
    in_specs = (
        P("ctx", "ch"),
        P("ctx", "ch"),
        P("ctx", "ch"),
        P("ctx", "ch"),
        P(None, None, "ch"),
        P("ch"),
        P("ch", None),
        P("ctx", "ch"),
    )
    out_specs = (
        P("ctx", "ch"),
        P("ctx", "ch"),
        P("ctx", "ch"),
        P("ctx", "ch"),
        P(None, None, "ch"),
        P("ch"),
    )
    return jax.shard_map(
        per_device, mesh=mesh, in_specs=in_specs, out_specs=out_specs, check_vma=False
    )
```

```python
import functools
import math
import types

import jax
import jax.numpy as jnp
import numpy as np
from jax import lax
from jax.experimental import pallas as pl
from jax.experimental.pallas import tpu as pltpu
from jax.sharding import PartitionSpec as P

PAD = 8
TAIL = 16
PARAMS = dict(vmem_limit_bytes=60 * 1024 * 1024)
F32 = jnp.float32
BF16 = jnp.bfloat16
MESH = pl.DeviceIdType.MESH


def split_table(table):
    table = table.astype(np.float32)
    high = table.astype(BF16)
    low = (table - high.astype(np.float32)).astype(BF16)
    return np.concatenate([high[None], low[None]], axis=0)


def tables(block):
    freq = np.arange(block)[:, None]
    place = np.arange(block)[None, :]
    angle = (2 * freq + 1) * place % (4 * block) * (math.pi / (2 * block))
    forward = np.concatenate([np.cos(angle), -np.sin(angle)], axis=0)
    return split_table(forward), split_table(forward.T / block)


def fill(scratch, before, own, after, rim):
    rows = own.shape[0]
    scratch[0:PAD, :] = jnp.zeros_like(scratch[0:PAD, :])
    scratch[PAD + rows :, :] = jnp.zeros_like(scratch[PAD + rows :, :])
    scratch[PAD - rim : PAD, :] = before.astype(F32)
    scratch[PAD : PAD + rows, :] = own.astype(F32)
    if after is not None:
        scratch[PAD + rows : PAD + rows + rim, :] = after.astype(F32)


def short(scratch, taps, rows, lanes, s):
    total = None
    for j in range(taps.shape[1]):
        term = taps[s, j : j + 1, lanes] * scratch[PAD - j : PAD - j + rows, :]
        total = term if total is None else total + term
    return total


def times(a, b):
    return a[0] * b[0] - a[1] * b[1], a[0] * b[1] + a[1] * b[0]


def conj_times(a, b):
    return a[0] * b[0] + a[1] * b[1], a[0] * b[1] - a[1] * b[0]


def add(a, b):
    return b if a is None else (a[0] + b[0], a[1] + b[1])


def spectra(table, blocks, spec):
    for at in range(0, len(blocks), 2):
        pair = blocks[at : at + 2]
        data = jnp.concatenate([ref[...] for ref, _, _ in pair], axis=1)
        out = jnp.dot(table[0], data, preferred_element_type=F32) + jnp.dot(
            table[1], data, preferred_element_type=F32
        )
        cw = data.shape[1] // len(pair)
        for p, (_, s, i) in enumerate(pair):
            spec[s, i] = out[:, p * cw : (p + 1) * cw]


def mix_spectra(first, spec, held):
    count, rows2, cw = spec.shape[1:]
    half = rows2 // 2
    step = 8
    sign = 1.0 - 2.0 * (lax.broadcasted_iota(jnp.int32, (step, cw), 0) % 2).astype(F32)
    zero = jnp.zeros((step, cw), F32)

    def primes(blocks):
        out = [blocks[0]]
        for d in range(1, count):
            re, im = blocks[d]
            old_re, old_im = blocks[d - 1]
            out.append((re - sign * old_im, im + sign * old_re))
        return out

    def chunk(r, carry):
        low = pl.ds(pl.multiple_of(r * step, step), step)
        high = pl.ds(pl.multiple_of(half + r * step, step), step)

        def load(s, i):
            return spec[s, i, low, :], spec[s, i, high, :]

        def save(s, i, value):
            spec[s, i, low, :] = value[0]
            spec[s, i, high, :] = value[1]

        def primed(s):
            values = primes([load(s, i) for i in range(count)])
            for i in range(count):
                save(s, i, values[i])
            return values

        if count <= 8 and first:
            taps = primed(1)
            mixed = [load(0, i) for i in range(count)]
            for i in range(count):
                total = None
                for d in range(i + 1):
                    total = add(total, times(taps[d], mixed[i - d]))
                save(2, i, total)
            return carry
        if count <= 8:
            grads = [load(2, i) for i in range(count)]
            for s in (1, 0):
                taps = [load(s, i) for i in range(count)]
                if s == 0:
                    taps = primes(taps)
                for b in range(count):
                    total = None
                    for e in range(count - b):
                        total = add(total, conj_times(taps[e], grads[b + e]))
                    save(s, b, total)
            return carry
        if first:
            primed(1)

            def one(b, inner):
                def of_y(d, total):
                    return add(total, times(load(1, d), load(0, b - d)))

                save(2, b, lax.fori_loop(0, b + 1, of_y, (zero, zero)))
                return inner

            lax.fori_loop(0, count, one, 0)
            return carry
        primed(0)

        def both(b, inner):
            def of_g(e, totals):
                grad = load(2, b + e)
                return (
                    add(totals[0], conj_times(load(1, e), grad)),
                    add(totals[1], conj_times(load(0, e), grad)),
                )

            pair = lax.fori_loop(0, count - b, of_g, ((zero, zero), (zero, zero)))
            for s in range(2):
                held[s, b, 0], held[s, b, 1] = pair[s]
            return inner

        lax.fori_loop(0, count, both, 0)
        for b in range(count):
            save(1, b, (held[0, b, 0], held[0, b, 1]))
            save(0, b, (held[1, b, 0], held[1, b, 1]))
        return carry

    lax.fori_loop(0, half // step, chunk, 0)


def back_pair(table, values):
    data = jnp.concatenate(values, axis=1)
    high = data.astype(BF16)
    low = (data - high.astype(F32)).astype(BF16)
    out = (
        jnp.dot(table[0], high, preferred_element_type=F32)
        + jnp.dot(table[0], low, preferred_element_type=F32)
        + jnp.dot(table[1], high, preferred_element_type=F32)
    )
    cw = data.shape[1] // len(values)
    return [out[:, p * cw : (p + 1) * cw].astype(BF16) for p in range(len(values))]


def greet(sizes):
    barrier = pltpu.get_barrier_semaphore()
    for axis, size in sizes:
        me = lax.axis_index(axis)
        for o in range(1, size):
            peer = lax.rem(me + o, size)
            pl.semaphore_signal(barrier, inc=1, device_id={axis: peer}, device_id_type=MESH)
    pl.semaphore_wait(barrier, sum(size - 1 for _, size in sizes))


def send(source, target, send_sem, recv_sem, peer, axis="ctx"):
    return pltpu.make_async_remote_copy(
        src_ref=source,
        dst_ref=target,
        send_sem=send_sem,
        recv_sem=recv_sem,
        device_id={axis: peer},
        device_id_type=MESH,
    )


def far_first(size):
    return sorted(range(1, size), key=lambda o: abs(o - size // 2))


def gather_kernel(q_ref, k_ref, v_ref, long_ref, taps, d_ref, w_hbm,
                  mh_ref, go_ref, before, after, ext, mh_tx, held, weights, total,
                  edge_sent, edge_came, sent, came, own_sent, pass_sent, d_came, w_sem):
    count, _, rows, cw = mh_ref.shape
    parts, halves = held.shape[:2]
    cols = d_ref.shape[1]
    piece = cols // halves
    rim = taps.shape[1] - 1
    me = lax.axis_index("ctx")
    mine = lax.axis_index("ch")
    partner = mine + 1 - 2 * lax.rem(mine, 2)
    greet([("ctx", count), ("ch", parts)])

    rest = [lax.rem(mine + 2 * o, parts) for o in range(1, parts // 2)]
    other = [lax.rem(partner + 2 * o, parts) for o in range(1, parts // 2)]
    after_me = lax.rem(me + 1, count)
    before_me = lax.rem(me + count - 1, count)

    edges = []
    for s, ref in ((1, k_ref), (2, v_ref), (0, q_ref)):
        edges.append(send(ref.at[rows - TAIL : rows], before.at[s], edge_sent.at[s],
                          edge_came.at[s], after_me))
    for s, ref in ((0, q_ref), (1, k_ref), (2, v_ref)):
        edges.append(send(ref.at[0:TAIL], after.at[s], edge_sent.at[3 + s],
                          edge_came.at[3 + s], before_me))
    for edge in edges:
        edge.start()

    def own(slot, half, peer):
        lanes = slice(half * piece, (half + 1) * piece)
        return send(d_ref.at[:, lanes], held.at[mine, half], own_sent.at[slot, half],
                    d_came.at[mine, half], peer, "ch")

    def passed(slot, half, part):
        return send(held.at[part, half], held.at[part, half], pass_sent.at[slot, half],
                    d_came.at[part, half], partner, "ch")

    for half in range(halves):
        for slot, peer in enumerate(rest + [partner]):
            own(slot, half, peer).start()

    def weight(part):
        lanes = pl.ds(pl.multiple_of(part * cols, cols), cols)
        return pltpu.make_async_copy(w_hbm.at[:, lanes], weights.at[part], w_sem.at[part])

    order = [mine, partner] + [p for pair in zip(rest, other) for p in pair]
    for part in order:
        weight(part).start()
    for edge in edges:
        edge.wait()

    @pl.when(me == 0)
    def _():
        before[...] = jnp.zeros_like(before)

    @pl.when(me == count - 1)
    def _():
        after[...] = jnp.zeros_like(after)

    for c in range(count):
        lanes = slice(c * cw, (c + 1) * cw)
        fill(ext, before[1, TAIL - rim :, lanes], k_ref[:, lanes], None, rim)
        keyed = short(ext, taps, rows, lanes, 1)
        fill(ext, before[2, TAIL - rim :, lanes], v_ref[:, lanes], None, rim)
        mh_tx[c, 0] = (keyed * short(ext, taps, rows, lanes, 2)).astype(BF16)
        mh_tx[c, 1] = long_ref[:, lanes].astype(BF16)

    def exchange(peer):
        return send(mh_tx.at[peer], mh_ref.at[me], sent.at[peer], came.at[me], peer)

    def arrival(peer):
        return send(mh_tx.at[peer], mh_ref.at[peer], sent.at[peer], came.at[peer], peer)

    peers = [lax.rem(me + o, count) for o in far_first(count)]
    for peer in peers:
        exchange(peer).start()
    mh_ref[me] = mh_tx[me]

    def product(data, part, half=None):
        lanes = slice(None) if half is None else slice(half * piece, (half + 1) * piece)
        return lax.dot_general(data, weights[part, :, lanes], (((1,), (1,)), ((), ())),
                               preferred_element_type=F32)

    def take(part, half):
        total[...] += product(held[part, half], part, half)

    weight(mine).wait()
    total[...] = product(d_ref[...], mine)
    weight(partner).wait()
    for half in range(halves):
        passed(0, half, partner).wait_recv()
        take(partner, half)
    for slot, (direct, relayed) in enumerate(zip(rest, other)):
        weight(direct).wait()
        weight(relayed).wait()
        for half in range(halves):
            passed(slot, half, direct).wait_recv()
            passed(slot, half, direct).start()
            take(direct, half)
            passed(slot, half, relayed).wait_recv()
            take(relayed, half)
    go_ref[...] = total[...].astype(BF16)

    for peer in peers:
        arrival(peer).wait_recv()
    for peer in peers:
        exchange(peer).wait_send()
    for half in range(halves):
        for slot, peer in enumerate(rest + [partner]):
            own(slot, half, peer).wait_send()
        for slot, direct in enumerate(rest):
            passed(slot, half, direct).wait_send()


def conv_kernel(q_ref, before, go_ref, taps, mh_ref, forward, inverse, y_ref, b_ref, edge_ref,
                ext, g_tx, g_rx, y_tx, b_tx, spec, held, sent, came, edge_sem):
    count, _, rows, cw = mh_ref.shape
    rim = taps.shape[1] - 1
    me = lax.axis_index("ctx")
    greet([("ctx", count)])
    edge_rows = edge_ref.shape[0]
    previous = lax.rem(me + count - 1, count)
    edge = send(go_ref.at[0:edge_rows], edge_ref, edge_sem.at[0], edge_sem.at[1], previous)
    edge.start()
    for c in range(count):
        lanes = slice(c * cw, (c + 1) * cw)
        fill(ext, before[0, TAIL - rim :, lanes], q_ref[:, lanes], None, rim)
        g_tx[c] = (go_ref[:, lanes].astype(F32) * short(ext, taps, rows, lanes, 0)).astype(BF16)

    def exchange(kind, source, target, peer):
        return send(
            source.at[peer], target.at[me], sent.at[kind, peer], came.at[kind, me], peer
        )

    def arrival(kind, source, target, peer):
        return send(
            source.at[peer], target.at[peer], sent.at[kind, peer], came.at[kind, peer], peer
        )

    peers = [lax.rem(me + o, count) for o in far_first(count)]
    for peer in peers:
        exchange(0, g_tx, g_rx, peer).start()
    g_rx[me] = g_tx[me]

    blocks = []
    for i in range(count):
        blocks += [(mh_ref.at[i, 0], 0, i), (mh_ref.at[i, 1], 1, i)]
    spectra(forward, blocks, spec)
    mix_spectra(True, spec, held)
    for i in range(0, count, 2):
        for p, value in enumerate(back_pair(inverse, [spec[2, i], spec[2, i + 1]])):
            y_tx[i + p, 0:rows, :] = value
            if i + p > 0:
                y_tx[i + p - 1, rows : rows + TAIL, :] = value[:TAIL]
    y_tx[count - 1, rows : rows + TAIL, :] = jnp.zeros((TAIL, cw), BF16)
    for peer in peers:
        exchange(1, y_tx, y_ref, peer).start()
    y_ref[me] = y_tx[me]

    for peer in peers:
        arrival(0, g_tx, g_rx, peer).wait_recv()
    spectra(forward, [(g_rx.at[i], 2, i) for i in range(count)], spec)
    mix_spectra(False, spec, held)

    def give(piece):
        @pl.when(piece != me)
        def _():
            exchange(2, b_tx, b_ref, piece).start()

        @pl.when(piece == me)
        def _():
            b_ref[me] = b_tx[me]

    half = count // 2
    start = lax.rem(me // 2 + half // 2, half)
    for k in range(half):
        at = 2 * lax.rem(start + k, half)
        last = lax.rem(at + count - 1, count)
        backs = back_pair(inverse, [spec[1, at], spec[1, at + 1]])
        longs = back_pair(inverse, [spec[0, at], spec[0, at + 1]])
        for p in range(2):
            b_tx[at + p, 0:rows, :] = backs[p]
            b_tx[at + p, rows + TAIL : 2 * rows + TAIL, :] = longs[p]
        b_tx[at, rows : rows + TAIL, :] = backs[1][:TAIL]
        head = backs[0][:TAIL]
        b_tx[last, rows : rows + TAIL, :] = jnp.where(at == 0, jnp.zeros_like(head), head)
        if k > 0:
            give(last)
        give(at)
    give(lax.rem(2 * start + count - 1, count))

    for kind, source, target in ((1, y_tx, y_ref), (2, b_tx, b_ref)):
        for peer in peers:
            arrival(kind, source, target, peer).wait_recv()
    for kind, source, target in ((0, g_tx, g_rx), (1, y_tx, y_ref), (2, b_tx, b_ref)):
        for peer in peers:
            exchange(kind, source, target, peer).wait_send()
    edge.wait()

    @pl.when(me == count - 1)
    def _():
        edge_ref[...] = jnp.zeros_like(edge_ref)


def sum_kernel(part_ref, short_ref, skip_ref, one_rx, total, two_rx, sent, came):
    count = part_ref.shape[0]
    cw = part_ref.shape[2]
    tap_count = short_ref.shape[1]
    me = lax.axis_index("ctx")
    greet([("ctx", count)])
    peers = [lax.rem(me + o, count) for o in far_first(count)]

    def exchange(kind, source, target, peer):
        return send(source, target.at[me], sent.at[kind, peer], came.at[kind, me], peer)

    def arrival(kind, source, target, peer):
        return send(source, target.at[peer], sent.at[kind, peer], came.at[kind, peer], peer)

    for peer in peers:
        exchange(0, part_ref.at[peer], one_rx, peer).start()
    one_rx[me] = part_ref[me]
    for peer in peers:
        arrival(0, part_ref.at[peer], one_rx, peer).wait_recv()
    value = one_rx[0]
    for c in range(1, count):
        value = value + one_rx[c]
    total[...] = value
    for peer in peers:
        exchange(1, total, two_rx, peer).start()
    two_rx[me] = value
    for peer in peers:
        arrival(1, total, two_rx, peer).wait_recv()
    for c in range(count):
        lanes = slice(c * cw, (c + 1) * cw)
        for s in range(3):
            short_ref[s, :, lanes] = two_rx[c, s * tap_count : (s + 1) * tap_count, :]
        skip_ref[:, lanes] = two_rx[c, 3 * tap_count : 3 * tap_count + 1, :]
    for peer in peers:
        exchange(0, part_ref.at[peer], one_rx, peer).wait_send()
        exchange(1, total, two_rx, peer).wait_send()


def leave_kernel(pieces, q_ref, k_ref, v_ref, before, after, go_ref, go_after, taps, skip_ref,
                 y_ref, b_ref, dq_ref, dk_ref, dv_ref, long_ref, sums_ref, ext, go_ext, grad_ext):
    rows, width = q_ref.shape
    cw = width // pieces
    rim = taps.shape[1] - 1
    tap_count = taps.shape[1]
    more = rows + PAD
    sums_ref[...] = jnp.zeros_like(sums_ref)
    for c in range(pieces):
        lanes = slice(c * cw, (c + 1) * cw)
        filtered = []
        for s, ref in enumerate((q_ref, k_ref, v_ref)):
            fill(ext.at[s], before[s, TAIL - rim :, lanes], ref[:, lanes], after[s, 0:rim, lanes], rim)
            filtered.append(short(ext.at[s], taps, more, lanes, s))
        fill(go_ext, jnp.zeros((rim, cw), F32), go_ref[:, lanes], go_after[0:rim, lanes], rim)
        grad_o = go_ext[PAD : PAD + more, :]
        mixed = filtered[1] * filtered[2]
        grad_y = grad_o * filtered[0]
        gain = skip_ref[:, lanes]
        y_full = y_ref[c, 0:more, :].astype(F32) + gain * mixed
        at = rows + TAIL
        grad_mixed = b_ref[c, 0:more, :].astype(F32) + gain * grad_y
        grad_ext[0, 0:more, :] = grad_o * y_full
        grad_ext[1, 0:more, :] = grad_mixed * filtered[2]
        grad_ext[2, 0:more, :] = grad_mixed * filtered[1]
        long_ref[:, lanes] = b_ref[c, at : at + rows, :].astype(F32)
        for s, ref in enumerate((dq_ref, dk_ref, dv_ref)):
            total = None
            own = grad_ext[s, 0:rows, :]
            for j in range(tap_count):
                term = taps[s, j : j + 1, lanes] * grad_ext[s, j : j + rows, :]
                total = term if total is None else total + term
                stream = ext[s, PAD - j : PAD - j + rows, :]
                row = s * tap_count + j
                sums_ref[c, row : row + 1, :] = jnp.sum(own * stream, axis=0, keepdims=True)
            ref[:, lanes] = total.astype(BF16)
        row = 3 * tap_count
        sums_ref[c, row : row + 1, :] = jnp.sum(
            grad_y[0:rows] * mixed[0:rows], axis=0, keepdims=True
        )


def call(kernel, out_shape, scratch, *args, hbm=(), **params):
    vmem = pl.BlockSpec(memory_space=pltpu.VMEM)
    return pl.pallas_call(
        kernel,
        out_shape=out_shape,
        in_specs=[pl.BlockSpec(memory_space=pl.ANY) if i in hbm else vmem
                  for i in range(len(args))],
        out_specs=jax.tree.map(lambda _: vmem, out_shape),
        scratch_shapes=scratch,
        compiler_params=pltpu.CompilerParams(**PARAMS, **params),
    )(*args)


def whole_kernel(names, *refs):
    s = types.SimpleNamespace(**dict(zip(names, refs)))
    count, rows, cw = s.h_rx.shape
    parts, _, pieces, tall, _ = s.held.shape
    cols = s.d_own.shape[1]
    piece = cols // pieces
    tap_count = s.taps.shape[1]
    rim = tap_count - 1
    me = lax.axis_index("ctx")
    mine = lax.axis_index("ch")
    partner = mine + 1 - 2 * lax.rem(mine, 2)
    rest = [lax.rem(mine + 2 * o, parts) for o in range(1, parts // 2)]
    other = [lax.rem(partner + 2 * o, parts) for o in range(1, parts // 2)]
    after_me = lax.rem(me + 1, count)
    before_me = lax.rem(me + count - 1, count)
    peers = [lax.rem(me + o, count) for o in far_first(count)]
    sources = [lax.rem(me + count - o, count) for o in far_first(count)]
    streams = (s.q_hbm, s.k_hbm, s.v_hbm)

    def load(source, target, i):
        return pltpu.make_async_copy(source, target, s.load_sem.at[i])

    long_load = load(s.long_hbm, s.long_own, 0)
    stream_loads = [load(streams[i], s.own.at[i], 1 + i) for i in range(3)]
    d_load = load(s.d_hbm, s.d_own, 4)
    table_loads = [load(s.fwd_hbm, s.fwd, 5), load(s.inv_hbm, s.inv, 6)]

    def weight(part):
        lanes = pl.ds(pl.multiple_of(part * cols, cols), cols)
        return pltpu.make_async_copy(s.w_hbm.at[:, lanes], s.weights.at[part], s.w_sem.at[part])

    small_loads = [load(s.taps_hbm, s.taps, 7), load(s.skip_hbm, s.skip, 8)]
    long_load.start()
    for i in (1, 2, 0):
        stream_loads[i].start()
    for small in small_loads:
        small.start()
    d_load.start()
    weight(mine).start()
    weight(partner).start()
    for table in table_loads:
        table.start()
    for part in [p for pair in zip(rest, other) for p in pair]:
        weight(part).start()

    greet([("ctx", count), ("ch", parts)])

    edges = []
    for i in (1, 2, 0):
        edges.append(send(streams[i].at[rows - TAIL : rows], s.before.at[i], s.edge_sent.at[i],
                          s.edge_came.at[i], after_me))
    for edge in edges:
        edge.start()

    batches = [(h, p) for h in range(rows // tall) for p in range(pieces)]

    def own(slot, h, p, peer):
        part = s.d_hbm.at[h * tall : (h + 1) * tall, p * piece : (p + 1) * piece]
        return send(part, s.held.at[mine, h, p], s.own_sent.at[slot, h, p],
                    s.d_came.at[mine, h, p], peer, "ch")

    def passed(slot, h, p, part):
        return send(s.held.at[part, h, p], s.held.at[part, h, p], s.pass_sent.at[slot, h, p],
                    s.d_came.at[part, h, p], partner, "ch")

    for h, p in batches:
        for slot, peer in enumerate(rest + [partner]):
            own(slot, h, p, peer).start()

    def exchange(kind, source, target, peer):
        return send(source.at[peer], target.at[me], s.sent.at[kind, peer], s.came.at[kind, me],
                    peer)

    def arrival(kind, source, target, peer):
        return send(source.at[peer], target.at[peer], s.sent.at[kind, peer],
                    s.came.at[kind, peer], peer)

    def arrive(kind, source, target):
        for peer in peers:
            arrival(kind, source, target, peer).wait_recv()

    def chunk(c):
        return pl.ds(pl.multiple_of(c * cw, cw), cw)

    def filtered(i, lanes):
        total = None
        for j in range(tap_count):
            term = s.taps[i, j : j + 1, lanes] * s.ext[i, PAD - j : PAD - j + rows, lanes]
            total = term if total is None else total + term
        return total

    def fill_own(i):
        def body(c, carry):
            lanes = chunk(c)
            s.ext[i, 0:PAD, lanes] = jnp.zeros((PAD, cw), F32)
            s.ext[i, PAD : PAD + rows, lanes] = s.own[i, :, lanes].astype(F32)
            return carry

        lax.fori_loop(0, count, body, 0)

    def fill_rim(i):
        s.ext[i, PAD - rim : PAD, :] = s.before[i, TAIL - rim :, :].astype(F32)

    long_load.wait()
    for peer in peers + [me]:
        s.h_tx[peer] = s.long_own[:, chunk(peer)].astype(BF16)
        if peer is not me:
            exchange(0, s.h_tx, s.h_rx, peer).start()
    s.h_rx[me] = s.h_tx[me]

    for i in (1, 2, 0):
        stream_loads[i].wait()
        fill_own(i)
    for edge in edges:
        edge.wait()

    @pl.when(me == 0)
    def _():
        s.before[...] = jnp.zeros_like(s.before)

    for small in small_loads:
        small.wait()
    for i in (1, 2, 0):
        fill_rim(i)
    for peer in peers + [me]:
        lanes = chunk(peer)
        keyed = filtered(1, lanes)
        valued = filtered(2, lanes)
        s.filt[1, :, lanes] = keyed
        s.filt[2, :, lanes] = valued
        s.m_tx[peer] = (keyed * valued).astype(BF16)
        if peer is not me:
            exchange(1, s.m_tx, s.m_rx, peer).start()
    s.m_rx[me] = s.m_tx[me]

    def query(c, carry):
        s.filt[0, :, chunk(c)] = filtered(0, chunk(c))
        return carry

    lax.fori_loop(0, count, query, 0)

    def product(data, part, p=None):
        lanes = slice(None) if p is None else slice(p * piece, (p + 1) * piece)
        return lax.dot_general(data, s.weights[part, :, lanes], (((1,), (1,)), ((), ())),
                               preferred_element_type=F32)

    def take(part, h, p):
        s.total[h * tall : (h + 1) * tall, :] += product(s.held[part, h, p], part, p)

    def g_send(h, source, target, peer, slot):
        at = slice(h * tall, (h + 1) * tall)
        return send(source.at[peer, at], target.at[slot, at], s.g_sent.at[h, peer],
                    s.g_came.at[h, slot], peer)

    def gradient(h):
        at = slice(h * tall, (h + 1) * tall)
        for peer in peers + [me]:
            lanes = chunk(peer)
            value = s.total[at, lanes].astype(BF16).astype(F32)
            s.go[at, lanes] = value
            s.g_tx[peer, at, :] = (value * s.filt[0, at, lanes]).astype(BF16)
            if peer is not me:
                g_send(h, s.g_tx, s.g_rx, peer, me).start()
        s.g_rx[me, at, :] = s.g_tx[me, at, :]

    def long_spectra():
        arrive(0, s.h_tx, s.h_rx)
        spectra(s.fwd, [(s.h_rx.at[i], 1, i) for i in range(count)], s.spec)

    d_load.wait()
    weight(mine).wait()
    s.total[...] = product(s.d_own[...], mine)
    weight(partner).wait()
    for h, p in batches:
        passed(0, h, p, partner).wait_recv()
        take(partner, h, p)
    for direct, relayed in zip(rest, other):
        weight(direct).wait()
        weight(relayed).wait()
    for table in table_loads:
        table.wait()
    for h in range(rows // tall):
        for p in range(pieces):
            for slot, (direct, relayed) in enumerate(zip(rest, other)):
                passed(slot, h, p, direct).wait_recv()
                passed(slot, h, p, direct).start()
                take(direct, h, p)
                passed(slot, h, p, relayed).wait_recv()
                take(relayed, h, p)
        gradient(h)
        if h == 0:
            long_spectra()

    half = count // 2
    start = lax.rem(me // 2 + half // 2, half)

    def give_b(to):
        @pl.when(to != me)
        def _():
            exchange(4, s.b_tx, s.b_rx, to).start()

    def keep(to):
        pass

    def deliver(give, source, at_spec):
        for k in range(half):
            at = 2 * lax.rem(start + k, half)
            out = back_pair(s.inv, [s.spec[at_spec, at], s.spec[at_spec, at + 1]])
            for p in range(2):
                source[at + p] = out[p]
                give(at + p)

    arrive(1, s.m_tx, s.m_rx)
    spectra(s.fwd, [(s.m_rx.at[i], 0, i) for i in range(count)], s.spec)
    mix(s.spec, "y")
    deliver(keep, s.y_tx, 2)
    s.y_rx[me] = s.y_tx[me]

    for peer in sources:
        for h in range(rows // tall):
            g_send(h, s.g_tx, s.g_rx, peer, peer).wait_recv()
        exchange(3, s.y_tx, s.y_rx, peer).start()
    spectra(s.fwd, [(s.g_rx.at[i], 2, i) for i in range(count)], s.spec)
    mix(s.spec, "b")
    deliver(give_b, s.b_tx, 1)
    s.b_rx[me] = s.b_tx[me]
    mix(s.spec, "l")
    deliver(keep, s.l_tx, 0)
    l_own = pltpu.make_async_copy(s.l_tx.at[me], s.l_hbm.at[me], s.out_sem.at[3])
    l_own.start()

    def gather_sums(i, c, lanes, grad):
        s.grads[i, 0:rows, lanes] = grad
        s.head_tx[i * rim : (i + 1) * rim, lanes] = grad[0:rim]
        for j in range(tap_count):
            stream = s.ext[i, PAD - j : PAD - j + rows, lanes]
            row = i * tap_count + j
            s.part[c, row : row + 1, :] = jnp.sum(grad * stream, axis=0, keepdims=True)

    def write_out(c, carry):
        lanes = chunk(c)
        for i in range(3):
            total = None
            for j in range(tap_count):
                term = s.taps[i, j : j + 1, lanes] * s.grads[i, j : j + rows, lanes]
                total = term if total is None else total + term
            s.done[i, :, lanes] = total.astype(BF16)
        return carry

    def first_half(c, carry):
        lanes = chunk(c)
        mixed = s.filt[1, :, lanes] * s.filt[2, :, lanes]
        grad_o = s.go[:, lanes]
        row = 3 * tap_count
        s.part[c, row:, :] = jnp.zeros((16 - row, cw), F32)
        s.part[c, row : row + 1, :] = jnp.sum(
            grad_o * s.filt[0, :, lanes] * mixed, axis=0, keepdims=True
        )
        y_full = s.y_rx[c].astype(F32) + s.skip[:, lanes] * mixed
        gather_sums(0, c, lanes, grad_o * y_full)
        return carry

    def second_half(k, carry):
        middle = count // 2
        k = lax.rem(k + count - 1, count)
        c = lax.rem(me + count - middle + (2 * lax.rem(k, 2) - 1) * ((k + 1) // 2), count)

        @pl.when(c != me)
        def _():
            arrival(4, s.b_tx, s.b_rx, c).wait_recv()

        lanes = chunk(c)
        grad_y = s.go[:, lanes] * s.filt[0, :, lanes]
        grad_mixed = s.b_rx[c].astype(F32) + s.skip[:, lanes] * grad_y
        gather_sums(1, c, lanes, grad_mixed * s.filt[2, :, lanes])
        gather_sums(2, c, lanes, grad_mixed * s.filt[1, :, lanes])
        return carry

    heads = send(s.head_tx, s.head_rx, s.edge_sent.at[3], s.edge_came.at[3], before_me)
    outs = [pltpu.make_async_copy(s.done.at[i], ref, s.out_sem.at[i])
            for i, ref in enumerate((s.dq_hbm, s.dk_hbm, s.dv_hbm))]

    even = lax.rem(mine, 2) == 0
    steps_even, steps_odd = (0, 3, 3, 5, count), (0, 0, 0, 1, count)

    def long_send(stage):
        for n, peer in enumerate(sources):
            due_even = steps_even[stage] <= n < steps_even[stage + 1]
            due_odd = steps_odd[stage] <= n < steps_odd[stage + 1]
            if not due_even and not due_odd:
                continue

            @pl.when((even & due_even) | (jnp.logical_not(even) & due_odd))
            def _():
                exchange(5, s.l_tx, s.l_hbm, peer).start()

    arrive(3, s.y_tx, s.y_rx)
    long_send(0)
    s.head_tx[...] = jnp.zeros_like(s.head_tx)
    lax.fori_loop(0, count, first_half, 0)
    lax.fori_loop(0, count, second_half, 0)
    long_send(1)
    s.part_tx[...] = s.part[...].astype(BF16)
    for peer in peers:
        exchange(6, s.part_tx, s.one_rx, peer).start()
    heads.start()
    long_send(2)
    s.one_rx[me] = s.part_tx[me]
    arrive(6, s.part_tx, s.one_rx)
    value = s.one_rx[0].astype(F32)
    for c in range(1, count):
        value = value + s.one_rx[c].astype(F32)
    s.sum[...] = value.astype(BF16)

    def spread(peer):
        return send(s.sum, s.sums_hbm.at[me], s.sent.at[7, peer], s.came.at[7, me], peer)

    for peer in peers:
        spread(peer).start()
    long_send(3)
    heads.wait_recv()
    s.grads[:, rows:, :] = jnp.zeros_like(s.grads[:, rows:, :])

    @pl.when(me != count - 1)
    def _():
        for i in range(3):
            s.grads[i, rows : rows + rim, :] = s.head_rx[i * rim : (i + 1) * rim, :]

    lax.fori_loop(0, count, write_out, 0)
    for copy in outs:
        copy.start()
    sums_own = pltpu.make_async_copy(s.sum, s.sums_hbm.at[me], s.out_sem.at[4])
    sums_own.start()

    for peer in peers:
        send(s.sum, s.sums_hbm.at[peer], s.sent.at[7, peer], s.came.at[7, peer], peer).wait_recv()
    arrive(5, s.l_tx, s.l_hbm)
    for copy in outs + [l_own, sums_own]:
        copy.wait()
    sends = ((0, s.h_tx, s.h_rx), (1, s.m_tx, s.m_rx), (3, s.y_tx, s.y_rx),
             (4, s.b_tx, s.b_rx), (5, s.l_tx, s.l_hbm), (6, s.part_tx, s.one_rx))
    for kind, source, target in sends:
        for peer in peers:
            exchange(kind, source, target, peer).wait_send()
    for h in range(rows // tall):
        for peer in peers:
            g_send(h, s.g_tx, s.g_rx, peer, me).wait_send()
    for peer in peers:
        spread(peer).wait_send()
    heads.wait_send()
    for h, p in batches:
        for slot, peer in enumerate(rest + [partner]):
            own(slot, h, p, peer).wait_send()
        for slot, direct in enumerate(rest):
            passed(slot, h, p, direct).wait_send()


def mix(spec, what):
    count, rows2, cw = spec.shape[1:]
    half = rows2 // 2
    step = 8
    sign = 1.0 - 2.0 * (lax.broadcasted_iota(jnp.int32, (step, cw), 0) % 2).astype(F32)

    def primes(blocks):
        out = [blocks[0]]
        for d in range(1, count):
            re, im = blocks[d]
            old_re, old_im = blocks[d - 1]
            out.append((re - sign * old_im, im + sign * old_re))
        return out

    def chunk(r, carry):
        low = pl.ds(pl.multiple_of(r * step, step), step)
        high = pl.ds(pl.multiple_of(half + r * step, step), step)

        def load(s, i):
            return spec[s, i, low, :], spec[s, i, high, :]

        def save(s, i, value):
            spec[s, i, low, :] = value[0]
            spec[s, i, high, :] = value[1]

        if what == "y":
            taps = primes([load(1, i) for i in range(count)])
            for i in range(count):
                save(1, i, taps[i])
            mixed = [load(0, i) for i in range(count)]
            for i in range(count):
                total = None
                for d in range(i + 1):
                    total = add(total, times(taps[d], mixed[i - d]))
                save(2, i, total)
            return carry
        s = 1 if what == "b" else 0
        taps = [load(s, i) for i in range(count)]
        if what == "l":
            taps = primes(taps)
        grads = [load(2, i) for i in range(count)]
        for b in range(count):
            total = None
            for e in range(count - b):
                total = add(total, conj_times(taps[e], grads[b + e]))
            save(s, b, total)
        return carry

    lax.fori_loop(0, half // step, chunk, 0)


def result_kernel(dq_in, dk_in, dv_in, l_in, sums_in,
                  dq_out, dk_out, dv_out, long_out, short_out, skip_out,
                  streams, l_ref, long_ref, sums_ref, short_ref, skip_ref,
                  in_sem, out_sem, l_sem, long_sem):
    count, rows, cw = l_ref.shape
    tap_count = short_ref.shape[1]
    steps = l_sem.shape[0]
    tall = rows // steps
    copy = pltpu.make_async_copy
    l_loads, l_stores = [], []
    for n in range(steps):
        at = slice(n * tall, (n + 1) * tall)
        l_loads.append(copy(l_in.at[:, at], l_ref.at[:, at], l_sem.at[n]))
        l_stores.append(copy(long_ref.at[at], long_out.at[at], long_sem.at[n]))
    sums_load = copy(sums_in, sums_ref, in_sem.at[3])
    loads = [copy(ref, streams.at[i], in_sem.at[i])
             for i, ref in enumerate((dq_in, dk_in, dv_in))]
    stores = [copy(streams.at[i], ref, out_sem.at[i])
              for i, ref in enumerate((dq_out, dk_out, dv_out))]
    stores += [copy(short_ref, short_out, out_sem.at[3]), copy(skip_ref, skip_out, out_sem.at[4])]
    for load in [sums_load] + l_loads + loads:
        load.start()
    sums_load.wait()
    for c in range(count):
        lanes = slice(c * cw, (c + 1) * cw)
        sums = sums_ref[c].astype(F32)
        for i in range(3):
            short_ref[i, :, lanes] = sums[i * tap_count : (i + 1) * tap_count, :]
        skip_ref[:, lanes] = sums[3 * tap_count : 3 * tap_count + 1, :]
    stores[3].start()
    stores[4].start()
    for n in range(steps):
        l_loads[n].wait()
        at = slice(n * tall, (n + 1) * tall)
        for c in range(count):
            long_ref[at, c * cw : (c + 1) * cw] = l_ref[c, at, :].astype(F32)
        l_stores[n].start()
    for load, store in zip(loads, stores):
        load.wait()
        store.start()
    for store in stores + l_stores:
        store.wait()


def joined(queries, keys, values, long_filter, short_filters, skip, w_out, d_out):
    ctx = lax.axis_size("ctx")
    parts = lax.axis_size("ch")
    rows, width = queries.shape
    cw = width // ctx
    tap_count = short_filters.shape[1]
    cols = d_out.shape[1]
    halves, pieces = 2, 4
    shape = jax.ShapeDtypeStruct
    dma = pltpu.SemaphoreType.DMA
    forward, inverse = (jnp.asarray(t) for t in tables(rows))
    anyw = pl.BlockSpec(memory_space=pl.ANY)
    inputs = [
        ("q_hbm", queries, anyw), ("k_hbm", keys, anyw), ("v_hbm", values, anyw),
        ("long_hbm", long_filter, anyw), ("taps_hbm", short_filters, anyw),
        ("skip_hbm", skip[None], anyw), ("d_hbm", d_out, anyw), ("w_hbm", w_out, anyw),
        ("fwd_hbm", forward, anyw), ("inv_hbm", inverse, anyw),
    ]
    stream = shape((rows, width), BF16)
    outputs = [
        ("dq_hbm", stream), ("dk_hbm", stream), ("dv_hbm", stream),
        ("l_hbm", shape((ctx, rows, cw), BF16)), ("sums_hbm", shape((ctx, 16, cw), BF16)),
    ]
    bulk = pltpu.VMEM((ctx, rows, cw), BF16)
    small = pltpu.VMEM((ctx, 16, cw), BF16)
    rim = pltpu.VMEM((3, TAIL, width), BF16)
    rim_rows = -(-3 * (tap_count - 1) // PAD) * PAD
    scratch = [
        ("taps", pltpu.VMEM(short_filters.shape, F32)), ("skip", pltpu.VMEM((1, width), F32)),
        ("long_own", pltpu.VMEM((rows, width), F32)), ("own", pltpu.VMEM((3, rows, width), BF16)),
        ("d_own", pltpu.VMEM((rows, cols), BF16)), ("fwd", pltpu.VMEM(forward.shape, BF16)),
        ("inv", pltpu.VMEM(inverse.shape, BF16)), ("before", rim), ("head_tx", pltpu.VMEM((rim_rows, width), F32)),
        ("head_rx", pltpu.VMEM((rim_rows, width), F32)),
        ("ext", pltpu.VMEM((3, rows + PAD, width), F32)),
        ("filt", pltpu.VMEM((3, rows, width), F32)),
        ("held", pltpu.VMEM((parts, halves, pieces, rows // halves, cols // pieces), BF16)),
        ("weights", pltpu.VMEM((parts, width, cols), BF16)),
        ("total", pltpu.VMEM((rows, width), F32)),
        ("go", pltpu.VMEM((rows, width), F32)),
        ("h_tx", bulk), ("h_rx", bulk), ("m_tx", bulk), ("m_rx", bulk), ("g_tx", bulk),
        ("g_rx", bulk), ("y_tx", bulk), ("y_rx", bulk), ("b_tx", bulk), ("b_rx", bulk),
        ("l_tx", bulk), ("spec", pltpu.VMEM((3, ctx, 2 * rows, cw), F32)),
        ("grads", pltpu.VMEM((3, rows + PAD, width), F32)),
        ("done", pltpu.VMEM((3, rows, width), BF16)),
        ("part", pltpu.VMEM((ctx, 16, cw), F32)), ("part_tx", small), ("one_rx", small),
        ("sum", pltpu.VMEM((16, cw), BF16)),
        ("load_sem", dma((9,))), ("w_sem", dma((parts,))), ("edge_sent", dma((6,))),
        ("edge_came", dma((6,))), ("own_sent", dma((parts // 2, halves, pieces))),
        ("pass_sent", dma((parts // 2, halves, pieces))), ("d_came", dma((parts, halves, pieces))),
        ("sent", dma((8, ctx))), ("came", dma((8, ctx))), ("out_sem", dma((5,))),
        ("g_sent", dma((halves, ctx))), ("g_came", dma((halves, ctx))),
    ]
    names = tuple(name for name, *_ in inputs + outputs + scratch)
    dq, dk, dv, back, sums = pl.pallas_call(
        functools.partial(whole_kernel, names),
        out_shape=[out for _, out in outputs],
        in_specs=[spec for _, _, spec in inputs],
        out_specs=[anyw] * len(outputs),
        scratch_shapes=[kind for _, kind in scratch],
        compiler_params=pltpu.CompilerParams(**PARAMS, collective_id=0, has_side_effects=True),
    )(*[value for _, value, _ in inputs])
    dq, dk, dv, d_long, d_short, d_skip = pl.pallas_call(
        result_kernel,
        out_shape=[stream, stream, stream, shape((rows, width), F32),
                   shape((3, tap_count, width), F32), shape((1, width), F32)],
        in_specs=[anyw] * 5,
        out_specs=[anyw] * 6,
        scratch_shapes=[pltpu.VMEM((3, rows, width), BF16), pltpu.VMEM((ctx, rows, cw), BF16),
                        pltpu.VMEM((rows, width), F32), small,
                        pltpu.VMEM((3, tap_count, width), F32), pltpu.VMEM((1, width), F32),
                        dma((4,)), dma((5,)), dma((4,)), dma((4,))],
        compiler_params=pltpu.CompilerParams(**PARAMS),
    )(dq, dk, dv, back, sums)
    return dq, dk, dv, d_long, d_short, d_skip[0]


def per_device(queries, keys, values, long_filter, short_filters, skip, w_out, d_out):
    ctx = lax.axis_size("ctx")
    rows, width = queries.shape
    cw = width // ctx
    if cw % 128 == 0 and ctx <= 8 and ctx % 2 == 0:
        return joined(queries, keys, values, long_filter, short_filters, skip, w_out, d_out)
    tap_count = short_filters.shape[1]
    parts = lax.axis_size("ch")
    cols = d_out.shape[1]
    halves = 2
    ext = pltpu.VMEM((rows + 4 * PAD, cw), F32)
    shape = jax.ShapeDtypeStruct
    dma = pltpu.SemaphoreType.DMA
    edge = shape((3, TAIL, width), BF16)
    pair = (ctx, 2, rows, cw)
    mh, grad_o, before, after = call(
        gather_kernel,
        (shape(pair, BF16), shape((rows, width), BF16), edge, edge),
        [ext, pltpu.VMEM(pair, BF16), pltpu.VMEM((parts, halves, rows, cols // halves), BF16),
         pltpu.VMEM((parts, width, cols), BF16), pltpu.VMEM((rows, width), F32),
         dma((6,)), dma((6,)), dma((ctx,)), dma((ctx,)), dma((parts // 2, halves)),
         dma((parts // 2, halves)), dma((parts, halves)), dma((parts,))],
        queries, keys, values, long_filter, short_filters, d_out, w_out,
        hbm=(6,), collective_id=3, has_side_effects=True,
    )
    forward, inverse = tables(rows)
    spare = ctx if ctx > 8 else 1
    one = shape((ctx, rows + TAIL, cw), BF16)
    two = shape((ctx, 2 * rows + TAIL, cw), BF16)
    piece = pltpu.VMEM((ctx, rows, cw), BF16)
    y, back, go_after = call(
        conv_kernel,
        (one, two, shape((TAIL, width), BF16)),
        [ext, piece, piece, pltpu.VMEM(one.shape, BF16), pltpu.VMEM(two.shape, BF16),
         pltpu.VMEM((3, ctx, 2 * rows, cw), F32), pltpu.VMEM((2, spare, 2, 8, cw), F32),
         pltpu.SemaphoreType.DMA((3, ctx)), pltpu.SemaphoreType.DMA((3, ctx)),
         pltpu.SemaphoreType.DMA((2,))],
        queries, before, grad_o, short_filters, mh, jnp.asarray(forward), jnp.asarray(inverse),
        collective_id=1, has_side_effects=True,
    )
    stream = shape((rows, width), BF16)
    dq, dk, dv, d_long, sums = call(
        functools.partial(leave_kernel, ctx),
        (stream, stream, stream, shape((rows, width), F32), shape((ctx, 16, cw), F32)),
        [pltpu.VMEM((3, rows + 4 * PAD, cw), F32), ext, pltpu.VMEM((3, rows + 4 * PAD, cw), F32)],
        queries, keys, values, before, after, grad_o, go_after, short_filters, skip[None], y, back,
    )
    small = pltpu.VMEM((ctx, 16, cw), F32)
    d_short, d_skip = call(
        sum_kernel,
        (shape((3, tap_count, width), F32), shape((1, width), F32)),
        [small, pltpu.VMEM((16, cw), F32), small,
         pltpu.SemaphoreType.DMA((2, ctx)), pltpu.SemaphoreType.DMA((2, ctx))],
        sums,
        collective_id=2, has_side_effects=True,
    )
    return dq, dk, dv, d_long, d_short, d_skip[0]


def solution(mesh):
    in_specs = (
        P("ctx", "ch"),
        P("ctx", "ch"),
        P("ctx", "ch"),
        P("ctx", "ch"),
        P(None, None, "ch"),
        P("ch"),
        P("ch", None),
        P("ctx", "ch"),
    )
    out_specs = (
        P("ctx", "ch"),
        P("ctx", "ch"),
        P("ctx", "ch"),
        P("ctx", "ch"),
        P(None, None, "ch"),
        P("ch"),
    )
    return jax.shard_map(
        per_device, mesh=mesh, in_specs=in_specs, out_specs=out_specs, check_vma=False
    )
```
